32 devices in a mesh: shard: 2 (over y), ctx: 4 (over x, core), tp: 4 (over z).
Axes of the slice: x: 2, y: 2, z: 4, core: 2. Of those that a mesh axis runs over, the one named last changes fastest.
Arguments:
- tokens: bfloat16 [2, 2, 2560, 1280], P(None, 'shard', ('ctx', 'tp')), may hold values from -0.16992188 to 0.16992188
- parents: int32 [2, 2, 40], P(None, 'shard'), may hold values from 0 to 38, as said below
- slot_segment: int32 [2, 2, 40], P(None, 'shard'), may hold values from 0 to 39, each once within a row
- w_query: bfloat16 [1280, 1280], P(('shard', 'ctx'), 'tp'), may hold values from -0.15625 to 0.15625
- w_key: bfloat16 [1280, 1280], P(('shard', 'ctx'), 'tp'), may hold values from -0.15625 to 0.15625
- w_value: bfloat16 [1280, 1280], P(('shard', 'ctx'), 'tp'), may hold values from -0.15625 to 0.15625
- w_attn_out: bfloat16 [1280, 1280], P('tp', ('shard', 'ctx')), may hold values from -0.15625 to 0.15625
- w_up: bfloat16 [1280, 5120], P(('shard', 'ctx'), 'tp'), may hold values from -0.15625 to 0.15625
- w_gate: bfloat16 [1280, 5120], P(('shard', 'ctx'), 'tp'), may hold values from -0.15625 to 0.15625
- w_down: bfloat16 [5120, 1280], P('tp', ('shard', 'ctx')), may hold values from -0.078125 to 0.078125
- alpha_attn: float32 [1280], replicated, may hold values from 0.15 to 0.6
- alpha_mlp: float32 [1280], replicated, may hold values from 0.15 to 0.6
- scale_qk: float32 [1280], P('tp'), may hold values from 0.7 to 1.4
- scale_up: float32 [5120], P('tp'), may hold values from 0.5 to 2
- scale_gate: float32 [5120], P('tp'), may hold values from 0.5 to 2
- cotangent: bfloat16 [2, 2, 2560, 1280], P(None, 'shard', ('ctx', 'tp')), may hold values from -6 to 6
Outputs:
- block_out: bfloat16 [2, 2, 2560, 1280], P(None, 'shard', ('ctx', 'tp'))
- grad_tokens: float32 [2, 2, 2560, 1280], P(None, 'shard', ('ctx', 'tp'))
- grad_w_query: float32 [1280, 1280], P(('shard', 'ctx'), 'tp')
- grad_w_key: float32 [1280, 1280], P(('shard', 'ctx'), 'tp')
- grad_w_value: float32 [1280, 1280], P(('shard', 'ctx'), 'tp')
- grad_w_attn_out: float32 [1280, 1280], P('tp', ('shard', 'ctx'))
- grad_w_up: float32 [1280, 5120], P(('shard', 'ctx'), 'tp')
- grad_w_gate: float32 [1280, 5120], P(('shard', 'ctx'), 'tp')
- grad_w_down: float32 [5120, 1280], P('tp', ('shard', 'ctx'))
- grad_alpha_attn: float32 [1280], replicated
- grad_alpha_mlp: float32 [1280], replicated
- grad_scale_qk: float32 [1280], P('tp')
- grad_scale_up: float32 [5120], P('tp')
- grad_scale_gate: float32 [5120], P('tp')
The draws below stay inside these ranges and needn't reach their ends.
Inputs may be any that keep to these rules, and one draw needn't show every extreme that they name: `parents`: segment 0 of each tree is its root and names itself; every other segment names a segment with a lower number; every segment has 64 tokens. `slot_segment`: each tree's 40 slots hold its segments, each once.
All inputs are finite; a program needn't handle non-finite values.
Results may differ from the reference program's by a relative error of at most 0.019.
Values may be sent and summed in bfloat16 or wider, within the bound.
No kernel may reach another device: no remote copies, remote signals or barrier semaphores. Data moves between devices by JAX's collectives and lax.ppermute only.
A program may use at most 120 MiB of HBM per device.

```python
import math
import jax
import jax.numpy as jnp
from jax import lax

D = 1280
HEADS = 20
HDIM = 64
FF = 5120
HD = 1280
SEG = 64
SEGS = 40
TREE_TOK = 2560
MICRO = 2
TREES = 2


def draw_parents(key, part):
    trunk = SEGS - 24
    labels = jnp.arange(SEGS, dtype=jnp.int32)
    relative = labels - trunk
    branch_head = (relative >= 0) & (relative < 8) & (relative % 2 == 0)
    leaf_head = (relative >= 8) & (relative % 2 == 0)
    joints = jax.random.randint(key, (MICRO, TREES, SEGS), trunk // 2, trunk, dtype=jnp.int32)
    leaf_parent = trunk + 2 * ((relative - 8) // 4) + 1
    chain = jnp.maximum(labels - 1, 0)
    table = jnp.where(leaf_head, leaf_parent, chain)
    return jnp.where(branch_head[None, None, :], joints, table[None, None, :]).astype(jnp.int32)


def level_of(rng, dims, split, least, top_value):
    gain = 1.0
    for dim, blocks in split:
        heights = jax.random.uniform(jax.random.fold_in(jax.random.fold_in(rng, 6), dim), (blocks,), jnp.float32, least / len(split), top_value / len(split))
        gain = gain * jnp.repeat(jnp.exp(heights), dims[dim] // blocks).reshape((-1,) + (1,) * (len(dims) - 1 - dim))
    return gain


def bell_draw(own_key, extent, scale, bound, split=(), held_as=jnp.bfloat16):
    array = jax.random.normal(own_key, extent, jnp.float32) * scale
    if len(split) > 0:
        array = level_of(own_key, extent, split, -0.22, 0.18) * array
    return jnp.clip(array, min=-bound, max=bound).astype(held_as)


def setup_inputs(seed: int = 0) -> dict:
    arg_keys = jax.random.split(jax.random.key(seed), 17)
    tokens = bell_draw(arg_keys[0], (MICRO, TREES, TREE_TOK, D), 0.028, 0.16992188, ((1, 2), (2, 16)))
    parents = draw_parents(jax.random.fold_in(arg_keys[16], 71), 0)
    slot_segment = jax.vmap(lambda own: jax.random.permutation(own, SEGS))(jax.random.split(arg_keys[2], MICRO * TREES)).reshape((MICRO, TREES, SEGS)).astype(jnp.int32)
    w_query = bell_draw(arg_keys[3], (D, HD), D ** -0.5, 0.15625, ((0, 8), (1, 4)))
    w_key = bell_draw(arg_keys[4], (D, HD), D ** -0.5, 0.15625, ((0, 8), (1, 4)))
    w_value = bell_draw(arg_keys[5], (D, HD), D ** -0.5, 0.15625, ((0, 8), (1, 4)))
    w_attn_out = bell_draw(arg_keys[6], (HD, D), HD ** -0.5, 0.15625, ((0, 4), (1, 8)))
    w_up = bell_draw(arg_keys[7], (D, FF), D ** -0.5, 0.15625, ((0, 8), (1, 4)))
    w_gate = bell_draw(arg_keys[8], (D, FF), D ** -0.5, 0.15625, ((0, 8), (1, 4)))
    w_down = bell_draw(arg_keys[9], (FF, D), FF ** -0.5, 0.078125, ((0, 4), (1, 8)))
    alpha_attn = jnp.clip(jnp.exp(jax.random.uniform(arg_keys[10], (D,), jnp.float32, math.log(0.15), math.log(0.6))), 0.15, 0.6)
    alpha_mlp = jnp.clip(jnp.exp(jax.random.uniform(arg_keys[11], (D,), jnp.float32, math.log(0.15), math.log(0.6))), 0.15, 0.6)
    scale_qk = jnp.clip(jnp.exp(math.log(1.4) - 0.6931472 * jax.random.uniform(arg_keys[12], (HD,), jnp.float32) ** level_of(arg_keys[12], (HD,), ((0, 4),), -0.2, 0.2)), 0.7, 1.4)
    scale_up = jnp.clip(jnp.exp(math.log(2.0) - 1.3862944 * jax.random.uniform(arg_keys[13], (FF,), jnp.float32) ** level_of(arg_keys[13], (FF,), ((0, 4),), -0.2, 0.2)), 0.5, 2.0)
    scale_gate = jnp.clip(jnp.exp(math.log(2.0) - 1.3862944 * jax.random.uniform(arg_keys[14], (FF,), jnp.float32) ** level_of(arg_keys[14], (FF,), ((0, 4),), -0.2, 0.2)), 0.5, 2.0)
    cotangent = bell_draw(arg_keys[15], (MICRO, TREES, TREE_TOK, D), 1.0, 6.0, ((1, 2), (2, 16)))
    return dict(tokens=tokens, parents=parents, slot_segment=slot_segment, w_query=w_query, w_key=w_key, w_value=w_value, w_attn_out=w_attn_out, w_up=w_up, w_gate=w_gate, w_down=w_down, alpha_attn=alpha_attn, alpha_mlp=alpha_mlp, scale_qk=scale_qk, scale_up=scale_up, scale_gate=scale_gate, cotangent=cotangent)


@jax.custom_vjp
def low(v):
    return lax.optimization_barrier(v.astype(jnp.bfloat16)).astype(jnp.float32)

@jax.custom_vjp
def low_back(v):
    return v

def low_keep(v):
    return (low(v), None)

def low_pass(kept, grad):
    return (grad,)

def back_keep(v):
    return (v, None)

def back_low(kept, grad):
    return (low(grad),)
low.defvjp(low_keep, low_pass)
low_back.defvjp(back_keep, back_low)
EPSILON = 1e-06
MASKED = -1e+30
HIGHEST = lax.Precision.HIGHEST

def matmul(former, latter):
    return jnp.dot(former, latter, precision=HIGHEST, preferred_element_type=jnp.float32)

def unit_rows(values):
    return values * lax.rsqrt(lax.optimization_barrier(jnp.sum(values * values, axis=-1, keepdims=True)) + EPSILON)

def unit_heads(values):
    shaped = values.reshape(values.shape[0], HEADS, HDIM)
    return unit_rows(shaped).reshape(values.shape[0], HEADS * HDIM)

def ancestors(parents):
    labels = jnp.arange(SEGS, dtype=jnp.int32)
    linked = (parents[:, None] == labels[None, :]).astype(jnp.float32)
    reachable = jnp.maximum(linked, jnp.eye(SEGS, dtype=jnp.float32))
    for doubling in range(SEGS.bit_length()):
        reachable = jnp.minimum(matmul(reachable, reachable), 1.0)
    return reachable

def tree_layer(params, hidden, parents, slots):
    w_query, w_key, w_value, w_attn_out, w_up, w_gate, w_down, alpha_attn, alpha_mlp, scale_qk, scale_up, scale_gate = params
    reachable = ancestors(parents)
    labels = jnp.arange(SEGS, dtype=jnp.int32)
    segment = jnp.repeat(slots, SEG, total_repeat_length=TREE_TOK)
    offset = jnp.arange(TREE_TOK, dtype=jnp.int32) % SEG
    key_onehot = (segment[:, None] == labels[None, :]).astype(jnp.float32)
    query_raw = low_back(matmul(hidden, w_query))
    key_raw = low_back(matmul(hidden, w_key))
    values = low(low_back(matmul(hidden, w_value)))
    queries = low(unit_heads(query_raw) * scale_qk)
    keys = low(unit_heads(key_raw) * scale_qk)
    key_cube = keys.reshape(TREE_TOK, HEADS, HDIM)
    value_cube = values.reshape(TREE_TOK, HEADS, HDIM)
    score_scale = math.sqrt(HDIM)
    block_rows = math.gcd(TREE_TOK, 512)

    def attend(record):
        query_block, seg_block, off_block = record
        onehot = (seg_block[:, None] == labels[None, :]).astype(jnp.float32)
        visible = matmul(matmul(onehot, reachable), key_onehot.T) > 0.5
        visible = visible & ((seg_block[:, None] != segment[None, :]) | (offset[None, :] <= off_block[:, None]))
        scores = low_back(jnp.einsum('qhd,khd->hqk', query_block.reshape(block_rows, HEADS, HDIM), key_cube, precision=HIGHEST) * score_scale)
        scores = jnp.where(visible[None, :, :], scores, MASKED)
        row_peak = lax.optimization_barrier(jnp.max(scores, axis=-1, keepdims=True))
        lifted = jnp.exp(scores - row_peak)
        soft_weights = lifted / lax.optimization_barrier(jnp.sum(lifted, axis=-1, keepdims=True))
        mixed_heads = jnp.einsum('hqk,khd->qhd', low(soft_weights), value_cube, precision=HIGHEST)
        return mixed_heads.reshape(block_rows, HEADS * HDIM)
    attended = lax.map(jax.checkpoint(attend), (queries.reshape(-1, block_rows, HEADS * HDIM), segment.reshape(-1, block_rows), offset.reshape(-1, block_rows)))
    attended = attended.reshape(TREE_TOK, HEADS * HDIM)
    heads_out = low(low_back(attended))
    branch_one = low_back(matmul(heads_out, w_attn_out))
    hidden_one = unit_rows(hidden + alpha_attn * (unit_rows(branch_one) - hidden))
    hidden_low = low(hidden_one)
    up_raw = low_back(matmul(hidden_low, w_up))
    gate_raw = low_back(matmul(hidden_low, w_gate))
    mixed = low(low_back(up_raw * scale_up * jax.nn.silu(gate_raw * (scale_gate * math.sqrt(D)))))
    branch_two = low_back(matmul(mixed, w_down))
    return unit_rows(hidden_one + alpha_mlp * (unit_rows(branch_two) - hidden_one))

def reference(tokens, parents, slot_segment, w_query, w_key, w_value, w_attn_out, w_up, w_gate, w_down, alpha_attn, alpha_mlp, scale_qk, scale_up, scale_gate, cotangent):
    weights = (w_query.astype(jnp.float32), w_key.astype(jnp.float32), w_value.astype(jnp.float32), w_attn_out.astype(jnp.float32), w_up.astype(jnp.float32), w_gate.astype(jnp.float32), w_down.astype(jnp.float32))
    vectors = (alpha_attn, alpha_mlp, scale_qk, scale_up, scale_gate)
    tree_count = MICRO * TREES
    hidden = tokens.astype(jnp.float32).reshape(tree_count, TREE_TOK, D)
    links = parents.reshape(tree_count, SEGS)
    slots = slot_segment.reshape(tree_count, SEGS)

    def forward(weights, vectors, hidden):
        params = weights + vectors

        def one_tree(record):
            return tree_layer(params, record[0], record[1], record[2])
        return lax.map(one_tree, (hidden, links, slots))
    outputs, pullback = jax.vjp(forward, weights, vectors, hidden)
    grad_weights, grad_vectors, grad_hidden = pullback(cotangent.astype(jnp.float32).reshape(tree_count, TREE_TOK, D))
    return (outputs.astype(jnp.bfloat16).reshape(tokens.shape), grad_hidden.reshape(tokens.shape), grad_weights[0], grad_weights[1], grad_weights[2], grad_weights[3], grad_weights[4], grad_weights[5], grad_weights[6], grad_vectors[0], grad_vectors[1], grad_vectors[2], grad_vectors[3], grad_vectors[4])
```

```python
import math

import jax
import jax.numpy as jnp
from jax import lax
from jax.sharding import PartitionSpec as P

D = 1280
HDIM = 64
SEG = 64
SEGS = 40
TREE_TOK = 2560


EPSILON = 1e-06
MASKED = -1e30
HIGHEST = lax.Precision.HIGHEST


def unit_rows(values):
    return values * lax.rsqrt(jnp.sum(values * values, axis=-1, keepdims=True) + EPSILON)


def unit_heads(values):
    shaped = values.reshape(values.shape[0], values.shape[1] // HDIM, HDIM)
    return unit_rows(shaped).reshape(values.shape)


def contract_rows(former, latter):
    return lax.dot_general(
        former, latter, (((0,), (0,)), ((), ())), preferred_element_type=jnp.float32
    )


def contract_cols(former, latter):
    return lax.dot_general(
        former, latter, (((1,), (1,)), ((), ())), preferred_element_type=jnp.float32
    )


def split_heads(values):
    return values.reshape(values.shape[0], values.shape[1] // HDIM, HDIM).transpose(1, 0, 2)


def merge_heads(values):
    return values.transpose(1, 0, 2).reshape(values.shape[1], values.shape[0] * values.shape[2])


def mix_rows(residual, branch, mixing):
    return unit_rows(residual + mixing * (unit_rows(branch) - residual))


def query_key(query_raw, key_raw, gain_qk):
    return (unit_heads(query_raw) * gain_qk, unit_heads(key_raw) * gain_qk)


def middle(up_raw, gate_raw, scale_up, scale_gate):
    return up_raw * scale_up * jax.nn.silu(gate_raw * (scale_gate * math.sqrt(D)))


def group_rows(own_block):
    return lax.all_gather(own_block, "tp", axis=0, tiled=True)


def group_grads(own_block):
    return lax.all_gather(own_block, "tp", axis=0, tiled=True)


def own_rows(partial_value):
    return own_grads(partial_value)


def own_grads(partial_value):
    return lax.psum_scatter(
        partial_value.astype(jnp.bfloat16), "tp", scatter_dimension=0, tiled=True
    ).astype(jnp.float32)


def visibility(parents, slots, group_size):
    labels = jnp.arange(SEGS, dtype=jnp.int32)
    linked = (parents[:, None] == labels[None, :]).astype(jnp.float32)
    reachable = jnp.maximum(linked, jnp.eye(SEGS, dtype=jnp.float32))
    for doubling in range(SEGS.bit_length()):
        reachable = jnp.minimum(jnp.dot(reachable, reachable, precision=HIGHEST), 1.0)
    segment = jnp.broadcast_to(slots[:, None], (SEGS, SEG)).reshape(TREE_TOK)
    offset = lax.broadcasted_iota(jnp.int32, (SEGS, SEG), 1).reshape(TREE_TOK)
    first_row = lax.axis_index("ctx") * group_size
    seg_query = lax.dynamic_slice_in_dim(segment, first_row, group_size)
    off_query = lax.dynamic_slice_in_dim(offset, first_row, group_size)
    key_onehot = (segment[:, None] == labels[None, :]).astype(jnp.float32)
    query_onehot = (seg_query[:, None] == labels[None, :]).astype(jnp.float32)
    linked_rows = jnp.dot(query_onehot, reachable, precision=HIGHEST)
    seen = (
        lax.dot_general(linked_rows, key_onehot, (((1,), (1,)), ((), ())), precision=HIGHEST) > 0.5
    )
    return seen & (
        (seg_query[:, None] != segment[None, :]) | (offset[None, :] <= off_query[:, None])
    )


def forward_attention(gathered, vectors, tokens_own, parents, slots):
    w_query, w_key, w_value, w_attn_out = gathered[:4]
    alpha_attn, alpha_mlp, scale_qk, scale_up, scale_gate = vectors
    score_scale = math.sqrt(HDIM)
    hidden_group = group_rows(tokens_own)
    visible = visibility(parents, slots, hidden_group.shape[0])
    query_raw = jnp.dot(hidden_group, w_query, preferred_element_type=jnp.float32)
    key_raw = jnp.dot(hidden_group, w_key, preferred_element_type=jnp.float32)
    value_low = jnp.dot(hidden_group, w_value, preferred_element_type=jnp.float32).astype(
        jnp.bfloat16
    )
    query_unit, key_unit = query_key(query_raw, key_raw, scale_qk)
    queries = query_unit.astype(jnp.bfloat16)
    keys_own = key_unit.astype(jnp.bfloat16)
    keys_values = lax.all_gather(
        jnp.concatenate([keys_own, value_low], axis=1), "ctx", axis=0, tiled=True
    )
    keys_tree, values_tree = jnp.split(keys_values, 2, axis=1)
    query_heads = split_heads(queries)
    key_heads = split_heads(keys_tree)
    value_heads = split_heads(values_tree)

    def head_forward(record):
        query_one, key_one, value_one = record
        scores = jnp.where(visible, contract_cols(query_one, key_one) * score_scale, MASKED)
        row_peak = jnp.max(scores, axis=-1, keepdims=True)
        lifted = jnp.exp(scores - row_peak)
        row_total = jnp.sum(lifted, axis=-1, keepdims=True)
        soft_weights = lifted / row_total
        head_value = jnp.dot(
            soft_weights.astype(jnp.bfloat16), value_one, preferred_element_type=jnp.float32
        )
        return (head_value, (row_peak + jnp.log(row_total))[:, 0])

    head_values, log_totals = lax.map(head_forward, (query_heads, key_heads, value_heads))
    heads_low = merge_heads(head_values).astype(jnp.bfloat16)
    branch_one = own_rows(jnp.dot(heads_low, w_attn_out, preferred_element_type=jnp.float32))
    kept = (
        hidden_group,
        visible,
        query_raw,
        key_raw,
        query_heads,
        key_heads,
        value_heads,
        log_totals,
        heads_low,
    )
    return branch_one, kept


def feed_forward(gathered, vectors, tokens_own, branch_one, cotangent_own):
    w_up, w_gate, w_down = gathered[4:]
    alpha_attn, alpha_mlp, scale_qk, scale_up, scale_gate = vectors
    tokens_wide = tokens_own.astype(jnp.float32)
    hidden_one = mix_rows(tokens_wide, branch_one, alpha_attn)
    hidden_one_group = group_rows(hidden_one.astype(jnp.bfloat16))
    up_raw = jnp.dot(hidden_one_group, w_up, preferred_element_type=jnp.float32)
    gate_raw = jnp.dot(hidden_one_group, w_gate, preferred_element_type=jnp.float32)
    mixed_low = middle(up_raw, gate_raw, scale_up, scale_gate).astype(jnp.bfloat16)
    branch_two = own_rows(jnp.dot(mixed_low, w_down, preferred_element_type=jnp.float32))
    output_wide, pull_out = jax.vjp(mix_rows, hidden_one, branch_two, alpha_mlp)
    upstream = cotangent_own.astype(jnp.float32)
    hidden_one_direct, branch_two_grad, grad_alpha_mlp = pull_out(upstream)
    branch_two_group = group_grads(branch_two_grad.astype(jnp.bfloat16))
    mixed_grad = contract_cols(branch_two_group, w_down).astype(jnp.bfloat16).astype(jnp.float32)
    middle_value, pull_mid = jax.vjp(middle, up_raw, gate_raw, scale_up, scale_gate)
    up_grad, gate_grad, grad_scale_up, grad_scale_gate = pull_mid(mixed_grad)
    up_low = up_grad.astype(jnp.bfloat16)
    gate_low = gate_grad.astype(jnp.bfloat16)
    hidden_one_grad = hidden_one_direct + own_grads(
        contract_cols(up_low, w_up) + contract_cols(gate_low, w_gate)
    )
    hidden_again, pull_in = jax.vjp(mix_rows, tokens_wide, branch_one, alpha_attn)
    tokens_direct, branch_one_grad, grad_alpha_attn = pull_in(hidden_one_grad)
    factors = (mixed_low, branch_two_group, hidden_one_group, up_low, gate_low)
    sums = (grad_alpha_attn, grad_alpha_mlp, grad_scale_up, grad_scale_gate)
    return output_wide.astype(jnp.bfloat16), tokens_direct, branch_one_grad, factors, sums


def backward_attention(gathered, vectors, kept, branch_one_grad, tokens_direct):
    w_query, w_key, w_value, w_attn_out = gathered[:4]
    scale_qk = vectors[2]
    score_scale = math.sqrt(HDIM)
    (
        hidden_group,
        visible,
        query_raw,
        key_raw,
        query_heads,
        key_heads,
        value_heads,
        log_totals,
        heads_low,
    ) = kept
    branch_one_group = group_grads(branch_one_grad.astype(jnp.bfloat16))
    heads_grad = split_heads(contract_cols(branch_one_group, w_attn_out).astype(jnp.bfloat16))

    def head_backward(record):
        query_one, key_one, value_one, upstream_one, log_total = record
        scores = jnp.where(visible, contract_cols(query_one, key_one) * score_scale, MASKED)
        soft_weights = jnp.exp(scores - log_total[:, None])
        weight_grad = contract_cols(upstream_one, value_one)
        row_inner = jnp.sum(soft_weights * weight_grad, axis=-1, keepdims=True)
        score_grad = (soft_weights * (weight_grad - row_inner)).astype(jnp.bfloat16)
        query_grad = jnp.dot(score_grad, key_one, preferred_element_type=jnp.float32) * score_scale
        key_grad = contract_rows(score_grad, query_one) * score_scale
        value_grad = contract_rows(soft_weights.astype(jnp.bfloat16), upstream_one)
        return (query_grad, key_grad, value_grad)

    query_grads, key_grads, value_grads = lax.map(
        head_backward, (query_heads, key_heads, value_heads, heads_grad, log_totals)
    )
    both = lax.psum_scatter(
        jnp.concatenate([merge_heads(key_grads), merge_heads(value_grads)], axis=1).astype(
            jnp.bfloat16
        ),
        "ctx",
        scatter_dimension=0,
        tiled=True,
    ).astype(jnp.float32)
    key_own_grad, value_own_grad = jnp.split(both, 2, axis=1)
    unit_again, pull_qk = jax.vjp(query_key, query_raw, key_raw, scale_qk)
    query_raw_grad, key_raw_grad, grad_scale_qk = pull_qk((merge_heads(query_grads), key_own_grad))
    query_low = query_raw_grad.astype(jnp.bfloat16)
    key_low = key_raw_grad.astype(jnp.bfloat16)
    value_grad_low = value_own_grad.astype(jnp.bfloat16)
    input_part = (
        contract_cols(query_low, w_query)
        + contract_cols(key_low, w_key)
        + contract_cols(value_grad_low, w_value)
    )
    grad_tokens = tokens_direct + own_grads(input_part)
    factors = (hidden_group, query_low, key_low, value_grad_low, heads_low, branch_one_group)
    return grad_tokens, factors, grad_scale_qk


def per_device(
    tokens,
    parents,
    slot_segment,
    w_query,
    w_key,
    w_value,
    w_attn_out,
    w_up,
    w_gate,
    w_down,
    alpha_attn,
    alpha_mlp,
    scale_qk,
    scale_up,
    scale_gate,
    cotangent,
):
    local_heads = w_query.shape[1]
    local_hidden = w_up.shape[1]
    vectors = (alpha_attn, alpha_mlp, scale_qk, scale_up, scale_gate)
    spread = ("shard", "ctx")
    gathered = (
        lax.all_gather(w_query, spread, axis=0, tiled=True),
        lax.all_gather(w_key, spread, axis=0, tiled=True),
        lax.all_gather(w_value, spread, axis=0, tiled=True),
        lax.all_gather(w_attn_out, spread, axis=1, tiled=True),
        lax.all_gather(w_up, spread, axis=0, tiled=True),
        lax.all_gather(w_gate, spread, axis=0, tiled=True),
        lax.all_gather(w_down, spread, axis=1, tiled=True),
    )
    micros = range(tokens.shape[0])
    front = [
        forward_attention(gathered, vectors, tokens[m, 0], parents[m, 0], slot_segment[m, 0])
        for m in micros
    ]
    mid = [
        feed_forward(gathered, vectors, tokens[m, 0], front[m][0], cotangent[m, 0]) for m in micros
    ]
    back = [
        backward_attention(gathered, vectors, front[m][1], mid[m][2], mid[m][1]) for m in micros
    ]

    def stack(pick):
        return jnp.concatenate([pick(m) for m in micros], axis=0)

    mixed_all, top_all, hidden_all, up_all, gate_all = (
        stack(lambda m: mid[m][3][place]) for place in range(5)
    )
    tokens_all, query_all, key_all, value_all, heads_all, branch_all = (
        stack(lambda m: back[m][1][place]) for place in range(6)
    )

    def to_owner(former, latter, axis):
        product = contract_rows(former, latter).astype(jnp.bfloat16)
        return lax.psum_scatter(product, spread, scatter_dimension=axis, tiled=True).astype(
            jnp.float32
        )

    grad_d = to_owner(mixed_all, top_all, 1)
    grad_u = to_owner(hidden_all, up_all, 0)
    grad_g = to_owner(hidden_all, gate_all, 0)
    grad_o = to_owner(heads_all, branch_all, 1)
    grad_q = to_owner(tokens_all, query_all, 0)
    grad_k = to_owner(tokens_all, key_all, 0)
    grad_v = to_owner(tokens_all, value_all, 0)

    sum_attn, sum_mlp, sum_up, sum_gate = (
        sum(mid[m][4][place] for m in micros) for place in range(4)
    )
    sum_qk = sum(back[m][2] for m in micros)
    tp_count = lax.axis_size("tp")
    tp_place = lax.axis_index("tp")

    def padded(vector):
        return lax.dynamic_update_slice_in_dim(
            jnp.zeros((vector.shape[0] * tp_count,), jnp.float32),
            vector,
            tp_place * vector.shape[0],
            0,
        )

    alpha_attn_sum, alpha_mlp_sum, qk_sum, up_sum, gate_sum = lax.psum(
        (sum_attn, sum_mlp, padded(sum_qk), padded(sum_up), padded(sum_gate)),
        ("shard", "ctx", "tp"),
    )
    return (
        jnp.stack([mid[m][0] for m in micros])[:, None],
        jnp.stack([back[m][0] for m in micros])[:, None],
        grad_q,
        grad_k,
        grad_v,
        grad_o,
        grad_u,
        grad_g,
        grad_d,
        alpha_attn_sum,
        alpha_mlp_sum,
        lax.dynamic_slice_in_dim(qk_sum, tp_place * local_heads, local_heads),
        lax.dynamic_slice_in_dim(up_sum, tp_place * local_hidden, local_hidden),
        lax.dynamic_slice_in_dim(gate_sum, tp_place * local_hidden, local_hidden),
    )


def solution(mesh):
    return jax.shard_map(
        per_device,
        mesh=mesh,
        in_specs=(
            P(None, "shard", ("ctx", "tp"), None),
            P(None, "shard", None),
            P(None, "shard", None),
            P(("shard", "ctx"), "tp"),
            P(("shard", "ctx"), "tp"),
            P(("shard", "ctx"), "tp"),
            P("tp", ("shard", "ctx")),
            P(("shard", "ctx"), "tp"),
            P(("shard", "ctx"), "tp"),
            P("tp", ("shard", "ctx")),
            P(),
            P(),
            P("tp"),
            P("tp"),
            P("tp"),
            P(None, "shard", ("ctx", "tp"), None),
        ),
        out_specs=(
            P(None, "shard", ("ctx", "tp"), None),
            P(None, "shard", ("ctx", "tp"), None),
            P(("shard", "ctx"), "tp"),
            P(("shard", "ctx"), "tp"),
            P(("shard", "ctx"), "tp"),
            P("tp", ("shard", "ctx")),
            P(("shard", "ctx"), "tp"),
            P(("shard", "ctx"), "tp"),
            P("tp", ("shard", "ctx")),
            P(),
            P(),
            P("tp"),
            P("tp"),
            P("tp"),
        ),
        check_vma=False,
    )
```

```python
import math

import jax
import jax.numpy as jnp
from jax import lax
from jax.sharding import PartitionSpec as P

D = 1280
HDIM = 64
SEG = 64
SEGS = 40
TREE_TOK = 2560


EPSILON = 1e-06
MASKED = -1e30
HIGHEST = lax.Precision.HIGHEST


def unit_rows(values):
    return values * lax.rsqrt(jnp.sum(values * values, axis=-1, keepdims=True) + EPSILON)


def unit_heads(values):
    shaped = values.reshape(values.shape[0], values.shape[1] // HDIM, HDIM)
    return unit_rows(shaped).reshape(values.shape)


def contract_rows(former, latter):
    return lax.dot_general(
        former, latter, (((0,), (0,)), ((), ())), preferred_element_type=jnp.float32
    )


def contract_cols(former, latter):
    return lax.dot_general(
        former, latter, (((1,), (1,)), ((), ())), preferred_element_type=jnp.float32
    )


def split_heads(values):
    return values.reshape(values.shape[0], values.shape[1] // HDIM, HDIM).transpose(1, 0, 2)


def merge_heads(values):
    return values.transpose(1, 0, 2).reshape(values.shape[1], values.shape[0] * values.shape[2])


def mix_rows(residual, branch, mixing):
    return unit_rows(residual + mixing * (unit_rows(branch) - residual))


def query_key(query_raw, key_raw, gain_qk):
    return (unit_heads(query_raw) * gain_qk, unit_heads(key_raw) * gain_qk)


def middle(up_raw, gate_raw, scale_up, scale_gate):
    return up_raw * scale_up * jax.nn.silu(gate_raw * (scale_gate * math.sqrt(D)))


def swap(value, axis, bit):
    size = lax.axis_size(axis)
    return lax.ppermute(value, axis, [(place, place ^ bit) for place in range(size)])


def add_low(former, latter):
    return (former.astype(jnp.float32) + latter.astype(jnp.float32)).astype(jnp.bfloat16)


def butterfly(value, axes):
    for axis in axes:
        bit = 1
        while bit < lax.axis_size(axis):
            value = value + swap(value, axis, bit)
            bit *= 2
    return value


def line_order():
    size = lax.axis_size("tp")
    places = jnp.arange(size, dtype=jnp.int32)
    if size != 4:
        return places
    return (places + lax.axis_index("tp")) % size


def line_gather(own_block):
    if lax.axis_size("tp") != 4:
        return lax.all_gather(own_block, "tp", axis=0, tiled=True)
    right_one = lax.ppermute(own_block, "tp", [(0, 1), (1, 2), (2, 3)])
    left_one = lax.ppermute(own_block, "tp", [(3, 2), (2, 1), (1, 0)])
    right_two = lax.ppermute(right_one, "tp", [(1, 2), (2, 3)])
    left_two = lax.ppermute(left_one, "tp", [(2, 1), (1, 0)])
    right_three = lax.ppermute(right_two, "tp", [(2, 3)])
    left_three = lax.ppermute(left_two, "tp", [(1, 0)])
    return jnp.concatenate(
        [own_block, left_one + right_three, left_two + right_two, left_three + right_one], axis=0
    )


def line_scatter(partial_low):
    if lax.axis_size("tp") != 4:
        return lax.psum_scatter(partial_low, "tp", scatter_dimension=0, tiled=True).astype(
            jnp.float32
        )
    own, one, two, three = jnp.split(partial_low, 4, axis=0)
    right = lax.ppermute(three, "tp", [(0, 1)])
    left = lax.ppermute(one, "tp", [(3, 2)])
    right = lax.ppermute(add_low(right, two), "tp", [(0, 1), (1, 2)])
    left = lax.ppermute(add_low(left, two), "tp", [(3, 2), (2, 1)])
    right = lax.ppermute(add_low(right, one), "tp", [(0, 1), (1, 2), (2, 3)])
    left = lax.ppermute(add_low(left, three), "tp", [(3, 2), (2, 1), (1, 0)])
    return own.astype(jnp.float32) + right.astype(jnp.float32) + left.astype(jnp.float32)


def tree_order():
    size = lax.axis_size("ctx")
    places = jnp.arange(size, dtype=jnp.int32)
    if size != 4:
        return places
    return places ^ lax.axis_index("ctx")


def tree_gather(own_block):
    if lax.axis_size("ctx") != 4:
        return lax.all_gather(own_block, "ctx", axis=0, tiled=True)
    across = swap(own_block, "ctx", 2)
    beside = swap(own_block, "ctx", 1)
    return jnp.concatenate([own_block, beside, across, swap(across, "ctx", 1)], axis=0)


def tree_scatter(partial_low):
    if lax.axis_size("ctx") != 4:
        return lax.psum_scatter(partial_low, "ctx", scatter_dimension=0, tiled=True).astype(
            jnp.float32
        )
    own, beside, across, far = jnp.split(partial_low, 4, axis=0)
    across = add_low(across, swap(far, "ctx", 1))
    beside = swap(beside, "ctx", 1)
    across = swap(across, "ctx", 2)
    return own.astype(jnp.float32) + beside.astype(jnp.float32) + across.astype(jnp.float32)


def owner_scatter(product_low):
    if lax.axis_size("ctx") != 4 or lax.axis_size("shard") != 2:
        return lax.psum_scatter(
            product_low, ("shard", "ctx"), scatter_dimension=0, tiled=True
        ).astype(jnp.float32)
    place = lax.axis_index("ctx")
    core, along = place % 2, place // 2
    plane = lax.axis_index("shard")
    rows, width = product_low.shape
    blocks = product_low.reshape(2, 2, 2, rows // 8, width)

    def pick(value, index, axis):
        return lax.dynamic_index_in_dim(value, index, axis, keepdims=False)

    blocks = add_low(pick(blocks, core, 2), swap(pick(blocks, 1 - core, 2), "ctx", 1))
    former, latter = blocks[..., : width // 2], blocks[..., width // 2 :]
    former_in = swap(pick(former, 1 - along, 1), "ctx", 2)
    latter_in = swap(pick(latter, 1 - plane, 0), "shard", 1)
    former = add_low(pick(former, along, 1), former_in)
    latter = add_low(pick(latter, plane, 0), latter_in)
    former_in = swap(pick(former, 1 - plane, 0), "shard", 1)
    latter_in = swap(pick(latter, 1 - along, 0), "ctx", 2)
    return jnp.concatenate(
        [
            pick(former, plane, 0).astype(jnp.float32) + former_in.astype(jnp.float32),
            pick(latter, along, 0).astype(jnp.float32) + latter_in.astype(jnp.float32),
        ],
        axis=1,
    )


def row_labels(slots, group_size):
    tree_rows = group_size * lax.axis_size("ctx")
    chunk = group_size // lax.axis_size("tp")
    within = (line_order()[:, None] * chunk + jnp.arange(chunk, dtype=jnp.int32)).reshape(-1)
    keys = (tree_order()[:, None] * group_size + within[None, :]).reshape(-1)
    onehot = (keys[:, None] // SEG == jnp.arange(tree_rows // SEG, dtype=jnp.int32)[None, :])
    segment = jnp.sum(jnp.where(onehot, slots[None, :], 0), axis=1)
    offset = keys % SEG
    if lax.axis_size("ctx") != 4:
        first = lax.axis_index("ctx") * group_size
    else:
        first = 0
    return (
        lax.dynamic_slice_in_dim(segment, first, group_size),
        lax.dynamic_slice_in_dim(offset, first, group_size),
        segment,
        offset,
    )


def visibility(parents, slots, group_size):
    labels = jnp.arange(SEGS, dtype=jnp.int32)
    linked = (parents[:, None] == labels[None, :]).astype(jnp.float32)
    reachable = jnp.maximum(linked, jnp.eye(SEGS, dtype=jnp.float32))
    for doubling in range(SEGS.bit_length()):
        reachable = jnp.minimum(jnp.dot(reachable, reachable, precision=HIGHEST), 1.0)
    seg_query, off_query, segment, offset = row_labels(slots, group_size)
    key_onehot = (segment[:, None] == labels[None, :]).astype(jnp.float32)
    query_onehot = (seg_query[:, None] == labels[None, :]).astype(jnp.float32)
    linked_rows = jnp.dot(query_onehot, reachable, precision=HIGHEST)
    seen = (
        lax.dot_general(linked_rows, key_onehot, (((1,), (1,)), ((), ())), precision=HIGHEST) > 0.5
    )
    return seen & (
        (seg_query[:, None] != segment[None, :]) | (offset[None, :] <= off_query[:, None])
    )


def forward_attention(gathered, vectors, tokens_own, parents, slots):
    w_query, w_key, w_value, w_attn_out = gathered[:4]
    alpha_attn, alpha_mlp, scale_qk, scale_up, scale_gate = vectors
    score_scale = math.sqrt(HDIM)
    hidden_group = line_gather(tokens_own)
    visible = visibility(parents, slots, hidden_group.shape[0])
    query_raw = jnp.dot(hidden_group, w_query, preferred_element_type=jnp.float32)
    key_raw = jnp.dot(hidden_group, w_key, preferred_element_type=jnp.float32)
    value_low = jnp.dot(hidden_group, w_value, preferred_element_type=jnp.float32).astype(
        jnp.bfloat16
    )
    query_unit, key_unit = query_key(query_raw, key_raw, scale_qk)
    queries = query_unit.astype(jnp.bfloat16)
    keys_own = key_unit.astype(jnp.bfloat16)
    keys_values = tree_gather(jnp.concatenate([keys_own, value_low], axis=1))
    keys_tree, values_tree = jnp.split(keys_values, 2, axis=1)
    query_heads = split_heads(queries)
    key_heads = split_heads(keys_tree)
    value_heads = split_heads(values_tree)

    def head_forward(record):
        query_one, key_one, value_one = record
        scores = jnp.where(visible, contract_cols(query_one, key_one) * score_scale, MASKED)
        row_peak = jnp.max(scores, axis=-1, keepdims=True)
        lifted = jnp.exp(scores - row_peak)
        row_total = jnp.sum(lifted, axis=-1, keepdims=True)
        soft_weights = lifted / row_total
        head_value = jnp.dot(
            soft_weights.astype(jnp.bfloat16), value_one, preferred_element_type=jnp.float32
        )
        return (head_value, (row_peak + jnp.log(row_total))[:, 0])

    head_values, log_totals = lax.map(head_forward, (query_heads, key_heads, value_heads))
    heads_low = merge_heads(head_values).astype(jnp.bfloat16)
    branch_one = line_scatter(contract_cols(heads_low, w_attn_out).astype(jnp.bfloat16))
    kept = (
        hidden_group,
        visible,
        query_raw,
        key_raw,
        query_heads,
        key_heads,
        value_heads,
        log_totals,
        heads_low,
    )
    return branch_one, kept


def feed_forward(gathered, vectors, tokens_own, branch_one, cotangent_own):
    w_up, w_gate, w_down = gathered[4:]
    alpha_attn, alpha_mlp, scale_qk, scale_up, scale_gate = vectors
    tokens_wide = tokens_own.astype(jnp.float32)
    hidden_one = mix_rows(tokens_wide, branch_one, alpha_attn)
    hidden_one_group = line_gather(hidden_one.astype(jnp.bfloat16))
    up_raw = jnp.dot(hidden_one_group, w_up, preferred_element_type=jnp.float32)
    gate_raw = jnp.dot(hidden_one_group, w_gate, preferred_element_type=jnp.float32)
    mixed_low = middle(up_raw, gate_raw, scale_up, scale_gate).astype(jnp.bfloat16)
    branch_two = line_scatter(contract_cols(mixed_low, w_down).astype(jnp.bfloat16))
    output_wide, pull_out = jax.vjp(mix_rows, hidden_one, branch_two, alpha_mlp)
    upstream = cotangent_own.astype(jnp.float32)
    hidden_one_direct, branch_two_grad, grad_alpha_mlp = pull_out(upstream)
    branch_two_group = line_gather(branch_two_grad.astype(jnp.bfloat16))
    mixed_grad = (
        jnp.dot(branch_two_group, w_down, preferred_element_type=jnp.float32)
        .astype(jnp.bfloat16)
        .astype(jnp.float32)
    )
    middle_value, pull_mid = jax.vjp(middle, up_raw, gate_raw, scale_up, scale_gate)
    up_grad, gate_grad, grad_scale_up, grad_scale_gate = pull_mid(mixed_grad)
    up_low = up_grad.astype(jnp.bfloat16)
    gate_low = gate_grad.astype(jnp.bfloat16)
    hidden_one_grad = hidden_one_direct + line_scatter(
        (contract_cols(up_low, w_up) + contract_cols(gate_low, w_gate)).astype(jnp.bfloat16)
    )
    hidden_again, pull_in = jax.vjp(mix_rows, tokens_wide, branch_one, alpha_attn)
    tokens_direct, branch_one_grad, grad_alpha_attn = pull_in(hidden_one_grad)
    factors = (mixed_low, branch_two_group, hidden_one_group, up_low, gate_low)
    sums = (grad_alpha_attn, grad_alpha_mlp, grad_scale_up, grad_scale_gate)
    return output_wide.astype(jnp.bfloat16), tokens_direct, branch_one_grad, factors, sums


def backward_attention(gathered, vectors, kept, branch_one_grad, tokens_direct):
    w_query, w_key, w_value, w_attn_out = gathered[:4]
    scale_qk = vectors[2]
    score_scale = math.sqrt(HDIM)
    (
        hidden_group,
        visible,
        query_raw,
        key_raw,
        query_heads,
        key_heads,
        value_heads,
        log_totals,
        heads_low,
    ) = kept
    branch_one_group = line_gather(branch_one_grad.astype(jnp.bfloat16))
    heads_grad = split_heads(
        jnp.dot(branch_one_group, w_attn_out, preferred_element_type=jnp.float32).astype(
            jnp.bfloat16
        )
    )

    def head_backward(record):
        query_one, key_one, value_one, upstream_one, log_total = record
        scores = jnp.where(visible, contract_cols(query_one, key_one) * score_scale, MASKED)
        soft_weights = jnp.exp(scores - log_total[:, None])
        weight_grad = contract_cols(upstream_one, value_one)
        row_inner = jnp.sum(soft_weights * weight_grad, axis=-1, keepdims=True)
        score_grad = (soft_weights * (weight_grad - row_inner)).astype(jnp.bfloat16)
        query_grad = jnp.dot(score_grad, key_one, preferred_element_type=jnp.float32) * score_scale
        key_grad = contract_rows(score_grad, query_one) * score_scale
        value_grad = contract_rows(soft_weights.astype(jnp.bfloat16), upstream_one)
        return (query_grad, key_grad, value_grad)

    query_grads, key_grads, value_grads = lax.map(
        head_backward, (query_heads, key_heads, value_heads, heads_grad, log_totals)
    )
    both = tree_scatter(
        jnp.concatenate([merge_heads(key_grads), merge_heads(value_grads)], axis=1).astype(
            jnp.bfloat16
        )
    )
    key_own_grad, value_own_grad = jnp.split(both, 2, axis=1)
    unit_again, pull_qk = jax.vjp(query_key, query_raw, key_raw, scale_qk)
    query_raw_grad, key_raw_grad, grad_scale_qk = pull_qk((merge_heads(query_grads), key_own_grad))
    query_low = query_raw_grad.astype(jnp.bfloat16)
    key_low = key_raw_grad.astype(jnp.bfloat16)
    value_grad_low = value_own_grad.astype(jnp.bfloat16)
    input_part = (
        contract_cols(query_low, w_query)
        + contract_cols(key_low, w_key)
        + contract_cols(value_grad_low, w_value)
    )
    grad_tokens = tokens_direct + line_scatter(input_part.astype(jnp.bfloat16))
    factors = (hidden_group, query_low, key_low, value_grad_low, heads_low, branch_one_group)
    return grad_tokens, factors, grad_scale_qk


def per_device(
    tokens,
    parents,
    slot_segment,
    w_query,
    w_key,
    w_value,
    w_attn_out,
    w_up,
    w_gate,
    w_down,
    alpha_attn,
    alpha_mlp,
    scale_qk,
    scale_up,
    scale_gate,
    cotangent,
):
    local_heads = w_query.shape[1]
    local_hidden = w_up.shape[1]
    vectors = (alpha_attn, alpha_mlp, scale_qk, scale_up, scale_gate)
    spread = ("shard", "ctx")

    def spread_gather(own_block):
        return lax.all_gather(own_block, spread, axis=0, tiled=True)

    packed = spread_gather(jnp.concatenate([w_query, w_key, w_value, w_attn_out.T], axis=1))
    gathered = (
        packed[:, :local_heads],
        packed[:, local_heads : 2 * local_heads],
        packed[:, 2 * local_heads : 3 * local_heads],
        packed[:, 3 * local_heads :],
        spread_gather(w_up),
        spread_gather(w_gate),
        spread_gather(w_down.T),
    )
    micros = range(tokens.shape[0])
    front = [
        forward_attention(gathered, vectors, tokens[m, 0], parents[m, 0], slot_segment[m, 0])
        for m in micros
    ]
    mid = [
        feed_forward(gathered, vectors, tokens[m, 0], front[m][0], cotangent[m, 0]) for m in micros
    ]
    back = [
        backward_attention(gathered, vectors, front[m][1], mid[m][2], mid[m][1]) for m in micros
    ]

    def stack(pick):
        return jnp.concatenate([pick(m) for m in micros], axis=0)

    mixed_all, top_all, hidden_all, up_all, gate_all = (
        stack(lambda m: mid[m][3][place]) for place in range(5)
    )
    tokens_all, query_all, key_all, value_all, heads_all, branch_all = (
        stack(lambda m: back[m][1][place]) for place in range(6)
    )

    def to_owner(former, latter):
        return owner_scatter(contract_rows(former, latter).astype(jnp.bfloat16))

    grad_d = to_owner(top_all, mixed_all).T
    grad_u = to_owner(hidden_all, up_all)
    grad_g = to_owner(hidden_all, gate_all)
    attention_product = jnp.concatenate(
        [
            contract_rows(tokens_all, query_all),
            contract_rows(tokens_all, key_all),
            contract_rows(tokens_all, value_all),
            contract_rows(branch_all, heads_all),
        ],
        axis=1,
    )
    grad_attention = owner_scatter(attention_product.astype(jnp.bfloat16))
    grad_q, grad_k, grad_v, grad_o = jnp.split(grad_attention, 4, axis=1)

    sum_attn, sum_mlp, sum_up, sum_gate = (
        sum(mid[m][4][place] for m in micros) for place in range(4)
    )
    sum_qk = butterfly(sum(back[m][2] for m in micros), spread)
    width = sum_attn.shape[0]
    sums = butterfly(jnp.concatenate([sum_attn, sum_mlp, sum_up, sum_gate]), spread)
    alphas = butterfly(sums[: 2 * width], ("tp",))
    return (
        jnp.stack([mid[m][0] for m in micros])[:, None],
        jnp.stack([back[m][0] for m in micros])[:, None],
        grad_q,
        grad_k,
        grad_v,
        grad_o.T,
        grad_u,
        grad_g,
        grad_d,
        alphas[:width],
        alphas[width:],
        sum_qk,
        sums[2 * width : 2 * width + local_hidden],
        sums[2 * width + local_hidden :],
    )


def solution(mesh):
    return jax.shard_map(
        per_device,
        mesh=mesh,
        in_specs=(
            P(None, "shard", ("ctx", "tp"), None),
            P(None, "shard", None),
            P(None, "shard", None),
            P(("shard", "ctx"), "tp"),
            P(("shard", "ctx"), "tp"),
            P(("shard", "ctx"), "tp"),
            P("tp", ("shard", "ctx")),
            P(("shard", "ctx"), "tp"),
            P(("shard", "ctx"), "tp"),
            P("tp", ("shard", "ctx")),
            P(),
            P(),
            P("tp"),
            P("tp"),
            P("tp"),
            P(None, "shard", ("ctx", "tp"), None),
        ),
        out_specs=(
            P(None, "shard", ("ctx", "tp"), None),
            P(None, "shard", ("ctx", "tp"), None),
            P(("shard", "ctx"), "tp"),
            P(("shard", "ctx"), "tp"),
            P(("shard", "ctx"), "tp"),
            P("tp", ("shard", "ctx")),
            P(("shard", "ctx"), "tp"),
            P(("shard", "ctx"), "tp"),
            P("tp", ("shard", "ctx")),
            P(),
            P(),
            P("tp"),
            P("tp"),
            P("tp"),
        ),
        check_vma=False,
    )
```

```python
import math

import jax
import jax.numpy as jnp
from jax import lax
from jax.experimental import pallas as pl
from jax.experimental.pallas import tpu as pltpu
from jax.sharding import PartitionSpec as P

D = 1280
HDIM = 64
SEG = 64
SEGS = 40
TREE_TOK = 2560


EPSILON = 1e-06
MASKED = -1e30
HIGHEST = lax.Precision.HIGHEST


def unit_rows(values):
    return values * lax.rsqrt(jnp.sum(values * values, axis=-1, keepdims=True) + EPSILON)


def unit_heads(values):
    shaped = values.reshape(values.shape[0], values.shape[1] // HDIM, HDIM)
    return unit_rows(shaped).reshape(values.shape)


def contract_rows(former, latter):
    return lax.dot_general(
        former, latter, (((0,), (0,)), ((), ())), preferred_element_type=jnp.float32
    )


def contract_cols(former, latter):
    return lax.dot_general(
        former, latter, (((1,), (1,)), ((), ())), preferred_element_type=jnp.float32
    )


def mix_rows(residual, branch, mixing):
    return unit_rows(residual + mixing * (unit_rows(branch) - residual))


def query_key(query_raw, key_raw, gain_qk):
    return (unit_heads(query_raw) * gain_qk, unit_heads(key_raw) * gain_qk)


def middle(up_raw, gate_raw, scale_up, scale_gate):
    return up_raw * scale_up * jax.nn.silu(gate_raw * (scale_gate * math.sqrt(D)))


def swap(value, axis, bit):
    size = lax.axis_size(axis)
    return lax.ppermute(value, axis, [(place, place ^ bit) for place in range(size)])


def add_low(former, latter):
    return (former.astype(jnp.float32) + latter.astype(jnp.float32)).astype(jnp.bfloat16)


def butterfly(value, axes):
    for axis in axes:
        bit = 1
        while bit < lax.axis_size(axis):
            value = value + swap(value, axis, bit)
            bit *= 2
    return value


def line_order():
    size = lax.axis_size("tp")
    places = jnp.arange(size, dtype=jnp.int32)
    if size != 4:
        return places
    return (places + lax.axis_index("tp")) % size


def line_gather(own_block):
    if lax.axis_size("tp") != 4:
        return lax.all_gather(own_block, "tp", axis=0, tiled=True)
    right_one = lax.ppermute(own_block, "tp", [(0, 1), (1, 2), (2, 3)])
    left_one = lax.ppermute(own_block, "tp", [(3, 2), (2, 1), (1, 0)])
    right_two = lax.ppermute(right_one, "tp", [(1, 2), (2, 3)])
    left_two = lax.ppermute(left_one, "tp", [(2, 1), (1, 0)])
    right_three = lax.ppermute(right_two, "tp", [(2, 3)])
    left_three = lax.ppermute(left_two, "tp", [(1, 0)])
    return jnp.concatenate(
        [own_block, left_one + right_three, left_two + right_two, left_three + right_one], axis=0
    )


def line_scatter(partial_low):
    if lax.axis_size("tp") != 4:
        return lax.psum_scatter(partial_low, "tp", scatter_dimension=0, tiled=True).astype(
            jnp.float32
        )
    own, one, two, three = jnp.split(partial_low, 4, axis=0)
    right = lax.ppermute(three, "tp", [(0, 1)])
    left = lax.ppermute(one, "tp", [(3, 2)])
    right = lax.ppermute(add_low(right, two), "tp", [(0, 1), (1, 2)])
    left = lax.ppermute(add_low(left, two), "tp", [(3, 2), (2, 1)])
    right = lax.ppermute(add_low(right, one), "tp", [(0, 1), (1, 2), (2, 3)])
    left = lax.ppermute(add_low(left, three), "tp", [(3, 2), (2, 1), (1, 0)])
    return own.astype(jnp.float32) + right.astype(jnp.float32) + left.astype(jnp.float32)


def tree_order():
    size = lax.axis_size("ctx")
    places = jnp.arange(size, dtype=jnp.int32)
    if size != 4:
        return places
    return places ^ lax.axis_index("ctx")


def tree_gather(own_block):
    if lax.axis_size("ctx") != 4:
        return lax.all_gather(own_block, "ctx", axis=0, tiled=True)
    across = swap(own_block, "ctx", 2)
    beside = swap(own_block, "ctx", 1)
    return jnp.concatenate([own_block, beside, across, swap(across, "ctx", 1)], axis=0)


def tree_scatter(partial_low):
    if lax.axis_size("ctx") != 4:
        return lax.psum_scatter(partial_low, "ctx", scatter_dimension=0, tiled=True).astype(
            jnp.float32
        )
    own, beside, across, far = jnp.split(partial_low, 4, axis=0)
    across = add_low(across, swap(far, "ctx", 1))
    beside = swap(beside, "ctx", 1)
    across = swap(across, "ctx", 2)
    return own.astype(jnp.float32) + beside.astype(jnp.float32) + across.astype(jnp.float32)


def owner_scatter(product_low):
    if lax.axis_size("ctx") != 4 or lax.axis_size("shard") != 2:
        return lax.psum_scatter(
            product_low, ("shard", "ctx"), scatter_dimension=0, tiled=True
        ).astype(jnp.float32)
    place = lax.axis_index("ctx")
    core, along = place % 2, place // 2
    plane = lax.axis_index("shard")
    rows, width = product_low.shape
    blocks = product_low.reshape(2, 2, 2, rows // 8, width)

    def pick(value, index, axis):
        return lax.dynamic_index_in_dim(value, index, axis, keepdims=False)

    blocks = add_low(pick(blocks, core, 2), swap(pick(blocks, 1 - core, 2), "ctx", 1))
    former, latter = blocks[..., : width // 2], blocks[..., width // 2 :]
    former_in = swap(pick(former, 1 - along, 1), "ctx", 2)
    latter_in = swap(pick(latter, 1 - plane, 0), "shard", 1)
    former = add_low(pick(former, along, 1), former_in)
    latter = add_low(pick(latter, plane, 0), latter_in)
    former_in = swap(pick(former, 1 - plane, 0), "shard", 1)
    latter_in = swap(pick(latter, 1 - along, 0), "ctx", 2)
    return jnp.concatenate(
        [
            pick(former, plane, 0).astype(jnp.float32) + former_in.astype(jnp.float32),
            pick(latter, along, 0).astype(jnp.float32) + latter_in.astype(jnp.float32),
        ],
        axis=1,
    )


def row_labels(slots, group_size):
    tree_rows = group_size * lax.axis_size("ctx")
    chunk = group_size // lax.axis_size("tp")
    within = (line_order()[:, None] * chunk + jnp.arange(chunk, dtype=jnp.int32)).reshape(-1)
    keys = (tree_order()[:, None] * group_size + within[None, :]).reshape(-1)
    onehot = (keys[:, None] // SEG == jnp.arange(tree_rows // SEG, dtype=jnp.int32)[None, :])
    segment = jnp.sum(jnp.where(onehot, slots[None, :], 0), axis=1)
    offset = keys % SEG
    if lax.axis_size("ctx") != 4:
        first = lax.axis_index("ctx") * group_size
    else:
        first = 0
    return (
        lax.dynamic_slice_in_dim(segment, first, group_size),
        lax.dynamic_slice_in_dim(offset, first, group_size),
        segment,
        offset,
    )


LOG2_SCALE = math.sqrt(HDIM) * math.log2(math.e)
LANES = 128
KEY_TILE = 256


def half_kept(value, unit, axis):
    place = lax.broadcasted_iota(jnp.int32, value.shape, axis)
    inside = (place >= HDIM) if unit % 2 else (place < HDIM)
    return jnp.where(inside, value, jnp.zeros_like(value))


def seen_tile(hot_ref, side_ref):
    hot = hot_ref[...]
    strict = jnp.dot(hot, side_ref[0], preferred_element_type=jnp.float32)
    same = jnp.dot(hot, side_ref[1], preferred_element_type=jnp.float32)
    before = jnp.dot(hot, side_ref[2], preferred_element_type=jnp.float32)
    return (strict + same * before).astype(jnp.bfloat16)


def pair_of(unit):
    return slice(unit // 2 * LANES, unit // 2 * LANES + LANES)


def attend_body(query_ref, tree_ref, hot_ref, side_ref, out_ref, scale_ref, turned_ref, sum_ref):
    heads = query_ref.shape[1] // HDIM
    step = pl.program_id(0)

    @pl.when(step == 0)
    def prepare():
        turned = query_ref[...].astype(jnp.float32).T.astype(jnp.bfloat16)
        blank = jnp.zeros((HDIM, turned.shape[1]), jnp.bfloat16)
        for head in range(heads):
            own = turned[head * HDIM : (head + 1) * HDIM]
            halves = [blank, own] if head % 2 else [own, blank]
            turned_ref[head] = jnp.concatenate(halves, axis=0)
        sum_ref[...] = jnp.zeros_like(sum_ref)

    tree = tree_ref[...]
    values_turned = tree[:, heads * HDIM :].astype(jnp.float32).T.astype(jnp.bfloat16)
    seen = seen_tile(hot_ref, side_ref)
    ones = jnp.ones((sum_ref.shape[1] - HDIM, tree.shape[0]), jnp.bfloat16)
    for head in range(heads):
        scores = jnp.dot(tree[:, pair_of(head)], turned_ref[head], preferred_element_type=jnp.float32)
        lifted = jnp.exp2(scores * LOG2_SCALE).astype(jnp.bfloat16) * seen
        own = jnp.concatenate([values_turned[head * HDIM : (head + 1) * HDIM], ones], axis=0)
        sum_ref[head] += jnp.dot(own, lifted, preferred_element_type=jnp.float32)

    @pl.when(step == pl.num_programs(0) - 1)
    def finish():
        parts = []
        for head in range(heads):
            inverse = 1.0 / sum_ref[head, HDIM : HDIM + 1]
            scale_ref[head : head + 1] = inverse
            parts.append(sum_ref[head, :HDIM] * inverse)
        out_ref[...] = jnp.concatenate(parts, axis=0).T.astype(jnp.bfloat16)


def attend(query, tree, hot, side):
    rows, features = query.shape
    keys, width = tree.shape
    heads = features // HDIM
    whole = lambda step: (0, 0)
    return pl.pallas_call(
        attend_body,
        grid=(keys // KEY_TILE,),
        in_specs=[
            pl.BlockSpec((rows, features), whole),
            pl.BlockSpec((KEY_TILE, width), lambda step: (step, 0)),
            pl.BlockSpec((KEY_TILE, LANES), lambda step: (step, 0)),
            pl.BlockSpec((3, LANES, rows), lambda step: (0, 0, 0)),
        ],
        out_specs=[
            pl.BlockSpec((rows, features), whole),
            pl.BlockSpec((8, rows), whole),
        ],
        out_shape=[
            jax.ShapeDtypeStruct((rows, features), jnp.bfloat16),
            jax.ShapeDtypeStruct((8, rows), jnp.float32),
        ],
        scratch_shapes=[
            pltpu.VMEM((heads, LANES, rows), jnp.bfloat16),
            pltpu.VMEM((heads, HDIM + 16, rows), jnp.float32),
        ],
        compiler_params=pltpu.CompilerParams(vmem_limit_bytes=48 << 20),
        name="attend",
    )(query, tree, hot, side)


def attend_grad_body(
    both_ref, heads_ref, tree_ref, hot_ref, side_ref, scale_ref,
    query_out, tree_out, turned_ref, plain_ref, delta_ref, sum_ref,
):
    heads = heads_ref.shape[1] // HDIM
    units = 2 * heads
    step = pl.program_id(0)

    @pl.when(step == 0)
    def prepare():
        both = both_ref[...]
        turned = both.astype(jnp.float32).T
        outs = heads_ref[...].astype(jnp.float32).T
        blank = jnp.zeros((HDIM, turned.shape[1]), jnp.bfloat16)
        for unit in range(units):
            own = turned[unit * HDIM : (unit + 1) * HDIM].astype(jnp.bfloat16)
            halves = [blank, own] if unit % 2 else [own, blank]
            turned_ref[unit] = jnp.concatenate(halves, axis=0)
            plain_ref[unit] = half_kept(both[:, pair_of(unit)], unit, 1)
        for head in range(heads):
            rows = slice(head * HDIM, (head + 1) * HDIM)
            upstream = turned[(heads + head) * HDIM : (heads + head + 1) * HDIM]
            delta_ref[head : head + 1] = jnp.sum(outs[rows] * upstream, axis=0, keepdims=True)
        sum_ref[...] = jnp.zeros_like(sum_ref)

    tree = tree_ref[...]
    keys_turned = tree[:, : heads * HDIM].astype(jnp.float32).T.astype(jnp.bfloat16)
    seen = seen_tile(hot_ref, side_ref)
    weights, slopes = [], []
    for head in range(heads):
        scores = jnp.dot(tree[:, pair_of(head)], turned_ref[head], preferred_element_type=jnp.float32)
        weight = jnp.exp2(scores * LOG2_SCALE) * scale_ref[head : head + 1]
        pull = jnp.dot(
            tree[:, pair_of(heads + head)], turned_ref[heads + head], preferred_element_type=jnp.float32
        )
        slope = (weight * (pull - delta_ref[head : head + 1])).astype(jnp.bfloat16) * seen
        rows = slice(head * HDIM, (head + 1) * HDIM)
        sum_ref[rows] += jnp.dot(keys_turned[rows], slope, preferred_element_type=jnp.float32)
        weights.append(weight.astype(jnp.bfloat16) * seen)
        slopes.append(slope)
    terms = slopes + weights
    score_scale = math.sqrt(HDIM)
    for pair in range(heads):
        total = 0.0
        for unit in (2 * pair, 2 * pair + 1):
            part = jnp.dot(terms[unit], plain_ref[unit], preferred_element_type=jnp.float32)
            total = total + (part * score_scale if unit < heads else part)
        tree_out[:, pair * LANES : (pair + 1) * LANES] = total.astype(jnp.bfloat16)

    @pl.when(step == pl.num_programs(0) - 1)
    def finish():
        query_out[...] = sum_ref[...].T * score_scale


def attend_grad(query, upstream, outs, tree, hot, side, scale):
    rows, features = query.shape
    keys, width = tree.shape
    heads = features // HDIM
    whole = lambda step: (0, 0)
    return pl.pallas_call(
        attend_grad_body,
        grid=(keys // KEY_TILE,),
        in_specs=[
            pl.BlockSpec((rows, 2 * features), whole),
            pl.BlockSpec((rows, features), whole),
            pl.BlockSpec((KEY_TILE, width), lambda step: (step, 0)),
            pl.BlockSpec((KEY_TILE, LANES), lambda step: (step, 0)),
            pl.BlockSpec((3, LANES, rows), lambda step: (0, 0, 0)),
            pl.BlockSpec((8, rows), whole),
        ],
        out_specs=[
            pl.BlockSpec((rows, features), whole),
            pl.BlockSpec((KEY_TILE, width), lambda step: (step, 0)),
        ],
        out_shape=[
            jax.ShapeDtypeStruct((rows, features), jnp.float32),
            jax.ShapeDtypeStruct((keys, width), jnp.bfloat16),
        ],
        scratch_shapes=[
            pltpu.VMEM((2 * heads, LANES, rows), jnp.bfloat16),
            pltpu.VMEM((2 * heads, rows, LANES), jnp.bfloat16),
            pltpu.VMEM((8, rows), jnp.float32),
            pltpu.VMEM((features, rows), jnp.float32),
        ],
        compiler_params=pltpu.CompilerParams(vmem_limit_bytes=48 << 20),
        name="attend_grad",
    )(jnp.concatenate([query, upstream], axis=1), outs, tree, hot, side, scale)


def seen_factors(reachable, seg_query, off_query, segment, offset):
    segs = reachable.shape[0]
    labels = jnp.arange(LANES, dtype=jnp.int32)
    key_mark = jnp.where(labels < HDIM, segment[:, None], offset[:, None] + HDIM)
    hot = (key_mark == labels[None, :]).astype(jnp.bfloat16)
    query_hot = (labels[:, None] == seg_query[None, :]).astype(jnp.float32)
    wide = jnp.zeros((LANES, LANES), jnp.float32).at[:segs, :segs].set(reachable.T - jnp.eye(segs, dtype=jnp.float32))
    strict = jnp.dot(wide, query_hot, preferred_element_type=jnp.float32)
    same = query_hot
    before = ((labels[:, None] >= HDIM) & (labels[:, None] - HDIM <= off_query[None, :])).astype(jnp.float32)
    return hot, jnp.stack([strict, same, before]).astype(jnp.bfloat16)


def visibility(parents, slots, group_size):
    labels = jnp.arange(SEGS, dtype=jnp.int32)
    linked = (parents[:, None] == labels[None, :]).astype(jnp.float32)
    reachable = jnp.maximum(linked, jnp.eye(SEGS, dtype=jnp.float32))
    for doubling in range(SEGS.bit_length()):
        reachable = jnp.minimum(jnp.dot(reachable, reachable, precision=HIGHEST), 1.0)
    return seen_factors(reachable, *row_labels(slots, group_size))


def forward_attention(gathered, vectors, tokens_own, parents, slots):
    w_query, w_key, w_value, w_attn_out = gathered[:4]
    alpha_attn, alpha_mlp, scale_qk, scale_up, scale_gate = vectors
    hidden_group = line_gather(tokens_own)
    visible = visibility(parents, slots, hidden_group.shape[0])
    query_raw = jnp.dot(hidden_group, w_query, preferred_element_type=jnp.float32)
    key_raw = jnp.dot(hidden_group, w_key, preferred_element_type=jnp.float32)
    value_low = jnp.dot(hidden_group, w_value, preferred_element_type=jnp.float32).astype(
        jnp.bfloat16
    )
    query_unit, key_unit = query_key(query_raw, key_raw, scale_qk)
    queries = query_unit.astype(jnp.bfloat16)
    keys_own = key_unit.astype(jnp.bfloat16)
    keys_values = tree_gather(jnp.concatenate([keys_own, value_low], axis=1))
    heads_low, scale = attend(queries, keys_values, *visible)
    branch_one = line_scatter(contract_cols(heads_low, w_attn_out).astype(jnp.bfloat16))
    kept = (
        hidden_group,
        visible,
        query_raw,
        key_raw,
        queries,
        keys_values,
        scale,
        heads_low,
    )
    return branch_one, kept


def feed_forward(gathered, vectors, tokens_own, branch_one, cotangent_own):
    w_up, w_gate, w_down = gathered[4:]
    alpha_attn, alpha_mlp, scale_qk, scale_up, scale_gate = vectors
    tokens_wide = tokens_own.astype(jnp.float32)
    hidden_one = mix_rows(tokens_wide, branch_one, alpha_attn)
    hidden_one_group = line_gather(hidden_one.astype(jnp.bfloat16))
    up_raw = jnp.dot(hidden_one_group, w_up, preferred_element_type=jnp.float32)
    gate_raw = jnp.dot(hidden_one_group, w_gate, preferred_element_type=jnp.float32)
    mixed_low = middle(up_raw, gate_raw, scale_up, scale_gate).astype(jnp.bfloat16)
    branch_two = line_scatter(contract_cols(mixed_low, w_down).astype(jnp.bfloat16))
    output_wide, pull_out = jax.vjp(mix_rows, hidden_one, branch_two, alpha_mlp)
    upstream = cotangent_own.astype(jnp.float32)
    hidden_one_direct, branch_two_grad, grad_alpha_mlp = pull_out(upstream)
    branch_two_group = line_gather(branch_two_grad.astype(jnp.bfloat16))
    mixed_grad = (
        jnp.dot(branch_two_group, w_down, preferred_element_type=jnp.float32)
        .astype(jnp.bfloat16)
        .astype(jnp.float32)
    )
    middle_value, pull_mid = jax.vjp(middle, up_raw, gate_raw, scale_up, scale_gate)
    up_grad, gate_grad, grad_scale_up, grad_scale_gate = pull_mid(mixed_grad)
    up_low = up_grad.astype(jnp.bfloat16)
    gate_low = gate_grad.astype(jnp.bfloat16)
    hidden_one_grad = hidden_one_direct + line_scatter(
        (contract_cols(up_low, w_up) + contract_cols(gate_low, w_gate)).astype(jnp.bfloat16)
    )
    hidden_again, pull_in = jax.vjp(mix_rows, tokens_wide, branch_one, alpha_attn)
    tokens_direct, branch_one_grad, grad_alpha_attn = pull_in(hidden_one_grad)
    factors = (mixed_low, branch_two_group, hidden_one_group, up_low, gate_low)
    sums = (grad_alpha_attn, grad_alpha_mlp, grad_scale_up, grad_scale_gate)
    return output_wide.astype(jnp.bfloat16), tokens_direct, branch_one_grad, factors, sums


def backward_attention(gathered, vectors, kept, branch_one_grad, tokens_direct):
    w_query, w_key, w_value, w_attn_out = gathered[:4]
    scale_qk = vectors[2]
    (
        hidden_group,
        visible,
        query_raw,
        key_raw,
        queries,
        keys_values,
        scale,
        heads_low,
    ) = kept
    branch_one_group = line_gather(branch_one_grad.astype(jnp.bfloat16))
    heads_grad = jnp.dot(
        branch_one_group, w_attn_out, preferred_element_type=jnp.float32
    ).astype(jnp.bfloat16)
    query_grads, tree_grads = attend_grad(
        queries, heads_grad, heads_low, keys_values, *visible, scale
    )
    key_own_grad, value_own_grad = jnp.split(tree_scatter(tree_grads), 2, axis=1)
    unit_again, pull_qk = jax.vjp(query_key, query_raw, key_raw, scale_qk)
    query_raw_grad, key_raw_grad, grad_scale_qk = pull_qk((query_grads, key_own_grad))
    query_low = query_raw_grad.astype(jnp.bfloat16)
    key_low = key_raw_grad.astype(jnp.bfloat16)
    value_grad_low = value_own_grad.astype(jnp.bfloat16)
    input_part = (
        contract_cols(query_low, w_query)
        + contract_cols(key_low, w_key)
        + contract_cols(value_grad_low, w_value)
    )
    grad_tokens = tokens_direct + line_scatter(input_part.astype(jnp.bfloat16))
    factors = (hidden_group, query_low, key_low, value_grad_low, heads_low, branch_one_group)
    return grad_tokens, factors, grad_scale_qk


def per_device(
    tokens,
    parents,
    slot_segment,
    w_query,
    w_key,
    w_value,
    w_attn_out,
    w_up,
    w_gate,
    w_down,
    alpha_attn,
    alpha_mlp,
    scale_qk,
    scale_up,
    scale_gate,
    cotangent,
):
    local_heads = w_query.shape[1]
    local_hidden = w_up.shape[1]
    vectors = (alpha_attn, alpha_mlp, scale_qk, scale_up, scale_gate)
    spread = ("shard", "ctx")

    def spread_gather(own_block):
        return lax.all_gather(own_block, spread, axis=0, tiled=True)

    packed = spread_gather(jnp.concatenate([w_query, w_key, w_value, w_attn_out.T], axis=1))
    gathered = (
        packed[:, :local_heads],
        packed[:, local_heads : 2 * local_heads],
        packed[:, 2 * local_heads : 3 * local_heads],
        packed[:, 3 * local_heads :],
        spread_gather(w_up),
        spread_gather(w_gate),
        spread_gather(w_down.T),
    )
    micros = range(tokens.shape[0])
    front = [
        forward_attention(gathered, vectors, tokens[m, 0], parents[m, 0], slot_segment[m, 0])
        for m in micros
    ]
    mid = [
        feed_forward(gathered, vectors, tokens[m, 0], front[m][0], cotangent[m, 0]) for m in micros
    ]
    back = [
        backward_attention(gathered, vectors, front[m][1], mid[m][2], mid[m][1]) for m in micros
    ]

    def stack(pick):
        return jnp.concatenate([pick(m) for m in micros], axis=0)

    mixed_all, top_all, hidden_all, up_all, gate_all = (
        stack(lambda m: mid[m][3][place]) for place in range(5)
    )
    tokens_all, query_all, key_all, value_all, heads_all, branch_all = (
        stack(lambda m: back[m][1][place]) for place in range(6)
    )

    def to_owner(former, latter):
        return owner_scatter(contract_rows(former, latter).astype(jnp.bfloat16))

    grad_d = to_owner(top_all, mixed_all).T
    grad_u = to_owner(hidden_all, up_all)
    grad_g = to_owner(hidden_all, gate_all)
    attention_product = jnp.concatenate(
        [
            contract_rows(tokens_all, query_all),
            contract_rows(tokens_all, key_all),
            contract_rows(tokens_all, value_all),
            contract_rows(branch_all, heads_all),
        ],
        axis=1,
    )
    grad_attention = owner_scatter(attention_product.astype(jnp.bfloat16))
    grad_q, grad_k, grad_v, grad_o = jnp.split(grad_attention, 4, axis=1)

    sum_attn, sum_mlp, sum_up, sum_gate = (
        sum(mid[m][4][place] for m in micros) for place in range(4)
    )
    sum_qk = butterfly(sum(back[m][2] for m in micros), spread)
    width = sum_attn.shape[0]
    sums = butterfly(jnp.concatenate([sum_attn, sum_mlp, sum_up, sum_gate]), spread)
    alphas = butterfly(sums[: 2 * width], ("tp",))
    return (
        jnp.stack([mid[m][0] for m in micros])[:, None],
        jnp.stack([back[m][0] for m in micros])[:, None],
        grad_q,
        grad_k,
        grad_v,
        grad_o.T,
        grad_u,
        grad_g,
        grad_d,
        alphas[:width],
        alphas[width:],
        sum_qk,
        sums[2 * width : 2 * width + local_hidden],
        sums[2 * width + local_hidden :],
    )


def solution(mesh):
    return jax.shard_map(
        per_device,
        mesh=mesh,
        in_specs=(
            P(None, "shard", ("ctx", "tp"), None),
            P(None, "shard", None),
            P(None, "shard", None),
            P(("shard", "ctx"), "tp"),
            P(("shard", "ctx"), "tp"),
            P(("shard", "ctx"), "tp"),
            P("tp", ("shard", "ctx")),
            P(("shard", "ctx"), "tp"),
            P(("shard", "ctx"), "tp"),
            P("tp", ("shard", "ctx")),
            P(),
            P(),
            P("tp"),
            P("tp"),
            P("tp"),
            P(None, "shard", ("ctx", "tp"), None),
        ),
        out_specs=(
            P(None, "shard", ("ctx", "tp"), None),
            P(None, "shard", ("ctx", "tp"), None),
            P(("shard", "ctx"), "tp"),
            P(("shard", "ctx"), "tp"),
            P(("shard", "ctx"), "tp"),
            P("tp", ("shard", "ctx")),
            P(("shard", "ctx"), "tp"),
            P(("shard", "ctx"), "tp"),
            P("tp", ("shard", "ctx")),
            P(),
            P(),
            P("tp"),
            P("tp"),
            P("tp"),
        ),
        check_vma=False,
    )
```

```python
import math

import jax
import jax.numpy as jnp
from jax import lax
from jax.experimental import pallas as pl
from jax.experimental.pallas import tpu as pltpu
from jax.sharding import PartitionSpec as P

D = 1280
HDIM = 64
SEG = 64
SEGS = 40
TREE_TOK = 2560


EPSILON = 1e-06
MASKED = -1e30
HIGHEST = lax.Precision.HIGHEST


def unit_rows(values):
    return values * lax.rsqrt(jnp.sum(values * values, axis=-1, keepdims=True) + EPSILON)


def unit_heads(values):
    shaped = values.reshape(values.shape[0], values.shape[1] // HDIM, HDIM)
    return unit_rows(shaped).reshape(values.shape)


def contract_rows(former, latter):
    return lax.dot_general(
        former, latter, (((0,), (0,)), ((), ())), preferred_element_type=jnp.float32
    )


def contract_cols(former, latter):
    return lax.dot_general(
        former, latter, (((1,), (1,)), ((), ())), preferred_element_type=jnp.float32
    )


def mix_rows(residual, branch, mixing):
    return unit_rows(residual + mixing * (unit_rows(branch) - residual))


def query_key(query_raw, key_raw, gain_qk):
    return (unit_heads(query_raw) * gain_qk, unit_heads(key_raw) * gain_qk)


def middle(up_raw, gate_raw, scale_up, scale_gate):
    return up_raw * scale_up * jax.nn.silu(gate_raw * (scale_gate * math.sqrt(D)))


def swap(value, axis, bit):
    size = lax.axis_size(axis)
    return lax.ppermute(value, axis, [(place, place ^ bit) for place in range(size)])


def add_low(former, latter):
    return (former.astype(jnp.float32) + latter.astype(jnp.float32)).astype(jnp.bfloat16)


def butterfly(value, axes):
    for axis in axes:
        bit = 1
        while bit < lax.axis_size(axis):
            value = value + swap(value, axis, bit)
            bit *= 2
    return value


def group_order(axis):
    size = lax.axis_size(axis)
    places = jnp.arange(size, dtype=jnp.int32)
    return places ^ lax.axis_index(axis) if size == 4 else places


def group_gather(own_block, axis):
    if lax.axis_size(axis) != 4:
        return lax.all_gather(own_block, axis, axis=0, tiled=True)
    across = swap(own_block, axis, 2)
    beside = swap(own_block, axis, 1)
    return jnp.concatenate([own_block, beside, across, swap(across, axis, 1)], axis=0)


def group_scatter(partial_low, axis):
    if lax.axis_size(axis) != 4:
        return lax.psum_scatter(partial_low, axis, scatter_dimension=0, tiled=True).astype(
            jnp.float32
        )
    own, beside, across, far = jnp.split(partial_low, 4, axis=0)
    far = swap(far, axis, 1)
    beside = swap(beside, axis, 1)
    across = swap(add_low(across, far), axis, 2)
    return own.astype(jnp.float32) + beside.astype(jnp.float32) + across.astype(jnp.float32)


def owner_scatter(product_low):
    if lax.axis_size("ctx") != 4 or lax.axis_size("shard") != 2:
        return lax.psum_scatter(
            product_low, ("shard", "ctx"), scatter_dimension=0, tiled=True
        ).astype(jnp.float32)
    place = lax.axis_index("ctx")
    core, along = place % 2, place // 2
    plane = lax.axis_index("shard")
    rows, width = product_low.shape
    blocks = product_low.reshape(2, 2, 2, rows // 8, width)

    def pick(value, index, axis):
        return lax.dynamic_index_in_dim(value, index, axis, keepdims=False)

    blocks = add_low(pick(blocks, core, 2), swap(pick(blocks, 1 - core, 2), "ctx", 1))
    former, latter = blocks[..., : width // 2], blocks[..., width // 2 :]
    former_in = swap(pick(former, 1 - along, 1), "ctx", 2)
    latter_in = swap(pick(latter, 1 - plane, 0), "shard", 1)
    former = add_low(pick(former, along, 1), former_in)
    latter = add_low(pick(latter, plane, 0), latter_in)
    former_in = swap(pick(former, 1 - plane, 0), "shard", 1)
    latter_in = swap(pick(latter, 1 - along, 0), "ctx", 2)
    return jnp.concatenate(
        [
            pick(former, plane, 0).astype(jnp.float32) + former_in.astype(jnp.float32),
            pick(latter, along, 0).astype(jnp.float32) + latter_in.astype(jnp.float32),
        ],
        axis=1,
    )


def row_labels(slots, group_size):
    tree_rows = group_size * lax.axis_size("ctx")
    chunk = group_size // lax.axis_size("tp")
    within = (group_order("tp")[:, None] * chunk + jnp.arange(chunk, dtype=jnp.int32)).reshape(-1)
    keys = (group_order("ctx")[:, None] * group_size + within[None, :]).reshape(-1)
    onehot = (keys[:, None] // SEG == jnp.arange(tree_rows // SEG, dtype=jnp.int32)[None, :])
    segment = jnp.sum(jnp.where(onehot, slots[None, :], 0), axis=1)
    offset = keys % SEG
    if lax.axis_size("ctx") != 4:
        first = lax.axis_index("ctx") * group_size
    else:
        first = 0
    return (
        lax.dynamic_slice_in_dim(segment, first, group_size),
        lax.dynamic_slice_in_dim(offset, first, group_size),
        segment,
        offset,
    )


LOG2_SCALE = math.sqrt(HDIM) * math.log2(math.e)
LANES = 128
KEY_TILE = 256


def half_kept(value, unit, axis):
    place = lax.broadcasted_iota(jnp.int32, value.shape, axis)
    inside = (place >= HDIM) if unit % 2 else (place < HDIM)
    return jnp.where(inside, value, jnp.zeros_like(value))


def seen_tile(hot_ref, side_ref):
    hot = hot_ref[...]
    strict = jnp.dot(hot, side_ref[0], preferred_element_type=jnp.float32)
    same = jnp.dot(hot, side_ref[1], preferred_element_type=jnp.float32)
    before = jnp.dot(hot, side_ref[2], preferred_element_type=jnp.float32)
    return (strict + same * before).astype(jnp.bfloat16)


def pair_of(unit):
    return slice(unit // 2 * LANES, unit // 2 * LANES + LANES)


def attend_body(query_ref, tree_ref, hot_ref, side_ref, out_ref, scale_ref, turned_ref, sum_ref):
    heads = query_ref.shape[1] // HDIM
    step = pl.program_id(0)

    @pl.when(step == 0)
    def prepare():
        turned = query_ref[...].astype(jnp.float32).T.astype(jnp.bfloat16)
        blank = jnp.zeros((HDIM, turned.shape[1]), jnp.bfloat16)
        for head in range(heads):
            own = turned[head * HDIM : (head + 1) * HDIM]
            halves = [blank, own] if head % 2 else [own, blank]
            turned_ref[head] = jnp.concatenate(halves, axis=0)
        sum_ref[...] = jnp.zeros_like(sum_ref)

    tree = tree_ref[...]
    values_turned = tree[:, heads * HDIM :].astype(jnp.float32).T.astype(jnp.bfloat16)
    seen = seen_tile(hot_ref, side_ref)
    ones = jnp.ones((sum_ref.shape[1] - HDIM, tree.shape[0]), jnp.bfloat16)
    for head in range(heads):
        scores = jnp.dot(tree[:, pair_of(head)], turned_ref[head], preferred_element_type=jnp.float32)
        lifted = jnp.exp2(scores * LOG2_SCALE).astype(jnp.bfloat16) * seen
        own = jnp.concatenate([values_turned[head * HDIM : (head + 1) * HDIM], ones], axis=0)
        sum_ref[head] += jnp.dot(own, lifted, preferred_element_type=jnp.float32)

    @pl.when(step == pl.num_programs(0) - 1)
    def finish():
        parts = []
        for head in range(heads):
            inverse = 1.0 / sum_ref[head, HDIM : HDIM + 1]
            scale_ref[head : head + 1] = inverse
            parts.append(sum_ref[head, :HDIM] * inverse)
        out_ref[...] = jnp.concatenate(parts, axis=0).T.astype(jnp.bfloat16)


def attend(query, tree, hot, side):
    rows, features = query.shape
    keys, width = tree.shape
    heads = features // HDIM
    whole = lambda step: (0, 0)
    return pl.pallas_call(
        attend_body,
        grid=(keys // KEY_TILE,),
        in_specs=[
            pl.BlockSpec((rows, features), whole),
            pl.BlockSpec((KEY_TILE, width), lambda step: (step, 0)),
            pl.BlockSpec((KEY_TILE, LANES), lambda step: (step, 0)),
            pl.BlockSpec((3, LANES, rows), lambda step: (0, 0, 0)),
        ],
        out_specs=[
            pl.BlockSpec((rows, features), whole),
            pl.BlockSpec((8, rows), whole),
        ],
        out_shape=[
            jax.ShapeDtypeStruct((rows, features), jnp.bfloat16),
            jax.ShapeDtypeStruct((8, rows), jnp.float32),
        ],
        scratch_shapes=[
            pltpu.VMEM((heads, LANES, rows), jnp.bfloat16),
            pltpu.VMEM((heads, HDIM + 16, rows), jnp.float32),
        ],
        compiler_params=pltpu.CompilerParams(vmem_limit_bytes=48 << 20),
        name="attend",
    )(query, tree, hot, side)


def attend_grad_body(
    both_ref, heads_ref, tree_ref, hot_ref, side_ref, scale_ref,
    query_out, tree_out, turned_ref, plain_ref, delta_ref, sum_ref,
):
    heads = heads_ref.shape[1] // HDIM
    units = 2 * heads
    step = pl.program_id(0)

    @pl.when(step == 0)
    def prepare():
        both = both_ref[...]
        turned = both.astype(jnp.float32).T
        outs = heads_ref[...].astype(jnp.float32).T
        blank = jnp.zeros((HDIM, turned.shape[1]), jnp.bfloat16)
        for unit in range(units):
            own = turned[unit * HDIM : (unit + 1) * HDIM].astype(jnp.bfloat16)
            halves = [blank, own] if unit % 2 else [own, blank]
            turned_ref[unit] = jnp.concatenate(halves, axis=0)
            plain_ref[unit] = half_kept(both[:, pair_of(unit)], unit, 1)
        for head in range(heads):
            rows = slice(head * HDIM, (head + 1) * HDIM)
            upstream = turned[(heads + head) * HDIM : (heads + head + 1) * HDIM]
            delta_ref[head : head + 1] = jnp.sum(outs[rows] * upstream, axis=0, keepdims=True)
        sum_ref[...] = jnp.zeros_like(sum_ref)

    tree = tree_ref[...]
    keys_turned = tree[:, : heads * HDIM].astype(jnp.float32).T.astype(jnp.bfloat16)
    seen = seen_tile(hot_ref, side_ref)
    weights, slopes = [], []
    for head in range(heads):
        scores = jnp.dot(tree[:, pair_of(head)], turned_ref[head], preferred_element_type=jnp.float32)
        weight = jnp.exp2(scores * LOG2_SCALE) * scale_ref[head : head + 1]
        pull = jnp.dot(
            tree[:, pair_of(heads + head)], turned_ref[heads + head], preferred_element_type=jnp.float32
        )
        slope = (weight * (pull - delta_ref[head : head + 1])).astype(jnp.bfloat16) * seen
        rows = slice(head * HDIM, (head + 1) * HDIM)
        sum_ref[rows] += jnp.dot(keys_turned[rows], slope, preferred_element_type=jnp.float32)
        weights.append(weight.astype(jnp.bfloat16) * seen)
        slopes.append(slope)
    terms = slopes + weights
    score_scale = math.sqrt(HDIM)
    for pair in range(heads):
        total = 0.0
        for unit in (2 * pair, 2 * pair + 1):
            part = jnp.dot(terms[unit], plain_ref[unit], preferred_element_type=jnp.float32)
            total = total + (part * score_scale if unit < heads else part)
        tree_out[:, pair * LANES : (pair + 1) * LANES] = total.astype(jnp.bfloat16)

    @pl.when(step == pl.num_programs(0) - 1)
    def finish():
        query_out[...] = sum_ref[...].T * score_scale


def attend_grad(query, upstream, outs, tree, hot, side, scale):
    rows, features = query.shape
    keys, width = tree.shape
    heads = features // HDIM
    whole = lambda step: (0, 0)
    return pl.pallas_call(
        attend_grad_body,
        grid=(keys // KEY_TILE,),
        in_specs=[
            pl.BlockSpec((rows, 2 * features), whole),
            pl.BlockSpec((rows, features), whole),
            pl.BlockSpec((KEY_TILE, width), lambda step: (step, 0)),
            pl.BlockSpec((KEY_TILE, LANES), lambda step: (step, 0)),
            pl.BlockSpec((3, LANES, rows), lambda step: (0, 0, 0)),
            pl.BlockSpec((8, rows), whole),
        ],
        out_specs=[
            pl.BlockSpec((rows, features), whole),
            pl.BlockSpec((KEY_TILE, width), lambda step: (step, 0)),
        ],
        out_shape=[
            jax.ShapeDtypeStruct((rows, features), jnp.float32),
            jax.ShapeDtypeStruct((keys, width), jnp.bfloat16),
        ],
        scratch_shapes=[
            pltpu.VMEM((2 * heads, LANES, rows), jnp.bfloat16),
            pltpu.VMEM((2 * heads, rows, LANES), jnp.bfloat16),
            pltpu.VMEM((8, rows), jnp.float32),
            pltpu.VMEM((features, rows), jnp.float32),
        ],
        compiler_params=pltpu.CompilerParams(vmem_limit_bytes=48 << 20),
        name="attend_grad",
    )(jnp.concatenate([query, upstream], axis=1), outs, tree, hot, side, scale)


def seen_factors(reachable, seg_query, off_query, segment, offset):
    segs = reachable.shape[0]
    labels = jnp.arange(LANES, dtype=jnp.int32)
    key_mark = jnp.where(labels < HDIM, segment[:, None], offset[:, None] + HDIM)
    hot = (key_mark == labels[None, :]).astype(jnp.bfloat16)
    query_hot = (labels[:, None] == seg_query[None, :]).astype(jnp.float32)
    wide = jnp.zeros((LANES, LANES), jnp.float32).at[:segs, :segs].set(reachable.T - jnp.eye(segs, dtype=jnp.float32))
    strict = jnp.dot(wide, query_hot, preferred_element_type=jnp.float32)
    same = query_hot
    before = ((labels[:, None] >= HDIM) & (labels[:, None] - HDIM <= off_query[None, :])).astype(jnp.float32)
    return hot, jnp.stack([strict, same, before]).astype(jnp.bfloat16)


def visibility(parents, slots, group_size):
    labels = jnp.arange(SEGS, dtype=jnp.int32)
    linked = (parents[:, None] == labels[None, :]).astype(jnp.float32)
    reachable = jnp.maximum(linked, jnp.eye(SEGS, dtype=jnp.float32))
    for doubling in range(SEGS.bit_length()):
        reachable = jnp.minimum(jnp.dot(reachable, reachable, precision=HIGHEST), 1.0)
    return seen_factors(reachable, *row_labels(slots, group_size))


def forward_attention(gathered, vectors, tokens_own, parents, slots):
    w_query, w_key, w_value, w_attn_out = gathered[:4]
    alpha_attn, alpha_mlp, scale_qk, scale_up, scale_gate = vectors
    hidden_group = group_gather(tokens_own, "tp")
    visible = visibility(parents, slots, hidden_group.shape[0])
    query_raw = jnp.dot(hidden_group, w_query, preferred_element_type=jnp.float32)
    key_raw = jnp.dot(hidden_group, w_key, preferred_element_type=jnp.float32)
    value_low = jnp.dot(hidden_group, w_value, preferred_element_type=jnp.float32).astype(
        jnp.bfloat16
    )
    query_unit, key_unit = query_key(query_raw, key_raw, scale_qk)
    queries = query_unit.astype(jnp.bfloat16)
    keys_own = key_unit.astype(jnp.bfloat16)
    keys_values = group_gather(jnp.concatenate([keys_own, value_low], axis=1), "ctx")
    heads_low, scale = attend(queries, keys_values, *visible)
    branch_one = group_scatter(contract_cols(heads_low, w_attn_out).astype(jnp.bfloat16), "tp")
    kept = (
        hidden_group,
        visible,
        query_raw,
        key_raw,
        queries,
        keys_values,
        scale,
        heads_low,
    )
    return branch_one, kept


def feed_forward(gathered, vectors, tokens_own, branch_one, cotangent_own):
    w_up, w_gate, w_down = gathered[4:]
    alpha_attn, alpha_mlp, scale_qk, scale_up, scale_gate = vectors
    tokens_wide = tokens_own.astype(jnp.float32)
    hidden_one = mix_rows(tokens_wide, branch_one, alpha_attn)
    hidden_one_group = group_gather(hidden_one.astype(jnp.bfloat16), "tp")
    up_raw = jnp.dot(hidden_one_group, w_up, preferred_element_type=jnp.float32)
    gate_raw = jnp.dot(hidden_one_group, w_gate, preferred_element_type=jnp.float32)
    mixed_low = middle(up_raw, gate_raw, scale_up, scale_gate).astype(jnp.bfloat16)
    branch_two = group_scatter(contract_cols(mixed_low, w_down).astype(jnp.bfloat16), "tp")
    output_wide, pull_out = jax.vjp(mix_rows, hidden_one, branch_two, alpha_mlp)
    upstream = cotangent_own.astype(jnp.float32)
    hidden_one_direct, branch_two_grad, grad_alpha_mlp = pull_out(upstream)
    branch_two_group = group_gather(branch_two_grad.astype(jnp.bfloat16), "tp")
    mixed_grad = (
        jnp.dot(branch_two_group, w_down, preferred_element_type=jnp.float32)
        .astype(jnp.bfloat16)
        .astype(jnp.float32)
    )
    middle_value, pull_mid = jax.vjp(middle, up_raw, gate_raw, scale_up, scale_gate)
    up_grad, gate_grad, grad_scale_up, grad_scale_gate = pull_mid(mixed_grad)
    up_low = up_grad.astype(jnp.bfloat16)
    gate_low = gate_grad.astype(jnp.bfloat16)
    hidden_one_grad = hidden_one_direct + group_scatter(
        (contract_cols(up_low, w_up) + contract_cols(gate_low, w_gate)).astype(jnp.bfloat16), "tp"
    )
    hidden_again, pull_in = jax.vjp(mix_rows, tokens_wide, branch_one, alpha_attn)
    tokens_direct, branch_one_grad, grad_alpha_attn = pull_in(hidden_one_grad)
    factors = (mixed_low, branch_two_group, hidden_one_group, up_low, gate_low)
    sums = (grad_alpha_attn, grad_alpha_mlp, grad_scale_up, grad_scale_gate)
    return output_wide.astype(jnp.bfloat16), tokens_direct, branch_one_grad, factors, sums


def backward_attention(gathered, vectors, kept, branch_one_grad, tokens_direct):
    w_query, w_key, w_value, w_attn_out = gathered[:4]
    scale_qk = vectors[2]
    (
        hidden_group,
        visible,
        query_raw,
        key_raw,
        queries,
        keys_values,
        scale,
        heads_low,
    ) = kept
    branch_one_group = group_gather(branch_one_grad.astype(jnp.bfloat16), "tp")
    heads_grad = jnp.dot(
        branch_one_group, w_attn_out, preferred_element_type=jnp.float32
    ).astype(jnp.bfloat16)
    query_grads, tree_grads = attend_grad(
        queries, heads_grad, heads_low, keys_values, *visible, scale
    )
    key_own_grad, value_own_grad = jnp.split(group_scatter(tree_grads, "ctx"), 2, axis=1)
    unit_again, pull_qk = jax.vjp(query_key, query_raw, key_raw, scale_qk)
    query_raw_grad, key_raw_grad, grad_scale_qk = pull_qk((query_grads, key_own_grad))
    query_low = query_raw_grad.astype(jnp.bfloat16)
    key_low = key_raw_grad.astype(jnp.bfloat16)
    value_grad_low = value_own_grad.astype(jnp.bfloat16)
    input_part = (
        contract_cols(query_low, w_query)
        + contract_cols(key_low, w_key)
        + contract_cols(value_grad_low, w_value)
    )
    grad_tokens = tokens_direct + group_scatter(input_part.astype(jnp.bfloat16), "tp")
    factors = (hidden_group, query_low, key_low, value_grad_low, heads_low, branch_one_group)
    return grad_tokens, factors, grad_scale_qk


def per_device(
    tokens,
    parents,
    slot_segment,
    w_query,
    w_key,
    w_value,
    w_attn_out,
    w_up,
    w_gate,
    w_down,
    alpha_attn,
    alpha_mlp,
    scale_qk,
    scale_up,
    scale_gate,
    cotangent,
):
    local_heads = w_query.shape[1]
    local_hidden = w_up.shape[1]
    vectors = (alpha_attn, alpha_mlp, scale_qk, scale_up, scale_gate)
    spread = ("shard", "ctx")

    def spread_gather(own_block):
        return lax.all_gather(own_block, spread, axis=0, tiled=True)

    packed = spread_gather(jnp.concatenate([w_query, w_key, w_value, w_attn_out.T], axis=1))
    gathered = (
        packed[:, :local_heads],
        packed[:, local_heads : 2 * local_heads],
        packed[:, 2 * local_heads : 3 * local_heads],
        packed[:, 3 * local_heads :],
        spread_gather(w_up),
        spread_gather(w_gate),
        spread_gather(w_down.T),
    )
    micros = range(tokens.shape[0])
    front = [
        forward_attention(gathered, vectors, tokens[m, 0], parents[m, 0], slot_segment[m, 0])
        for m in micros
    ]
    mid = [
        feed_forward(gathered, vectors, tokens[m, 0], front[m][0], cotangent[m, 0]) for m in micros
    ]
    back = [
        backward_attention(gathered, vectors, front[m][1], mid[m][2], mid[m][1]) for m in micros
    ]

    def stack(pick):
        return jnp.concatenate([pick(m) for m in micros], axis=0)

    mixed_all, top_all, hidden_all, up_all, gate_all = (
        stack(lambda m: mid[m][3][place]) for place in range(5)
    )
    tokens_all, query_all, key_all, value_all, heads_all, branch_all = (
        stack(lambda m: back[m][1][place]) for place in range(6)
    )

    def to_owner(former, latter):
        return owner_scatter(contract_rows(former, latter).astype(jnp.bfloat16))

    grad_d = to_owner(top_all, mixed_all).T
    grad_u = to_owner(hidden_all, up_all)
    grad_g = to_owner(hidden_all, gate_all)
    attention_product = jnp.concatenate(
        [
            contract_rows(tokens_all, query_all),
            contract_rows(tokens_all, key_all),
            contract_rows(tokens_all, value_all),
            contract_rows(branch_all, heads_all),
        ],
        axis=1,
    )
    grad_attention = owner_scatter(attention_product.astype(jnp.bfloat16))
    grad_q, grad_k, grad_v, grad_o = jnp.split(grad_attention, 4, axis=1)

    sum_attn, sum_mlp, sum_up, sum_gate = (
        sum(mid[m][4][place] for m in micros) for place in range(4)
    )
    sum_qk = butterfly(sum(back[m][2] for m in micros), spread)
    width = sum_attn.shape[0]
    sums = butterfly(jnp.concatenate([sum_attn, sum_mlp, sum_up, sum_gate]), spread)
    alphas = butterfly(sums[: 2 * width], ("tp",))
    return (
        jnp.stack([mid[m][0] for m in micros])[:, None],
        jnp.stack([back[m][0] for m in micros])[:, None],
        grad_q,
        grad_k,
        grad_v,
        grad_o.T,
        grad_u,
        grad_g,
        grad_d,
        alphas[:width],
        alphas[width:],
        sum_qk,
        sums[2 * width : 2 * width + local_hidden],
        sums[2 * width + local_hidden :],
    )


def solution(mesh):
    return jax.shard_map(
        per_device,
        mesh=mesh,
        in_specs=(
            P(None, "shard", ("ctx", "tp"), None),
            P(None, "shard", None),
            P(None, "shard", None),
            P(("shard", "ctx"), "tp"),
            P(("shard", "ctx"), "tp"),
            P(("shard", "ctx"), "tp"),
            P("tp", ("shard", "ctx")),
            P(("shard", "ctx"), "tp"),
            P(("shard", "ctx"), "tp"),
            P("tp", ("shard", "ctx")),
            P(),
            P(),
            P("tp"),
            P("tp"),
            P("tp"),
            P(None, "shard", ("ctx", "tp"), None),
        ),
        out_specs=(
            P(None, "shard", ("ctx", "tp"), None),
            P(None, "shard", ("ctx", "tp"), None),
            P(("shard", "ctx"), "tp"),
            P(("shard", "ctx"), "tp"),
            P(("shard", "ctx"), "tp"),
            P("tp", ("shard", "ctx")),
            P(("shard", "ctx"), "tp"),
            P(("shard", "ctx"), "tp"),
            P("tp", ("shard", "ctx")),
            P(),
            P(),
            P("tp"),
            P("tp"),
            P("tp"),
        ),
        check_vma=False,
    )
```

```python
import math

import jax
import jax.numpy as jnp
from jax import lax
from jax.experimental import pallas as pl
from jax.experimental.pallas import tpu as pltpu
from jax.sharding import PartitionSpec as P

D = 1280
HDIM = 64
SEG = 64
SEGS = 40
TREE_TOK = 2560


EPSILON = 1e-06
HIGHEST = lax.Precision.HIGHEST
SPREAD = ("shard", "ctx")


def unit_rows(values):
    return values * lax.rsqrt(jnp.sum(values * values, axis=-1, keepdims=True) + EPSILON)


def unit_heads(values):
    shaped = values.reshape(values.shape[0], values.shape[1] // HDIM, HDIM)
    return unit_rows(shaped).reshape(values.shape)


def contract_rows(former, latter):
    return lax.dot_general(
        former, latter, (((0,), (0,)), ((), ())), preferred_element_type=jnp.float32
    )


def contract_cols(former, latter):
    return lax.dot_general(
        former, latter, (((1,), (1,)), ((), ())), preferred_element_type=jnp.float32
    )


def mix_rows(residual, branch, mixing):
    return unit_rows(residual + mixing * (unit_rows(branch) - residual))


def query_key(query_raw, key_raw, gain_qk):
    return (unit_heads(query_raw) * gain_qk, unit_heads(key_raw) * gain_qk)


def middle(up_raw, gate_raw, scale_up, scale_gate):
    return up_raw * scale_up * jax.nn.silu(gate_raw * (scale_gate * math.sqrt(D)))


def swap(value, axis, bit):
    size = lax.axis_size(axis)
    return lax.ppermute(value, axis, [(place, place ^ bit) for place in range(size)])


def add_low(former, latter):
    return (former.astype(jnp.float32) + latter.astype(jnp.float32)).astype(jnp.bfloat16)


def butterfly(value, axes):
    for axis in axes:
        bit = 1
        while bit < lax.axis_size(axis):
            value = value + swap(value, axis, bit)
            bit *= 2
    return value


def group_order(axis):
    size = lax.axis_size(axis)
    places = jnp.arange(size, dtype=jnp.int32)
    return places ^ lax.axis_index(axis) if size == 4 else places


def group_gather(own_block, axis):
    if lax.axis_size(axis) != 4:
        return lax.all_gather(own_block, axis, axis=0, tiled=True)
    across = swap(own_block, axis, 2)
    beside = swap(own_block, axis, 1)
    return jnp.concatenate([own_block, beside, across, swap(across, axis, 1)], axis=0)


def group_scatter(partial_low, axis):
    if lax.axis_size(axis) != 4:
        return lax.psum_scatter(partial_low, axis, scatter_dimension=0, tiled=True).astype(
            jnp.float32
        )
    own, beside, across, far = jnp.split(partial_low, 4, axis=0)
    far = swap(far, axis, 1)
    beside = swap(beside, axis, 1)
    across = swap(add_low(across, far), axis, 2)
    return own.astype(jnp.float32) + beside.astype(jnp.float32) + across.astype(jnp.float32)


def in_plane():
    return (lax.axis_size("shard"), lax.axis_size("ctx"), lax.axis_size("tp")) == (2, 4, 4)


def hop(value, bits):
    return lax.ppermute(value, SPREAD, [(place, place ^ bits) for place in range(8)])


def hidden_gather(own_block):
    if not in_plane():
        return group_gather(own_block, "tp")
    return jnp.concatenate([own_block] + [hop(own_block, bits) for bits in (2, 4, 6)], axis=0)


def hidden_scatter(partial_low):
    if not in_plane():
        return group_scatter(partial_low, "tp")
    own, along, aside, across = jnp.split(partial_low, 4, axis=0)
    total = own.astype(jnp.float32)
    for value, bits in ((along, 2), (aside, 4), (across, 6)):
        total = total + hop(value, bits).astype(jnp.float32)
    return total


def hidden_weights(w_up, w_gate, w_down):
    if not in_plane():
        return tuple(
            lax.all_gather(matrix, SPREAD, axis=1, tiled=True)
            for matrix in (w_up.T, w_gate.T, w_down)
        )
    rows, hidden = w_up.shape
    part = hidden // 8
    packed = jnp.stack(
        [
            w_up.reshape(rows, 8, part).transpose(1, 2, 0),
            w_gate.reshape(rows, 8, part).transpose(1, 2, 0),
            w_down.reshape(8, part, rows),
        ],
        axis=1,
    )
    packed = lax.all_to_all(packed, SPREAD, 0, 0)
    matrices = packed.transpose(1, 2, 0, 3).reshape(3, part, 8 * rows)
    out = []
    for place in range(3):
        own_core = group_gather(matrices[place], "tp")
        out.append(jnp.concatenate([own_core, swap(own_core, "ctx", 1)], axis=0))
    return tuple(out)


def hidden_scales(*scales):
    if not in_plane():
        return scales
    part = scales[0].shape[0] // 8
    first = lax.axis_index(SPREAD) * part
    own = jnp.stack([lax.dynamic_slice_in_dim(scale, first, part) for scale in scales])
    line = group_gather(own[None], "tp")
    both = jnp.concatenate([line, swap(line, "ctx", 1)], axis=0)
    return tuple(both[:, place].reshape(-1) for place in range(len(scales)))


def hidden_weight_grads(products):
    if not in_plane():
        return [
            lax.psum_scatter(product, SPREAD, scatter_dimension=1, tiled=True).astype(jnp.float32)
            for product in products
        ]
    sums = []
    for product in products:
        half = product.shape[0] // 2
        line = add_low(product[:half], swap(product[half:], "ctx", 1))
        sums.append(group_scatter(line, "tp").astype(jnp.bfloat16))
    part, width = sums[0].shape
    packed = jnp.stack([total.reshape(part, 8, width // 8).transpose(1, 0, 2) for total in sums], 1)
    packed = lax.all_to_all(packed, SPREAD, 0, 0).astype(jnp.float32)
    return [packed[:, place].reshape(8 * part, width // 8) for place in range(3)]


def hidden_scale_grads(sums):
    if not in_plane():
        return butterfly(sums, SPREAD)
    count, hidden = sums.shape
    parts = sums.reshape(count, 2, 4, hidden // 8)
    line = hidden_line_sum(parts[:, 0] + swap(parts[:, 1], "ctx", 1))
    blank = jnp.zeros((count, 8, hidden // 8), jnp.float32)
    place = lax.axis_index(SPREAD)
    spread_out = lax.dynamic_update_slice_in_dim(blank, line[:, None], place, 1)
    return butterfly(spread_out, SPREAD).reshape(count, hidden)


def hidden_line_sum(parts):
    own, beside, across, far = (parts[:, place] for place in range(4))
    across = across + swap(far, "tp", 1)
    return own + swap(beside, "tp", 1) + swap(across, "tp", 2)


def owner_scatter(product_low):
    if lax.axis_size("ctx") != 4 or lax.axis_size("shard") != 2:
        return lax.psum_scatter(
            product_low, ("shard", "ctx"), scatter_dimension=0, tiled=True
        ).astype(jnp.float32)
    place = lax.axis_index("ctx")
    core, along = place % 2, place // 2
    plane = lax.axis_index("shard")
    rows, width = product_low.shape
    blocks = product_low.reshape(2, 2, 2, rows // 8, width)

    def pick(value, index, axis):
        return lax.dynamic_index_in_dim(value, index, axis, keepdims=False)

    blocks = add_low(pick(blocks, core, 2), swap(pick(blocks, 1 - core, 2), "ctx", 1))
    former, latter = blocks[..., : width // 2], blocks[..., width // 2 :]
    former_in = swap(pick(former, 1 - along, 1), "ctx", 2)
    latter_in = swap(pick(latter, 1 - plane, 0), "shard", 1)
    former = add_low(pick(former, along, 1), former_in)
    latter = add_low(pick(latter, plane, 0), latter_in)
    former_in = swap(pick(former, 1 - plane, 0), "shard", 1)
    latter_in = swap(pick(latter, 1 - along, 0), "ctx", 2)
    return jnp.concatenate(
        [
            pick(former, plane, 0).astype(jnp.float32) + former_in.astype(jnp.float32),
            pick(latter, along, 0).astype(jnp.float32) + latter_in.astype(jnp.float32),
        ],
        axis=1,
    )


def row_labels(slots, group_size):
    tree_rows = group_size * lax.axis_size("ctx")
    chunk = group_size // lax.axis_size("tp")
    within = (group_order("tp")[:, None] * chunk + jnp.arange(chunk, dtype=jnp.int32)).reshape(-1)
    keys = (group_order("ctx")[:, None] * group_size + within[None, :]).reshape(-1)
    onehot = (keys[:, None] // SEG == jnp.arange(tree_rows // SEG, dtype=jnp.int32)[None, :])
    segment = jnp.sum(jnp.where(onehot, slots[None, :], 0), axis=1)
    offset = keys % SEG
    if lax.axis_size("ctx") != 4:
        first = lax.axis_index("ctx") * group_size
    else:
        first = 0
    return (
        lax.dynamic_slice_in_dim(segment, first, group_size),
        lax.dynamic_slice_in_dim(offset, first, group_size),
        segment,
        offset,
    )


LOG2_SCALE = math.sqrt(HDIM) * math.log2(math.e)
LANES = 128
KEY_TILE = 256


def half_kept(value, unit, axis):
    place = lax.broadcasted_iota(jnp.int32, value.shape, axis)
    inside = (place >= HDIM) if unit % 2 else (place < HDIM)
    return jnp.where(inside, value, jnp.zeros_like(value))


def seen_tile(hot_ref, side_ref):
    hot = hot_ref[...]
    strict = jnp.dot(hot, side_ref[0], preferred_element_type=jnp.float32)
    same = jnp.dot(hot, side_ref[1], preferred_element_type=jnp.float32)
    before = jnp.dot(hot, side_ref[2], preferred_element_type=jnp.float32)
    return (strict + same * before).astype(jnp.bfloat16)


def pair_of(unit):
    return slice(unit // 2 * LANES, unit // 2 * LANES + LANES)


def attend_body(query_ref, tree_ref, hot_ref, side_ref, out_ref, scale_ref, turned_ref, sum_ref):
    heads = query_ref.shape[1] // HDIM
    step = pl.program_id(0)

    @pl.when(step == 0)
    def prepare():
        turned = query_ref[...].astype(jnp.float32).T.astype(jnp.bfloat16)
        blank = jnp.zeros((HDIM, turned.shape[1]), jnp.bfloat16)
        for head in range(heads):
            own = turned[head * HDIM : (head + 1) * HDIM]
            halves = [blank, own] if head % 2 else [own, blank]
            turned_ref[head] = jnp.concatenate(halves, axis=0)
        sum_ref[...] = jnp.zeros_like(sum_ref)

    tree = tree_ref[...]
    values_turned = tree[:, heads * HDIM :].astype(jnp.float32).T.astype(jnp.bfloat16)
    seen = seen_tile(hot_ref, side_ref)
    ones = jnp.ones((sum_ref.shape[1] - HDIM, tree.shape[0]), jnp.bfloat16)
    for head in range(heads):
        scores = jnp.dot(tree[:, pair_of(head)], turned_ref[head], preferred_element_type=jnp.float32)
        lifted = jnp.exp2(scores * LOG2_SCALE).astype(jnp.bfloat16) * seen
        own = jnp.concatenate([values_turned[head * HDIM : (head + 1) * HDIM], ones], axis=0)
        sum_ref[head] += jnp.dot(own, lifted, preferred_element_type=jnp.float32)

    @pl.when(step == pl.num_programs(0) - 1)
    def finish():
        parts = []
        for head in range(heads):
            inverse = 1.0 / sum_ref[head, HDIM : HDIM + 1]
            scale_ref[head : head + 1] = inverse
            parts.append(sum_ref[head, :HDIM] * inverse)
        out_ref[...] = jnp.concatenate(parts, axis=0).T.astype(jnp.bfloat16)


def attend(query, tree, hot, side):
    rows, features = query.shape
    keys, width = tree.shape
    heads = features // HDIM
    whole = lambda step: (0, 0)
    return pl.pallas_call(
        attend_body,
        grid=(keys // KEY_TILE,),
        in_specs=[
            pl.BlockSpec((rows, features), whole),
            pl.BlockSpec((KEY_TILE, width), lambda step: (step, 0)),
            pl.BlockSpec((KEY_TILE, LANES), lambda step: (step, 0)),
            pl.BlockSpec((3, LANES, rows), lambda step: (0, 0, 0)),
        ],
        out_specs=[
            pl.BlockSpec((rows, features), whole),
            pl.BlockSpec((8, rows), whole),
        ],
        out_shape=[
            jax.ShapeDtypeStruct((rows, features), jnp.bfloat16),
            jax.ShapeDtypeStruct((8, rows), jnp.float32),
        ],
        scratch_shapes=[
            pltpu.VMEM((heads, LANES, rows), jnp.bfloat16),
            pltpu.VMEM((heads, HDIM + 16, rows), jnp.float32),
        ],
        compiler_params=pltpu.CompilerParams(vmem_limit_bytes=48 << 20),
        name="attend",
    )(query, tree, hot, side)


def attend_grad_body(
    both_ref, heads_ref, tree_ref, hot_ref, side_ref, scale_ref,
    query_out, tree_out, turned_ref, plain_ref, delta_ref, sum_ref,
):
    heads = heads_ref.shape[1] // HDIM
    units = 2 * heads
    step = pl.program_id(0)

    @pl.when(step == 0)
    def prepare():
        both = both_ref[...]
        turned = both.astype(jnp.float32).T
        outs = heads_ref[...].astype(jnp.float32).T
        blank = jnp.zeros((HDIM, turned.shape[1]), jnp.bfloat16)
        for unit in range(units):
            own = turned[unit * HDIM : (unit + 1) * HDIM].astype(jnp.bfloat16)
            halves = [blank, own] if unit % 2 else [own, blank]
            turned_ref[unit] = jnp.concatenate(halves, axis=0)
            plain_ref[unit] = half_kept(both[:, pair_of(unit)], unit, 1)
        for head in range(heads):
            rows = slice(head * HDIM, (head + 1) * HDIM)
            upstream = turned[(heads + head) * HDIM : (heads + head + 1) * HDIM]
            delta_ref[head : head + 1] = jnp.sum(outs[rows] * upstream, axis=0, keepdims=True)
        sum_ref[...] = jnp.zeros_like(sum_ref)

    tree = tree_ref[...]
    keys_turned = tree[:, : heads * HDIM].astype(jnp.float32).T.astype(jnp.bfloat16)
    seen = seen_tile(hot_ref, side_ref)
    weights, slopes = [], []
    for head in range(heads):
        scores = jnp.dot(tree[:, pair_of(head)], turned_ref[head], preferred_element_type=jnp.float32)
        weight = jnp.exp2(scores * LOG2_SCALE) * scale_ref[head : head + 1]
        pull = jnp.dot(
            tree[:, pair_of(heads + head)], turned_ref[heads + head], preferred_element_type=jnp.float32
        )
        slope = (weight * (pull - delta_ref[head : head + 1])).astype(jnp.bfloat16) * seen
        rows = slice(head * HDIM, (head + 1) * HDIM)
        sum_ref[rows] += jnp.dot(keys_turned[rows], slope, preferred_element_type=jnp.float32)
        weights.append(weight.astype(jnp.bfloat16) * seen)
        slopes.append(slope)
    terms = slopes + weights
    score_scale = math.sqrt(HDIM)
    for pair in range(heads):
        total = 0.0
        for unit in (2 * pair, 2 * pair + 1):
            part = jnp.dot(terms[unit], plain_ref[unit], preferred_element_type=jnp.float32)
            total = total + (part * score_scale if unit < heads else part)
        tree_out[:, pair * LANES : (pair + 1) * LANES] = total.astype(jnp.bfloat16)

    @pl.when(step == pl.num_programs(0) - 1)
    def finish():
        query_out[...] = sum_ref[...].T * score_scale


def attend_grad(query, upstream, outs, tree, hot, side, scale):
    rows, features = query.shape
    keys, width = tree.shape
    heads = features // HDIM
    whole = lambda step: (0, 0)
    return pl.pallas_call(
        attend_grad_body,
        grid=(keys // KEY_TILE,),
        in_specs=[
            pl.BlockSpec((rows, 2 * features), whole),
            pl.BlockSpec((rows, features), whole),
            pl.BlockSpec((KEY_TILE, width), lambda step: (step, 0)),
            pl.BlockSpec((KEY_TILE, LANES), lambda step: (step, 0)),
            pl.BlockSpec((3, LANES, rows), lambda step: (0, 0, 0)),
            pl.BlockSpec((8, rows), whole),
        ],
        out_specs=[
            pl.BlockSpec((rows, features), whole),
            pl.BlockSpec((KEY_TILE, width), lambda step: (step, 0)),
        ],
        out_shape=[
            jax.ShapeDtypeStruct((rows, features), jnp.float32),
            jax.ShapeDtypeStruct((keys, width), jnp.bfloat16),
        ],
        scratch_shapes=[
            pltpu.VMEM((2 * heads, LANES, rows), jnp.bfloat16),
            pltpu.VMEM((2 * heads, rows, LANES), jnp.bfloat16),
            pltpu.VMEM((8, rows), jnp.float32),
            pltpu.VMEM((features, rows), jnp.float32),
        ],
        compiler_params=pltpu.CompilerParams(vmem_limit_bytes=48 << 20),
        name="attend_grad",
    )(jnp.concatenate([query, upstream], axis=1), outs, tree, hot, side, scale)


def seen_factors(reachable, seg_query, off_query, segment, offset):
    segs = reachable.shape[0]
    labels = jnp.arange(LANES, dtype=jnp.int32)
    key_mark = jnp.where(labels < HDIM, segment[:, None], offset[:, None] + HDIM)
    hot = (key_mark == labels[None, :]).astype(jnp.bfloat16)
    query_hot = (labels[:, None] == seg_query[None, :]).astype(jnp.float32)
    wide = jnp.zeros((LANES, LANES), jnp.float32).at[:segs, :segs].set(reachable.T - jnp.eye(segs, dtype=jnp.float32))
    strict = jnp.dot(wide, query_hot, preferred_element_type=jnp.float32)
    same = query_hot
    before = ((labels[:, None] >= HDIM) & (labels[:, None] - HDIM <= off_query[None, :])).astype(jnp.float32)
    return hot, jnp.stack([strict, same, before]).astype(jnp.bfloat16)


def visibility(parents, slots, group_size):
    labels = jnp.arange(SEGS, dtype=jnp.int32)
    linked = (parents[:, None] == labels[None, :]).astype(jnp.float32)
    reachable = jnp.maximum(linked, jnp.eye(SEGS, dtype=jnp.float32))
    for doubling in range(SEGS.bit_length()):
        reachable = jnp.minimum(jnp.dot(reachable, reachable, precision=HIGHEST), 1.0)
    return seen_factors(reachable, *row_labels(slots, group_size))


def forward_attention(gathered, vectors, tokens_own, parents, slots):
    w_query, w_key, w_value, w_attn_out = gathered[:4]
    alpha_attn, alpha_mlp, scale_qk, scale_up, scale_gate = vectors
    hidden_group = group_gather(tokens_own, "tp")
    visible = visibility(parents, slots, hidden_group.shape[0])
    query_raw = jnp.dot(hidden_group, w_query, preferred_element_type=jnp.float32)
    key_raw = jnp.dot(hidden_group, w_key, preferred_element_type=jnp.float32)
    value_low = jnp.dot(hidden_group, w_value, preferred_element_type=jnp.float32).astype(
        jnp.bfloat16
    )
    query_unit, key_unit = query_key(query_raw, key_raw, scale_qk)
    queries = query_unit.astype(jnp.bfloat16)
    keys_own = key_unit.astype(jnp.bfloat16)
    keys_values = group_gather(jnp.concatenate([keys_own, value_low], axis=1), "ctx")
    heads_low, scale = attend(queries, keys_values, *visible)
    branch_one = group_scatter(contract_cols(heads_low, w_attn_out).astype(jnp.bfloat16), "tp")
    kept = (
        hidden_group,
        visible,
        query_raw,
        key_raw,
        queries,
        keys_values,
        scale,
        heads_low,
    )
    return branch_one, kept


def feed_forward(gathered, vectors, tokens_own, branch_one, cotangent_own):
    w_up, w_gate, w_down = gathered[4:]
    alpha_attn, alpha_mlp, scale_qk, scale_up, scale_gate = vectors
    tokens_wide = tokens_own.astype(jnp.float32)
    hidden_one = mix_rows(tokens_wide, branch_one, alpha_attn)
    hidden_one_group = hidden_gather(hidden_one.astype(jnp.bfloat16))
    up_raw = contract_cols(hidden_one_group, w_up)
    gate_raw = contract_cols(hidden_one_group, w_gate)
    mixed_low = middle(up_raw, gate_raw, scale_up, scale_gate).astype(jnp.bfloat16)
    branch_two = hidden_scatter(
        jnp.dot(mixed_low, w_down, preferred_element_type=jnp.float32).astype(jnp.bfloat16)
    )
    output_wide, pull_out = jax.vjp(mix_rows, hidden_one, branch_two, alpha_mlp)
    upstream = cotangent_own.astype(jnp.float32)
    hidden_one_direct, branch_two_grad, grad_alpha_mlp = pull_out(upstream)
    branch_two_group = hidden_gather(branch_two_grad.astype(jnp.bfloat16))
    mixed_grad = contract_cols(branch_two_group, w_down).astype(jnp.bfloat16).astype(jnp.float32)
    middle_value, pull_mid = jax.vjp(middle, up_raw, gate_raw, scale_up, scale_gate)
    up_grad, gate_grad, grad_scale_up, grad_scale_gate = pull_mid(mixed_grad)
    up_low = up_grad.astype(jnp.bfloat16)
    gate_low = gate_grad.astype(jnp.bfloat16)
    hidden_one_grad = hidden_one_direct + hidden_scatter(
        (
            jnp.dot(up_low, w_up, preferred_element_type=jnp.float32)
            + jnp.dot(gate_low, w_gate, preferred_element_type=jnp.float32)
        ).astype(jnp.bfloat16)
    )
    hidden_again, pull_in = jax.vjp(mix_rows, tokens_wide, branch_one, alpha_attn)
    tokens_direct, branch_one_grad, grad_alpha_attn = pull_in(hidden_one_grad)
    factors = (mixed_low, branch_two_group, hidden_one_group, up_low, gate_low)
    sums = (grad_alpha_attn, grad_alpha_mlp, grad_scale_up, grad_scale_gate)
    return output_wide.astype(jnp.bfloat16), tokens_direct, branch_one_grad, factors, sums


def backward_attention(gathered, vectors, kept, branch_one_grad, tokens_direct):
    w_query, w_key, w_value, w_attn_out = gathered[:4]
    scale_qk = vectors[2]
    (
        hidden_group,
        visible,
        query_raw,
        key_raw,
        queries,
        keys_values,
        scale,
        heads_low,
    ) = kept
    branch_one_group = group_gather(branch_one_grad.astype(jnp.bfloat16), "tp")
    heads_grad = jnp.dot(
        branch_one_group, w_attn_out, preferred_element_type=jnp.float32
    ).astype(jnp.bfloat16)
    query_grads, tree_grads = attend_grad(
        queries, heads_grad, heads_low, keys_values, *visible, scale
    )
    key_own_grad, value_own_grad = jnp.split(group_scatter(tree_grads, "ctx"), 2, axis=1)
    unit_again, pull_qk = jax.vjp(query_key, query_raw, key_raw, scale_qk)
    query_raw_grad, key_raw_grad, grad_scale_qk = pull_qk((query_grads, key_own_grad))
    query_low = query_raw_grad.astype(jnp.bfloat16)
    key_low = key_raw_grad.astype(jnp.bfloat16)
    value_grad_low = value_own_grad.astype(jnp.bfloat16)
    input_part = (
        contract_cols(query_low, w_query)
        + contract_cols(key_low, w_key)
        + contract_cols(value_grad_low, w_value)
    )
    grad_tokens = tokens_direct + group_scatter(input_part.astype(jnp.bfloat16), "tp")
    factors = (hidden_group, query_low, key_low, value_grad_low, heads_low, branch_one_group)
    return grad_tokens, factors, grad_scale_qk


def per_device(
    tokens,
    parents,
    slot_segment,
    w_query,
    w_key,
    w_value,
    w_attn_out,
    w_up,
    w_gate,
    w_down,
    alpha_attn,
    alpha_mlp,
    scale_qk,
    scale_up,
    scale_gate,
    cotangent,
):
    local_heads = w_query.shape[1]
    vectors = (alpha_attn, alpha_mlp, scale_qk) + hidden_scales(scale_up, scale_gate)

    def spread_gather(own_block):
        return lax.all_gather(own_block, SPREAD, axis=0, tiled=True)

    packed = spread_gather(jnp.concatenate([w_query, w_key, w_value, w_attn_out.T], axis=1))
    gathered = (
        packed[:, :local_heads],
        packed[:, local_heads : 2 * local_heads],
        packed[:, 2 * local_heads : 3 * local_heads],
        packed[:, 3 * local_heads :],
    ) + hidden_weights(w_up, w_gate, w_down)
    micros = range(tokens.shape[0])
    front = [
        forward_attention(gathered, vectors, tokens[m, 0], parents[m, 0], slot_segment[m, 0])
        for m in micros
    ]
    mid = [
        feed_forward(gathered, vectors, tokens[m, 0], front[m][0], cotangent[m, 0]) for m in micros
    ]
    back = [
        backward_attention(gathered, vectors, front[m][1], mid[m][2], mid[m][1]) for m in micros
    ]

    def stack(pick):
        return jnp.concatenate([pick(m) for m in micros], axis=0)

    mixed_all, top_all, hidden_all, up_all, gate_all = (
        stack(lambda m: mid[m][3][place]) for place in range(5)
    )
    tokens_all, query_all, key_all, value_all, heads_all, branch_all = (
        stack(lambda m: back[m][1][place]) for place in range(6)
    )

    grad_u, grad_g, grad_d = hidden_weight_grads(
        [
            contract_rows(former, latter).astype(jnp.bfloat16)
            for former, latter in (
                (up_all, hidden_all),
                (gate_all, hidden_all),
                (mixed_all, top_all),
            )
        ]
    )
    attention_product = jnp.concatenate(
        [
            contract_rows(tokens_all, query_all),
            contract_rows(tokens_all, key_all),
            contract_rows(tokens_all, value_all),
            contract_rows(branch_all, heads_all),
        ],
        axis=1,
    )
    grad_attention = owner_scatter(attention_product.astype(jnp.bfloat16))
    grad_q, grad_k, grad_v, grad_o = jnp.split(grad_attention, 4, axis=1)

    sum_attn, sum_mlp, sum_up, sum_gate = (
        sum(mid[m][4][place] for m in micros) for place in range(4)
    )
    sum_qk = butterfly(sum(back[m][2] for m in micros), SPREAD)
    width = sum_attn.shape[0]
    alphas = butterfly(jnp.concatenate([sum_attn, sum_mlp]), SPREAD + ("tp",))
    sum_up, sum_gate = hidden_scale_grads(jnp.stack([sum_up, sum_gate]))
    return (
        jnp.stack([mid[m][0] for m in micros])[:, None],
        jnp.stack([back[m][0] for m in micros])[:, None],
        grad_q,
        grad_k,
        grad_v,
        grad_o.T,
        grad_u.T,
        grad_g.T,
        grad_d,
        alphas[:width],
        alphas[width:],
        sum_qk,
        sum_up,
        sum_gate,
    )


def solution(mesh):
    return jax.shard_map(
        per_device,
        mesh=mesh,
        in_specs=(
            P(None, "shard", ("ctx", "tp"), None),
            P(None, "shard", None),
            P(None, "shard", None),
            P(("shard", "ctx"), "tp"),
            P(("shard", "ctx"), "tp"),
            P(("shard", "ctx"), "tp"),
            P("tp", ("shard", "ctx")),
            P(("shard", "ctx"), "tp"),
            P(("shard", "ctx"), "tp"),
            P("tp", ("shard", "ctx")),
            P(),
            P(),
            P("tp"),
            P("tp"),
            P("tp"),
            P(None, "shard", ("ctx", "tp"), None),
        ),
        out_specs=(
            P(None, "shard", ("ctx", "tp"), None),
            P(None, "shard", ("ctx", "tp"), None),
            P(("shard", "ctx"), "tp"),
            P(("shard", "ctx"), "tp"),
            P(("shard", "ctx"), "tp"),
            P("tp", ("shard", "ctx")),
            P(("shard", "ctx"), "tp"),
            P(("shard", "ctx"), "tp"),
            P("tp", ("shard", "ctx")),
            P(),
            P(),
            P("tp"),
            P("tp"),
            P("tp"),
        ),
        check_vma=False,
    )
```

```python
import math

import jax
import jax.numpy as jnp
from jax import lax
from jax.experimental import pallas as pl
from jax.experimental.pallas import tpu as pltpu
from jax.sharding import PartitionSpec as P

D = 1280
HDIM = 64
SEG = 64
SEGS = 40
TREE_TOK = 2560


EPSILON = 1e-06
HIGHEST = lax.Precision.HIGHEST
SPREAD = ("shard", "ctx")


def unit_rows(values):
    return values * lax.rsqrt(jnp.sum(values * values, axis=-1, keepdims=True) + EPSILON)


def unit_heads(values):
    shaped = values.reshape(values.shape[0], values.shape[1] // HDIM, HDIM)
    return unit_rows(shaped).reshape(values.shape)


def contract_rows(former, latter):
    return lax.dot_general(
        former, latter, (((0,), (0,)), ((), ())), preferred_element_type=jnp.float32
    )


def contract_cols(former, latter):
    return lax.dot_general(
        former, latter, (((1,), (1,)), ((), ())), preferred_element_type=jnp.float32
    )


def mix_rows(residual, branch, mixing):
    return unit_rows(residual + mixing * (unit_rows(branch) - residual))


def query_key(query_raw, key_raw, gain_qk):
    return (unit_heads(query_raw) * gain_qk, unit_heads(key_raw) * gain_qk)


def middle(up_raw, gate_raw, scale_up, scale_gate):
    return up_raw * scale_up * jax.nn.silu(gate_raw * (scale_gate * math.sqrt(D)))


def swap(value, axis, bit):
    size = lax.axis_size(axis)
    return lax.ppermute(value, axis, [(place, place ^ bit) for place in range(size)])


def add_low(former, latter):
    return (former.astype(jnp.float32) + latter.astype(jnp.float32)).astype(jnp.bfloat16)


def butterfly(value, axes):
    for axis in axes:
        bit = 1
        while bit < lax.axis_size(axis):
            value = value + swap(value, axis, bit)
            bit *= 2
    return value


def group_order(axis):
    size = lax.axis_size(axis)
    places = jnp.arange(size, dtype=jnp.int32)
    return places ^ lax.axis_index(axis) if size == 4 else places


def group_gather(own_block, axis):
    if lax.axis_size(axis) != 4:
        return lax.all_gather(own_block, axis, axis=0, tiled=True)
    across = swap(own_block, axis, 2)
    beside = swap(own_block, axis, 1)
    return jnp.concatenate([own_block, beside, across, swap(across, axis, 1)], axis=0)


def group_scatter(partial_low, axis):
    if lax.axis_size(axis) != 4:
        return lax.psum_scatter(partial_low, axis, scatter_dimension=0, tiled=True).astype(
            jnp.float32
        )
    own, beside, across, far = jnp.split(partial_low, 4, axis=0)
    far = swap(far, axis, 1)
    beside = swap(beside, axis, 1)
    across = swap(add_low(across, far), axis, 2)
    return own.astype(jnp.float32) + beside.astype(jnp.float32) + across.astype(jnp.float32)


def in_plane():
    return (lax.axis_size("shard"), lax.axis_size("ctx"), lax.axis_size("tp")) == (2, 4, 4)


def hop(value, bits):
    return lax.ppermute(value, SPREAD, [(place, place ^ bits) for place in range(8)])


def hidden_gather(own_block):
    if not in_plane():
        return group_gather(own_block, "tp")
    return jnp.concatenate([own_block] + [hop(own_block, bits) for bits in (2, 4, 6)], axis=0)


def hidden_scatter(partial_low):
    if not in_plane():
        return group_scatter(partial_low, "tp")
    own, along, aside, across = jnp.split(partial_low, 4, axis=0)
    total = own.astype(jnp.float32)
    for value, bits in ((along, 2), (aside, 4), (across, 6)):
        total = total + hop(value, bits).astype(jnp.float32)
    return total


def hidden_shards(w_up, w_gate, w_down):
    if not in_plane():
        return jnp.stack([w_up.T, w_gate.T, w_down])
    rows, hidden = w_up.shape
    part = hidden // 8
    packed = jnp.stack(
        [
            w_up.reshape(rows, 8, part).transpose(1, 2, 0),
            w_gate.reshape(rows, 8, part).transpose(1, 2, 0),
            w_down.reshape(8, part, rows),
        ],
        axis=1,
    )
    packed = lax.all_to_all(packed, SPREAD, 0, 0)
    return packed.transpose(1, 2, 0, 3).reshape(3, part, 8 * rows)


def hidden_weights(matrices):
    if not in_plane():
        return tuple(
            lax.all_gather(matrices[place], SPREAD, axis=1, tiled=True) for place in range(3)
        )
    out = []
    for place in range(3):
        own_core = group_gather(matrices[place], "tp")
        out.append(jnp.concatenate([own_core, swap(own_core, "ctx", 1)], axis=0))
    return tuple(out)


def hidden_scales(*scales):
    if not in_plane():
        return scales
    part = scales[0].shape[0] // 8
    first = lax.axis_index(SPREAD) * part
    own = jnp.stack([lax.dynamic_slice_in_dim(scale, first, part) for scale in scales])
    line = group_gather(own[None], "tp")
    both = jnp.concatenate([line, swap(line, "ctx", 1)], axis=0)
    return tuple(both[:, place].reshape(-1) for place in range(len(scales)))


def hidden_weight_grads(products):
    if not in_plane():
        return [
            lax.psum_scatter(product, SPREAD, scatter_dimension=1, tiled=True).astype(jnp.float32)
            for product in products
        ]
    sums = []
    for product in products:
        half = product.shape[0] // 2
        line = add_low(product[:half], swap(product[half:], "ctx", 1))
        sums.append(group_scatter(line, "tp").astype(jnp.bfloat16))
    part, width = sums[0].shape
    packed = jnp.stack([total.reshape(part, 8, width // 8).transpose(1, 0, 2) for total in sums], 1)
    packed = lax.all_to_all(packed, SPREAD, 0, 0).astype(jnp.float32)
    return [packed[:, place].reshape(8 * part, width // 8) for place in range(3)]


def hidden_scale_grads(sums):
    if not in_plane():
        return butterfly(sums, SPREAD)
    count, hidden = sums.shape
    parts = sums.reshape(count, 2, 4, hidden // 8)
    line = hidden_line_sum(parts[:, 0] + swap(parts[:, 1], "ctx", 1))
    blank = jnp.zeros((count, 8, hidden // 8), jnp.float32)
    place = lax.axis_index(SPREAD)
    spread_out = lax.dynamic_update_slice_in_dim(blank, line[:, None], place, 1)
    return butterfly(spread_out, SPREAD).reshape(count, hidden)


def hidden_line_sum(parts):
    own, beside, across, far = (parts[:, place] for place in range(4))
    across = across + swap(far, "tp", 1)
    return own + swap(beside, "tp", 1) + swap(across, "tp", 2)


def owner_scatter(product_low):
    if lax.axis_size("ctx") != 4 or lax.axis_size("shard") != 2:
        return lax.psum_scatter(
            product_low, ("shard", "ctx"), scatter_dimension=0, tiled=True
        ).astype(jnp.float32)
    place = lax.axis_index("ctx")
    core, along = place % 2, place // 2
    plane = lax.axis_index("shard")
    rows, width = product_low.shape
    blocks = product_low.reshape(2, 2, 2, rows // 8, width)

    def pick(value, index, axis):
        return lax.dynamic_index_in_dim(value, index, axis, keepdims=False)

    blocks = add_low(pick(blocks, core, 2), swap(pick(blocks, 1 - core, 2), "ctx", 1))
    former, latter = blocks[..., : width // 2], blocks[..., width // 2 :]
    former_in = swap(pick(former, 1 - along, 1), "ctx", 2)
    latter_in = swap(pick(latter, 1 - plane, 0), "shard", 1)
    former = add_low(pick(former, along, 1), former_in)
    latter = add_low(pick(latter, plane, 0), latter_in)
    former_in = swap(pick(former, 1 - plane, 0), "shard", 1)
    latter_in = swap(pick(latter, 1 - along, 0), "ctx", 2)
    return jnp.concatenate(
        [
            pick(former, plane, 0).astype(jnp.float32) + former_in.astype(jnp.float32),
            pick(latter, along, 0).astype(jnp.float32) + latter_in.astype(jnp.float32),
        ],
        axis=1,
    )


def row_labels(slots, group_size):
    tree_rows = group_size * lax.axis_size("ctx")
    chunk = group_size // lax.axis_size("tp")
    within = (group_order("tp")[:, None] * chunk + jnp.arange(chunk, dtype=jnp.int32)).reshape(-1)
    keys = (group_order("ctx")[:, None] * group_size + within[None, :]).reshape(-1)
    onehot = (keys[:, None] // SEG == jnp.arange(tree_rows // SEG, dtype=jnp.int32)[None, :])
    segment = jnp.sum(jnp.where(onehot, slots[None, :], 0), axis=1)
    offset = keys % SEG
    if lax.axis_size("ctx") != 4:
        first = lax.axis_index("ctx") * group_size
    else:
        first = 0
    return (
        lax.dynamic_slice_in_dim(segment, first, group_size),
        lax.dynamic_slice_in_dim(offset, first, group_size),
        segment,
        offset,
    )


LOG2_SCALE = math.sqrt(HDIM) * math.log2(math.e)
LANES = 128
KEY_TILE = 256


def half_kept(value, unit, axis):
    place = lax.broadcasted_iota(jnp.int32, value.shape, axis)
    inside = (place >= HDIM) if unit % 2 else (place < HDIM)
    return jnp.where(inside, value, jnp.zeros_like(value))


def seen_tile(hot_ref, side_ref):
    hot = hot_ref[...]
    strict = jnp.dot(hot, side_ref[0], preferred_element_type=jnp.float32)
    same = jnp.dot(hot, side_ref[1], preferred_element_type=jnp.float32)
    before = jnp.dot(hot, side_ref[2], preferred_element_type=jnp.float32)
    return (strict + same * before).astype(jnp.bfloat16)


def pair_of(unit):
    return slice(unit // 2 * LANES, unit // 2 * LANES + LANES)


def attend_body(query_ref, tree_ref, hot_ref, side_ref, out_ref, scale_ref, turned_ref, sum_ref):
    heads = query_ref.shape[1] // HDIM
    step = pl.program_id(0)

    @pl.when(step == 0)
    def prepare():
        turned = query_ref[...].astype(jnp.float32).T.astype(jnp.bfloat16)
        blank = jnp.zeros((HDIM, turned.shape[1]), jnp.bfloat16)
        for head in range(heads):
            own = turned[head * HDIM : (head + 1) * HDIM]
            halves = [blank, own] if head % 2 else [own, blank]
            turned_ref[head] = jnp.concatenate(halves, axis=0)
        sum_ref[...] = jnp.zeros_like(sum_ref)

    tree = tree_ref[...]
    values_turned = tree[:, heads * HDIM :].astype(jnp.float32).T.astype(jnp.bfloat16)
    seen = seen_tile(hot_ref, side_ref)
    ones = jnp.ones((sum_ref.shape[1] - HDIM, tree.shape[0]), jnp.bfloat16)
    for head in range(heads):
        scores = jnp.dot(tree[:, pair_of(head)], turned_ref[head], preferred_element_type=jnp.float32)
        lifted = jnp.exp2(scores * LOG2_SCALE).astype(jnp.bfloat16) * seen
        own = jnp.concatenate([values_turned[head * HDIM : (head + 1) * HDIM], ones], axis=0)
        sum_ref[head] += jnp.dot(own, lifted, preferred_element_type=jnp.float32)

    @pl.when(step == pl.num_programs(0) - 1)
    def finish():
        parts = []
        for head in range(heads):
            inverse = 1.0 / sum_ref[head, HDIM : HDIM + 1]
            scale_ref[head : head + 1] = inverse
            parts.append(sum_ref[head, :HDIM] * inverse)
        out_ref[...] = jnp.concatenate(parts, axis=0).T.astype(jnp.bfloat16)


def attend(query, tree, hot, side):
    rows, features = query.shape
    keys, width = tree.shape
    heads = features // HDIM
    whole = lambda step: (0, 0)
    return pl.pallas_call(
        attend_body,
        grid=(keys // KEY_TILE,),
        in_specs=[
            pl.BlockSpec((rows, features), whole),
            pl.BlockSpec((KEY_TILE, width), lambda step: (step, 0)),
            pl.BlockSpec((KEY_TILE, LANES), lambda step: (step, 0)),
            pl.BlockSpec((3, LANES, rows), lambda step: (0, 0, 0)),
        ],
        out_specs=[
            pl.BlockSpec((rows, features), whole),
            pl.BlockSpec((8, rows), whole),
        ],
        out_shape=[
            jax.ShapeDtypeStruct((rows, features), jnp.bfloat16),
            jax.ShapeDtypeStruct((8, rows), jnp.float32),
        ],
        scratch_shapes=[
            pltpu.VMEM((heads, LANES, rows), jnp.bfloat16),
            pltpu.VMEM((heads, HDIM + 16, rows), jnp.float32),
        ],
        compiler_params=pltpu.CompilerParams(vmem_limit_bytes=48 << 20),
        name="attend",
    )(query, tree, hot, side)


def attend_grad_body(
    both_ref, heads_ref, tree_ref, hot_ref, side_ref, scale_ref,
    query_out, tree_out, turned_ref, plain_ref, delta_ref, sum_ref,
):
    heads = heads_ref.shape[1] // HDIM
    units = 2 * heads
    step = pl.program_id(0)

    @pl.when(step == 0)
    def prepare():
        both = both_ref[...]
        turned = both.astype(jnp.float32).T
        outs = heads_ref[...].astype(jnp.float32).T
        blank = jnp.zeros((HDIM, turned.shape[1]), jnp.bfloat16)
        for unit in range(units):
            own = turned[unit * HDIM : (unit + 1) * HDIM].astype(jnp.bfloat16)
            halves = [blank, own] if unit % 2 else [own, blank]
            turned_ref[unit] = jnp.concatenate(halves, axis=0)
            plain_ref[unit] = half_kept(both[:, pair_of(unit)], unit, 1)
        for head in range(heads):
            rows = slice(head * HDIM, (head + 1) * HDIM)
            upstream = turned[(heads + head) * HDIM : (heads + head + 1) * HDIM]
            delta_ref[head : head + 1] = jnp.sum(outs[rows] * upstream, axis=0, keepdims=True)
        sum_ref[...] = jnp.zeros_like(sum_ref)

    tree = tree_ref[...]
    keys_turned = tree[:, : heads * HDIM].astype(jnp.float32).T.astype(jnp.bfloat16)
    seen = seen_tile(hot_ref, side_ref)
    weights, slopes = [], []
    for head in range(heads):
        scores = jnp.dot(tree[:, pair_of(head)], turned_ref[head], preferred_element_type=jnp.float32)
        weight = jnp.exp2(scores * LOG2_SCALE) * scale_ref[head : head + 1]
        pull = jnp.dot(
            tree[:, pair_of(heads + head)], turned_ref[heads + head], preferred_element_type=jnp.float32
        )
        slope = (weight * (pull - delta_ref[head : head + 1])).astype(jnp.bfloat16) * seen
        rows = slice(head * HDIM, (head + 1) * HDIM)
        sum_ref[rows] += jnp.dot(keys_turned[rows], slope, preferred_element_type=jnp.float32)
        weights.append(weight.astype(jnp.bfloat16) * seen)
        slopes.append(slope)
    terms = slopes + weights
    score_scale = math.sqrt(HDIM)
    for pair in range(heads):
        total = 0.0
        for unit in (2 * pair, 2 * pair + 1):
            part = jnp.dot(terms[unit], plain_ref[unit], preferred_element_type=jnp.float32)
            total = total + (part * score_scale if unit < heads else part)
        tree_out[:, pair * LANES : (pair + 1) * LANES] = total.astype(jnp.bfloat16)

    @pl.when(step == pl.num_programs(0) - 1)
    def finish():
        query_out[...] = sum_ref[...].T * score_scale


def attend_grad(query, upstream, outs, tree, hot, side, scale):
    rows, features = query.shape
    keys, width = tree.shape
    heads = features // HDIM
    whole = lambda step: (0, 0)
    return pl.pallas_call(
        attend_grad_body,
        grid=(keys // KEY_TILE,),
        in_specs=[
            pl.BlockSpec((rows, 2 * features), whole),
            pl.BlockSpec((rows, features), whole),
            pl.BlockSpec((KEY_TILE, width), lambda step: (step, 0)),
            pl.BlockSpec((KEY_TILE, LANES), lambda step: (step, 0)),
            pl.BlockSpec((3, LANES, rows), lambda step: (0, 0, 0)),
            pl.BlockSpec((8, rows), whole),
        ],
        out_specs=[
            pl.BlockSpec((rows, features), whole),
            pl.BlockSpec((KEY_TILE, width), lambda step: (step, 0)),
        ],
        out_shape=[
            jax.ShapeDtypeStruct((rows, features), jnp.float32),
            jax.ShapeDtypeStruct((keys, width), jnp.bfloat16),
        ],
        scratch_shapes=[
            pltpu.VMEM((2 * heads, LANES, rows), jnp.bfloat16),
            pltpu.VMEM((2 * heads, rows, LANES), jnp.bfloat16),
            pltpu.VMEM((8, rows), jnp.float32),
            pltpu.VMEM((features, rows), jnp.float32),
        ],
        compiler_params=pltpu.CompilerParams(vmem_limit_bytes=48 << 20),
        name="attend_grad",
    )(jnp.concatenate([query, upstream], axis=1), outs, tree, hot, side, scale)


def seen_factors(reachable, seg_query, off_query, segment, offset):
    segs = reachable.shape[0]
    labels = jnp.arange(LANES, dtype=jnp.int32)
    key_mark = jnp.where(labels < HDIM, segment[:, None], offset[:, None] + HDIM)
    hot = (key_mark == labels[None, :]).astype(jnp.bfloat16)
    query_hot = (labels[:, None] == seg_query[None, :]).astype(jnp.float32)
    wide = jnp.zeros((LANES, LANES), jnp.float32).at[:segs, :segs].set(reachable.T - jnp.eye(segs, dtype=jnp.float32))
    strict = jnp.dot(wide, query_hot, preferred_element_type=jnp.float32)
    same = query_hot
    before = ((labels[:, None] >= HDIM) & (labels[:, None] - HDIM <= off_query[None, :])).astype(jnp.float32)
    return hot, jnp.stack([strict, same, before]).astype(jnp.bfloat16)


def visibility(parents, slots, group_size):
    labels = jnp.arange(SEGS, dtype=jnp.int32)
    linked = (parents[:, None] == labels[None, :]).astype(jnp.float32)
    reachable = jnp.maximum(linked, jnp.eye(SEGS, dtype=jnp.float32))
    for doubling in range(SEGS.bit_length()):
        reachable = jnp.minimum(jnp.dot(reachable, reachable, precision=HIGHEST), 1.0)
    return seen_factors(reachable, *row_labels(slots, group_size))


def forward_attention(gathered, vectors, hidden_group, parents, slots):
    w_query, w_key, w_value, w_attn_out = gathered
    alpha_attn, alpha_mlp, scale_qk, scale_up, scale_gate = vectors
    visible = visibility(parents, slots, hidden_group.shape[0])
    query_raw = jnp.dot(hidden_group, w_query, preferred_element_type=jnp.float32)
    key_raw = jnp.dot(hidden_group, w_key, preferred_element_type=jnp.float32)
    value_low = jnp.dot(hidden_group, w_value, preferred_element_type=jnp.float32).astype(
        jnp.bfloat16
    )
    query_unit, key_unit = query_key(query_raw, key_raw, scale_qk)
    queries = query_unit.astype(jnp.bfloat16)
    keys_own = key_unit.astype(jnp.bfloat16)
    keys_values = group_gather(jnp.concatenate([keys_own, value_low], axis=1), "ctx")
    heads_low, scale = attend(queries, keys_values, *visible)
    branch_one = group_scatter(contract_cols(heads_low, w_attn_out).astype(jnp.bfloat16), "tp")
    kept = (
        hidden_group,
        visible,
        query_raw,
        key_raw,
        queries,
        keys_values,
        scale,
        heads_low,
    )
    return branch_one, kept


def feed_forward(gathered, vectors, tokens_own, branch_one, cotangent_own):
    w_up, w_gate, w_down = gathered
    alpha_attn, alpha_mlp, scale_qk, scale_up, scale_gate = vectors
    tokens_wide = tokens_own.astype(jnp.float32)
    hidden_one = mix_rows(tokens_wide, branch_one, alpha_attn)
    hidden_one_group = hidden_gather(hidden_one.astype(jnp.bfloat16))
    up_raw = contract_cols(hidden_one_group, w_up)
    gate_raw = contract_cols(hidden_one_group, w_gate)
    mixed_low = middle(up_raw, gate_raw, scale_up, scale_gate).astype(jnp.bfloat16)
    branch_two = hidden_scatter(
        jnp.dot(mixed_low, w_down, preferred_element_type=jnp.float32).astype(jnp.bfloat16)
    )
    output_wide, pull_out = jax.vjp(mix_rows, hidden_one, branch_two, alpha_mlp)
    upstream = cotangent_own.astype(jnp.float32)
    hidden_one_direct, branch_two_grad, grad_alpha_mlp = pull_out(upstream)
    branch_two_group = hidden_gather(branch_two_grad.astype(jnp.bfloat16))
    mixed_grad = contract_cols(branch_two_group, w_down).astype(jnp.bfloat16).astype(jnp.float32)
    middle_value, pull_mid = jax.vjp(middle, up_raw, gate_raw, scale_up, scale_gate)
    up_grad, gate_grad, grad_scale_up, grad_scale_gate = pull_mid(mixed_grad)
    up_low = up_grad.astype(jnp.bfloat16)
    gate_low = gate_grad.astype(jnp.bfloat16)
    hidden_one_grad = hidden_one_direct + hidden_scatter(
        (
            jnp.dot(up_low, w_up, preferred_element_type=jnp.float32)
            + jnp.dot(gate_low, w_gate, preferred_element_type=jnp.float32)
        ).astype(jnp.bfloat16)
    )
    hidden_again, pull_in = jax.vjp(mix_rows, tokens_wide, branch_one, alpha_attn)
    tokens_direct, branch_one_grad, grad_alpha_attn = pull_in(hidden_one_grad)
    factors = (mixed_low, branch_two_group, hidden_one_group, up_low, gate_low)
    sums = (grad_alpha_attn, grad_alpha_mlp, grad_scale_up, grad_scale_gate)
    return output_wide.astype(jnp.bfloat16), tokens_direct, branch_one_grad, factors, sums


def backward_attention(gathered, vectors, kept, branch_one_group, tokens_direct):
    w_query, w_key, w_value, w_attn_out = gathered
    scale_qk = vectors[2]
    (
        hidden_group,
        visible,
        query_raw,
        key_raw,
        queries,
        keys_values,
        scale,
        heads_low,
    ) = kept
    heads_grad = jnp.dot(
        branch_one_group, w_attn_out, preferred_element_type=jnp.float32
    ).astype(jnp.bfloat16)
    query_grads, tree_grads = attend_grad(
        queries, heads_grad, heads_low, keys_values, *visible, scale
    )
    key_own_grad, value_own_grad = jnp.split(group_scatter(tree_grads, "ctx"), 2, axis=1)
    unit_again, pull_qk = jax.vjp(query_key, query_raw, key_raw, scale_qk)
    query_raw_grad, key_raw_grad, grad_scale_qk = pull_qk((query_grads, key_own_grad))
    query_low = query_raw_grad.astype(jnp.bfloat16)
    key_low = key_raw_grad.astype(jnp.bfloat16)
    value_grad_low = value_own_grad.astype(jnp.bfloat16)
    input_part = (
        contract_cols(query_low, w_query)
        + contract_cols(key_low, w_key)
        + contract_cols(value_grad_low, w_value)
    )
    grad_tokens = tokens_direct + group_scatter(input_part.astype(jnp.bfloat16), "tp")
    factors = (hidden_group, query_low, key_low, value_grad_low, heads_low, branch_one_group)
    return grad_tokens, factors, grad_scale_qk


def per_device(
    tokens,
    parents,
    slot_segment,
    w_query,
    w_key,
    w_value,
    w_attn_out,
    w_up,
    w_gate,
    w_down,
    alpha_attn,
    alpha_mlp,
    scale_qk,
    scale_up,
    scale_gate,
    cotangent,
):
    local_heads = w_query.shape[1]
    vectors = (alpha_attn, alpha_mlp, scale_qk) + hidden_scales(scale_up, scale_gate)

    def spread_gather(own_block):
        return lax.all_gather(own_block, SPREAD, axis=0, tiled=True)

    packed = spread_gather(jnp.concatenate([w_query, w_key, w_value, w_attn_out.T], axis=1))
    gathered = (
        packed[:, :local_heads],
        packed[:, local_heads : 2 * local_heads],
        packed[:, 2 * local_heads : 3 * local_heads],
        packed[:, 3 * local_heads :],
    )
    micros = range(tokens.shape[0])
    groups = [group_gather(tokens[m, 0], "tp") for m in micros]
    shards, groups = lax.optimization_barrier((hidden_shards(w_up, w_gate, w_down), groups))
    hidden_gathered = hidden_weights(shards)
    front = [
        forward_attention(gathered, vectors, groups[m], parents[m, 0], slot_segment[m, 0])
        for m in micros
    ]
    mid = [
        feed_forward(hidden_gathered, vectors, tokens[m, 0], front[m][0], cotangent[m, 0])
        for m in micros
    ]
    tops = [group_gather(mid[m][2].astype(jnp.bfloat16), "tp") for m in micros]

    def stack(pick):
        return jnp.concatenate([pick(m) for m in micros], axis=0)

    mixed_all, top_all, hidden_all, up_all, gate_all = (
        stack(lambda m: mid[m][3][place]) for place in range(5)
    )
    products = [
        contract_rows(former, latter).astype(jnp.bfloat16)
        for former, latter in (
            (up_all, hidden_all),
            (gate_all, hidden_all),
            (mixed_all, top_all),
        )
    ]
    products, tops[-1] = lax.optimization_barrier((products, tops[-1]))
    back = [
        backward_attention(gathered, vectors, front[m][1], tops[m], mid[m][1]) for m in micros
    ]
    tokens_all, query_all, key_all, value_all, heads_all, branch_all = (
        stack(lambda m: back[m][1][place]) for place in range(6)
    )

    grad_u, grad_g, grad_d = hidden_weight_grads(products)
    attention_product = jnp.concatenate(
        [
            contract_rows(tokens_all, query_all),
            contract_rows(tokens_all, key_all),
            contract_rows(tokens_all, value_all),
            contract_rows(branch_all, heads_all),
        ],
        axis=1,
    )
    grad_attention = owner_scatter(attention_product.astype(jnp.bfloat16))
    grad_q, grad_k, grad_v, grad_o = jnp.split(grad_attention, 4, axis=1)

    sum_attn, sum_mlp, sum_up, sum_gate = (
        sum(mid[m][4][place] for m in micros) for place in range(4)
    )
    sum_qk = butterfly(sum(back[m][2] for m in micros), SPREAD)
    width = sum_attn.shape[0]
    alphas = butterfly(jnp.concatenate([sum_attn, sum_mlp]), SPREAD + ("tp",))
    sum_up, sum_gate = hidden_scale_grads(jnp.stack([sum_up, sum_gate]))
    return (
        jnp.stack([mid[m][0] for m in micros])[:, None],
        jnp.stack([back[m][0] for m in micros])[:, None],
        grad_q,
        grad_k,
        grad_v,
        grad_o.T,
        grad_u.T,
        grad_g.T,
        grad_d,
        alphas[:width],
        alphas[width:],
        sum_qk,
        sum_up,
        sum_gate,
    )


def solution(mesh):
    return jax.shard_map(
        per_device,
        mesh=mesh,
        in_specs=(
            P(None, "shard", ("ctx", "tp"), None),
            P(None, "shard", None),
            P(None, "shard", None),
            P(("shard", "ctx"), "tp"),
            P(("shard", "ctx"), "tp"),
            P(("shard", "ctx"), "tp"),
            P("tp", ("shard", "ctx")),
            P(("shard", "ctx"), "tp"),
            P(("shard", "ctx"), "tp"),
            P("tp", ("shard", "ctx")),
            P(),
            P(),
            P("tp"),
            P("tp"),
            P("tp"),
            P(None, "shard", ("ctx", "tp"), None),
        ),
        out_specs=(
            P(None, "shard", ("ctx", "tp"), None),
            P(None, "shard", ("ctx", "tp"), None),
            P(("shard", "ctx"), "tp"),
            P(("shard", "ctx"), "tp"),
            P(("shard", "ctx"), "tp"),
            P("tp", ("shard", "ctx")),
            P(("shard", "ctx"), "tp"),
            P(("shard", "ctx"), "tp"),
            P("tp", ("shard", "ctx")),
            P(),
            P(),
            P("tp"),
            P("tp"),
            P("tp"),
        ),
        check_vma=False,
    )
```

```python
import math

import jax
import jax.numpy as jnp
from jax import lax
from jax.experimental import pallas as pl
from jax.experimental.pallas import tpu as pltpu
from jax.sharding import PartitionSpec as P

D = 1280
HDIM = 64
SEG = 64
SEGS = 40
TREE_TOK = 2560


EPSILON = 1e-06
HIGHEST = lax.Precision.HIGHEST
SPREAD = ("shard", "ctx")


def unit_rows(values):
    return values * lax.rsqrt(jnp.sum(values * values, axis=-1, keepdims=True) + EPSILON)


def unit_heads(values):
    shaped = values.reshape(values.shape[0], values.shape[1] // HDIM, HDIM)
    return unit_rows(shaped).reshape(values.shape)


def contract_rows(former, latter):
    return lax.dot_general(
        former, latter, (((0,), (0,)), ((), ())), preferred_element_type=jnp.float32
    )


def contract_cols(former, latter):
    return lax.dot_general(
        former, latter, (((1,), (1,)), ((), ())), preferred_element_type=jnp.float32
    )


def mix_rows(residual, branch, mixing):
    return unit_rows(residual + mixing * (unit_rows(branch) - residual))


def query_key(query_raw, key_raw, gain_qk):
    return (unit_heads(query_raw) * gain_qk, unit_heads(key_raw) * gain_qk)


def middle(up_raw, gate_raw, scale_up, scale_gate):
    return up_raw * scale_up * jax.nn.silu(gate_raw * (scale_gate * math.sqrt(D)))


def swap(value, axis, bit):
    size = lax.axis_size(axis)
    return lax.ppermute(value, axis, [(place, place ^ bit) for place in range(size)])


def add_low(former, latter):
    return (former.astype(jnp.float32) + latter.astype(jnp.float32)).astype(jnp.bfloat16)


def butterfly(value, axes):
    for axis in axes:
        bit = 1
        while bit < lax.axis_size(axis):
            value = value + swap(value, axis, bit)
            bit *= 2
    return value


def group_order(axis):
    size = lax.axis_size(axis)
    places = jnp.arange(size, dtype=jnp.int32)
    return places ^ lax.axis_index(axis) if size == 4 else places


def group_gather(own_block, axis):
    if lax.axis_size(axis) != 4:
        return lax.all_gather(own_block, axis, axis=0, tiled=True)
    across = swap(own_block, axis, 2)
    beside = swap(own_block, axis, 1)
    return jnp.concatenate([own_block, beside, across, swap(across, axis, 1)], axis=0)


def group_scatter(partial_low, axis):
    if lax.axis_size(axis) != 4:
        return lax.psum_scatter(partial_low, axis, scatter_dimension=0, tiled=True).astype(
            jnp.float32
        )
    own, beside, across, far = jnp.split(partial_low, 4, axis=0)
    far = swap(far, axis, 1)
    beside = swap(beside, axis, 1)
    across = swap(add_low(across, far), axis, 2)
    return own.astype(jnp.float32) + beside.astype(jnp.float32) + across.astype(jnp.float32)


def in_plane():
    return (lax.axis_size("shard"), lax.axis_size("ctx"), lax.axis_size("tp")) == (2, 4, 4)


def hop(value, bits):
    return lax.ppermute(value, SPREAD, [(place, place ^ bits) for place in range(8)])


def hidden_gather(own_block):
    if not in_plane():
        return group_gather(own_block, "tp")
    return jnp.concatenate([own_block] + [hop(own_block, bits) for bits in (2, 4, 6)], axis=0)


def hidden_scatter(partial_low):
    if not in_plane():
        return group_scatter(partial_low, "tp")
    own, along, aside, across = jnp.split(partial_low, 4, axis=0)
    total = own.astype(jnp.float32)
    for value, bits in ((along, 2), (aside, 4), (across, 6)):
        total = total + hop(value, bits).astype(jnp.float32)
    return total


def hidden_shards(w_up, w_gate, w_down):
    if not in_plane():
        return jnp.stack([w_up.T, w_gate.T, w_down])
    rows, hidden = w_up.shape
    part = hidden // 8
    packed = jnp.stack(
        [
            w_up.reshape(rows, 8, part).transpose(1, 2, 0),
            w_gate.reshape(rows, 8, part).transpose(1, 2, 0),
            w_down.reshape(8, part, rows),
        ],
        axis=1,
    )
    packed = lax.all_to_all(packed, SPREAD, 0, 0)
    return packed.transpose(1, 2, 0, 3).reshape(3, part, 8 * rows)


def hidden_weights(matrices):
    if not in_plane():
        return tuple(
            lax.all_gather(matrices[place], SPREAD, axis=1, tiled=True) for place in range(3)
        )
    out = []
    for place in range(3):
        own_core = lax.all_gather(matrices[place], "tp", axis=0, tiled=True)
        out.append(jnp.concatenate([own_core, swap(own_core, "ctx", 1)], axis=0))
    return tuple(out)


def hidden_scales(*scales):
    if not in_plane():
        return scales
    part = scales[0].shape[0] // 8
    first = lax.axis_index(SPREAD) * part
    own = jnp.stack([lax.dynamic_slice_in_dim(scale, first, part) for scale in scales])
    line = lax.all_gather(own, "tp")
    both = jnp.concatenate([line, swap(line, "ctx", 1)], axis=0)
    return tuple(both[:, place].reshape(-1) for place in range(len(scales)))


def hidden_weight_grads(products):
    if not in_plane():
        return [
            lax.psum_scatter(product, SPREAD, scatter_dimension=1, tiled=True).astype(jnp.float32)
            for product in products
        ]
    sums = []
    for product in products:
        half = product.shape[0] // 2
        line = add_low(product[:half], swap(product[half:], "ctx", 1))
        sums.append(lax.psum_scatter(line, "tp", scatter_dimension=0, tiled=True))
    part, width = sums[0].shape
    packed = jnp.stack([total.reshape(part, 8, width // 8).transpose(1, 0, 2) for total in sums], 1)
    packed = lax.all_to_all(packed, SPREAD, 0, 0).astype(jnp.float32)
    return [packed[:, place].reshape(8 * part, width // 8) for place in range(3)]


def hidden_scale_grads(sums):
    if not in_plane():
        return butterfly(sums, SPREAD)
    count, hidden = sums.shape
    parts = sums.reshape(count, 2, 4, hidden // 8)
    line = butterfly(parts[:, 0] + swap(parts[:, 1], "ctx", 1), ("tp",))
    line = lax.dynamic_index_in_dim(line, lax.axis_index("tp"), 1, keepdims=False)
    blank = jnp.zeros((count, 8, hidden // 8), jnp.float32)
    place = lax.axis_index(SPREAD)
    spread_out = lax.dynamic_update_slice_in_dim(blank, line[:, None], place, 1)
    return butterfly(spread_out, SPREAD).reshape(count, hidden)


def owner_scatter(product_low):
    if lax.axis_size("ctx") != 4 or lax.axis_size("shard") != 2:
        return lax.psum_scatter(
            product_low, ("shard", "ctx"), scatter_dimension=0, tiled=True
        ).astype(jnp.float32)
    place = lax.axis_index("ctx")
    core, along = place % 2, place // 2
    plane = lax.axis_index("shard")
    rows, width = product_low.shape
    blocks = product_low.reshape(2, 2, 2, rows // 8, width)

    def pick(value, index, axis):
        return lax.dynamic_index_in_dim(value, index, axis, keepdims=False)

    blocks = add_low(pick(blocks, core, 2), swap(pick(blocks, 1 - core, 2), "ctx", 1))
    former, latter = blocks[..., : width // 2], blocks[..., width // 2 :]
    former_in = swap(pick(former, 1 - along, 1), "ctx", 2)
    latter_in = swap(pick(latter, 1 - plane, 0), "shard", 1)
    former = add_low(pick(former, along, 1), former_in)
    latter = add_low(pick(latter, plane, 0), latter_in)
    former_in = swap(pick(former, 1 - plane, 0), "shard", 1)
    latter_in = swap(pick(latter, 1 - along, 0), "ctx", 2)
    return jnp.concatenate(
        [
            pick(former, plane, 0).astype(jnp.float32) + former_in.astype(jnp.float32),
            pick(latter, along, 0).astype(jnp.float32) + latter_in.astype(jnp.float32),
        ],
        axis=1,
    )


def row_labels(slots, group_size):
    tree_rows = group_size * lax.axis_size("ctx")
    chunk = group_size // lax.axis_size("tp")
    within = (group_order("tp")[:, None] * chunk + jnp.arange(chunk, dtype=jnp.int32)).reshape(-1)
    keys = (group_order("ctx")[:, None] * group_size + within[None, :]).reshape(-1)
    onehot = (keys[:, None] // SEG == jnp.arange(tree_rows // SEG, dtype=jnp.int32)[None, :])
    segment = jnp.sum(jnp.where(onehot, slots[None, :], 0), axis=1)
    offset = keys % SEG
    if lax.axis_size("ctx") != 4:
        first = lax.axis_index("ctx") * group_size
    else:
        first = 0
    return (
        lax.dynamic_slice_in_dim(segment, first, group_size),
        lax.dynamic_slice_in_dim(offset, first, group_size),
        segment,
        offset,
    )


LOG2_SCALE = math.sqrt(HDIM) * math.log2(math.e)
LANES = 128
KEY_TILE = 256


def half_kept(value, unit, axis):
    place = lax.broadcasted_iota(jnp.int32, value.shape, axis)
    inside = (place >= HDIM) if unit % 2 else (place < HDIM)
    return jnp.where(inside, value, jnp.zeros_like(value))


def seen_tile(hot_ref, side_ref):
    hot = hot_ref[...]
    strict = jnp.dot(hot, side_ref[0], preferred_element_type=jnp.float32)
    same = jnp.dot(hot, side_ref[1], preferred_element_type=jnp.float32)
    before = jnp.dot(hot, side_ref[2], preferred_element_type=jnp.float32)
    return (strict + same * before).astype(jnp.bfloat16)


def pair_of(unit):
    return slice(unit // 2 * LANES, unit // 2 * LANES + LANES)


def attend_body(query_ref, tree_ref, hot_ref, side_ref, out_ref, scale_ref, turned_ref, sum_ref):
    heads = query_ref.shape[1] // HDIM
    step = pl.program_id(0)

    @pl.when(step == 0)
    def prepare():
        turned = query_ref[...].astype(jnp.float32).T.astype(jnp.bfloat16)
        blank = jnp.zeros((HDIM, turned.shape[1]), jnp.bfloat16)
        for head in range(heads):
            own = turned[head * HDIM : (head + 1) * HDIM]
            halves = [blank, own] if head % 2 else [own, blank]
            turned_ref[head] = jnp.concatenate(halves, axis=0)
        sum_ref[...] = jnp.zeros_like(sum_ref)

    tree = tree_ref[...]
    values_turned = tree[:, heads * HDIM :].astype(jnp.float32).T.astype(jnp.bfloat16)
    seen = seen_tile(hot_ref, side_ref)
    ones = jnp.ones((sum_ref.shape[1] - HDIM, tree.shape[0]), jnp.bfloat16)
    for head in range(heads):
        scores = jnp.dot(tree[:, pair_of(head)], turned_ref[head], preferred_element_type=jnp.float32)
        lifted = jnp.exp2(scores * LOG2_SCALE).astype(jnp.bfloat16) * seen
        own = jnp.concatenate([values_turned[head * HDIM : (head + 1) * HDIM], ones], axis=0)
        sum_ref[head] += jnp.dot(own, lifted, preferred_element_type=jnp.float32)

    @pl.when(step == pl.num_programs(0) - 1)
    def finish():
        parts = []
        for head in range(heads):
            inverse = 1.0 / sum_ref[head, HDIM : HDIM + 1]
            scale_ref[head : head + 1] = inverse
            parts.append(sum_ref[head, :HDIM] * inverse)
        out_ref[...] = jnp.concatenate(parts, axis=0).T.astype(jnp.bfloat16)


def attend(query, tree, hot, side):
    rows, features = query.shape
    keys, width = tree.shape
    heads = features // HDIM
    whole = lambda step: (0, 0)
    return pl.pallas_call(
        attend_body,
        grid=(keys // KEY_TILE,),
        in_specs=[
            pl.BlockSpec((rows, features), whole),
            pl.BlockSpec((KEY_TILE, width), lambda step: (step, 0)),
            pl.BlockSpec((KEY_TILE, LANES), lambda step: (step, 0)),
            pl.BlockSpec((3, LANES, rows), lambda step: (0, 0, 0)),
        ],
        out_specs=[
            pl.BlockSpec((rows, features), whole),
            pl.BlockSpec((8, rows), whole),
        ],
        out_shape=[
            jax.ShapeDtypeStruct((rows, features), jnp.bfloat16),
            jax.ShapeDtypeStruct((8, rows), jnp.float32),
        ],
        scratch_shapes=[
            pltpu.VMEM((heads, LANES, rows), jnp.bfloat16),
            pltpu.VMEM((heads, HDIM + 16, rows), jnp.float32),
        ],
        compiler_params=pltpu.CompilerParams(vmem_limit_bytes=48 << 20),
        name="attend",
    )(query, tree, hot, side)


def attend_grad_body(
    both_ref, heads_ref, tree_ref, hot_ref, side_ref, scale_ref,
    query_out, tree_out, turned_ref, plain_ref, delta_ref, sum_ref,
):
    heads = heads_ref.shape[1] // HDIM
    units = 2 * heads
    step = pl.program_id(0)

    @pl.when(step == 0)
    def prepare():
        both = both_ref[...]
        turned = both.astype(jnp.float32).T
        outs = heads_ref[...].astype(jnp.float32).T
        blank = jnp.zeros((HDIM, turned.shape[1]), jnp.bfloat16)
        for unit in range(units):
            own = turned[unit * HDIM : (unit + 1) * HDIM].astype(jnp.bfloat16)
            halves = [blank, own] if unit % 2 else [own, blank]
            turned_ref[unit] = jnp.concatenate(halves, axis=0)
            plain_ref[unit] = half_kept(both[:, pair_of(unit)], unit, 1)
        for head in range(heads):
            rows = slice(head * HDIM, (head + 1) * HDIM)
            upstream = turned[(heads + head) * HDIM : (heads + head + 1) * HDIM]
            delta_ref[head : head + 1] = jnp.sum(outs[rows] * upstream, axis=0, keepdims=True)
        sum_ref[...] = jnp.zeros_like(sum_ref)

    tree = tree_ref[...]
    keys_turned = tree[:, : heads * HDIM].astype(jnp.float32).T.astype(jnp.bfloat16)
    seen = seen_tile(hot_ref, side_ref)
    weights, slopes = [], []
    for head in range(heads):
        scores = jnp.dot(tree[:, pair_of(head)], turned_ref[head], preferred_element_type=jnp.float32)
        weight = jnp.exp2(scores * LOG2_SCALE) * scale_ref[head : head + 1]
        pull = jnp.dot(
            tree[:, pair_of(heads + head)], turned_ref[heads + head], preferred_element_type=jnp.float32
        )
        slope = (weight * (pull - delta_ref[head : head + 1])).astype(jnp.bfloat16) * seen
        rows = slice(head * HDIM, (head + 1) * HDIM)
        sum_ref[rows] += jnp.dot(keys_turned[rows], slope, preferred_element_type=jnp.float32)
        weights.append(weight.astype(jnp.bfloat16) * seen)
        slopes.append(slope)
    terms = slopes + weights
    score_scale = math.sqrt(HDIM)
    for pair in range(heads):
        total = 0.0
        for unit in (2 * pair, 2 * pair + 1):
            part = jnp.dot(terms[unit], plain_ref[unit], preferred_element_type=jnp.float32)
            total = total + (part * score_scale if unit < heads else part)
        tree_out[:, pair * LANES : (pair + 1) * LANES] = total.astype(jnp.bfloat16)

    @pl.when(step == pl.num_programs(0) - 1)
    def finish():
        query_out[...] = sum_ref[...].T * score_scale


def attend_grad(query, upstream, outs, tree, hot, side, scale):
    rows, features = query.shape
    keys, width = tree.shape
    heads = features // HDIM
    whole = lambda step: (0, 0)
    return pl.pallas_call(
        attend_grad_body,
        grid=(keys // KEY_TILE,),
        in_specs=[
            pl.BlockSpec((rows, 2 * features), whole),
            pl.BlockSpec((rows, features), whole),
            pl.BlockSpec((KEY_TILE, width), lambda step: (step, 0)),
            pl.BlockSpec((KEY_TILE, LANES), lambda step: (step, 0)),
            pl.BlockSpec((3, LANES, rows), lambda step: (0, 0, 0)),
            pl.BlockSpec((8, rows), whole),
        ],
        out_specs=[
            pl.BlockSpec((rows, features), whole),
            pl.BlockSpec((KEY_TILE, width), lambda step: (step, 0)),
        ],
        out_shape=[
            jax.ShapeDtypeStruct((rows, features), jnp.float32),
            jax.ShapeDtypeStruct((keys, width), jnp.bfloat16),
        ],
        scratch_shapes=[
            pltpu.VMEM((2 * heads, LANES, rows), jnp.bfloat16),
            pltpu.VMEM((2 * heads, rows, LANES), jnp.bfloat16),
            pltpu.VMEM((8, rows), jnp.float32),
            pltpu.VMEM((features, rows), jnp.float32),
        ],
        compiler_params=pltpu.CompilerParams(vmem_limit_bytes=48 << 20),
        name="attend_grad",
    )(jnp.concatenate([query, upstream], axis=1), outs, tree, hot, side, scale)


def seen_factors(reachable, seg_query, off_query, segment, offset):
    segs = reachable.shape[0]
    labels = jnp.arange(LANES, dtype=jnp.int32)
    key_mark = jnp.where(labels < HDIM, segment[:, None], offset[:, None] + HDIM)
    hot = (key_mark == labels[None, :]).astype(jnp.bfloat16)
    query_hot = (labels[:, None] == seg_query[None, :]).astype(jnp.float32)
    wide = jnp.zeros((LANES, LANES), jnp.float32).at[:segs, :segs].set(reachable.T - jnp.eye(segs, dtype=jnp.float32))
    strict = jnp.dot(wide, query_hot, preferred_element_type=jnp.float32)
    same = query_hot
    before = ((labels[:, None] >= HDIM) & (labels[:, None] - HDIM <= off_query[None, :])).astype(jnp.float32)
    return hot, jnp.stack([strict, same, before]).astype(jnp.bfloat16)


def visibility(parents, slots, group_size):
    labels = jnp.arange(SEGS, dtype=jnp.int32)
    linked = (parents[:, None] == labels[None, :]).astype(jnp.float32)
    reachable = jnp.maximum(linked, jnp.eye(SEGS, dtype=jnp.float32))
    for doubling in range(SEGS.bit_length()):
        reachable = jnp.minimum(jnp.dot(reachable, reachable, precision=HIGHEST), 1.0)
    return seen_factors(reachable, *row_labels(slots, group_size))


def forward_attention(gathered, vectors, hidden_group, parents, slots):
    w_query, w_key, w_value, w_attn_out = gathered
    alpha_attn, alpha_mlp, scale_qk, scale_up, scale_gate = vectors
    visible = visibility(parents, slots, hidden_group.shape[0])
    query_raw = jnp.dot(hidden_group, w_query, preferred_element_type=jnp.float32)
    key_raw = jnp.dot(hidden_group, w_key, preferred_element_type=jnp.float32)
    value_low = jnp.dot(hidden_group, w_value, preferred_element_type=jnp.float32).astype(
        jnp.bfloat16
    )
    query_unit, key_unit = query_key(query_raw, key_raw, scale_qk)
    queries = query_unit.astype(jnp.bfloat16)
    keys_own = key_unit.astype(jnp.bfloat16)
    keys_values = group_gather(jnp.concatenate([keys_own, value_low], axis=1), "ctx")
    heads_low, scale = attend(queries, keys_values, *visible)
    branch_one = group_scatter(contract_cols(heads_low, w_attn_out).astype(jnp.bfloat16), "tp")
    kept = (
        hidden_group,
        visible,
        query_raw,
        key_raw,
        queries,
        keys_values,
        scale,
        heads_low,
    )
    return branch_one, kept


def feed_forward(gathered, vectors, tokens_own, branch_one, cotangent_own):
    w_up, w_gate, w_down = gathered
    alpha_attn, alpha_mlp, scale_qk, scale_up, scale_gate = vectors
    tokens_wide = tokens_own.astype(jnp.float32)
    hidden_one = mix_rows(tokens_wide, branch_one, alpha_attn)
    hidden_one_group = hidden_gather(hidden_one.astype(jnp.bfloat16))
    up_raw = contract_cols(hidden_one_group, w_up)
    gate_raw = contract_cols(hidden_one_group, w_gate)
    mixed_low = middle(up_raw, gate_raw, scale_up, scale_gate).astype(jnp.bfloat16)
    branch_two = hidden_scatter(
        jnp.dot(mixed_low, w_down, preferred_element_type=jnp.float32).astype(jnp.bfloat16)
    )
    output_wide, pull_out = jax.vjp(mix_rows, hidden_one, branch_two, alpha_mlp)
    upstream = cotangent_own.astype(jnp.float32)
    hidden_one_direct, branch_two_grad, grad_alpha_mlp = pull_out(upstream)
    branch_two_group = hidden_gather(branch_two_grad.astype(jnp.bfloat16))
    mixed_grad = contract_cols(branch_two_group, w_down).astype(jnp.bfloat16).astype(jnp.float32)
    middle_value, pull_mid = jax.vjp(middle, up_raw, gate_raw, scale_up, scale_gate)
    up_grad, gate_grad, grad_scale_up, grad_scale_gate = pull_mid(mixed_grad)
    up_low = up_grad.astype(jnp.bfloat16)
    gate_low = gate_grad.astype(jnp.bfloat16)
    hidden_one_grad = hidden_one_direct + hidden_scatter(
        (
            jnp.dot(up_low, w_up, preferred_element_type=jnp.float32)
            + jnp.dot(gate_low, w_gate, preferred_element_type=jnp.float32)
        ).astype(jnp.bfloat16)
    )
    hidden_again, pull_in = jax.vjp(mix_rows, tokens_wide, branch_one, alpha_attn)
    tokens_direct, branch_one_grad, grad_alpha_attn = pull_in(hidden_one_grad)
    factors = (mixed_low, branch_two_group, hidden_one_group, up_low, gate_low)
    sums = (grad_alpha_attn, grad_alpha_mlp, grad_scale_up, grad_scale_gate)
    return output_wide.astype(jnp.bfloat16), tokens_direct, branch_one_grad, factors, sums


def backward_attention(gathered, vectors, kept, branch_one_group, tokens_direct):
    w_query, w_key, w_value, w_attn_out = gathered
    scale_qk = vectors[2]
    (
        hidden_group,
        visible,
        query_raw,
        key_raw,
        queries,
        keys_values,
        scale,
        heads_low,
    ) = kept
    heads_grad = jnp.dot(
        branch_one_group, w_attn_out, preferred_element_type=jnp.float32
    ).astype(jnp.bfloat16)
    query_grads, tree_grads = attend_grad(
        queries, heads_grad, heads_low, keys_values, *visible, scale
    )
    key_own_grad, value_own_grad = jnp.split(group_scatter(tree_grads, "ctx"), 2, axis=1)
    unit_again, pull_qk = jax.vjp(query_key, query_raw, key_raw, scale_qk)
    query_raw_grad, key_raw_grad, grad_scale_qk = pull_qk((query_grads, key_own_grad))
    query_low = query_raw_grad.astype(jnp.bfloat16)
    key_low = key_raw_grad.astype(jnp.bfloat16)
    value_grad_low = value_own_grad.astype(jnp.bfloat16)
    input_part = (
        contract_cols(query_low, w_query)
        + contract_cols(key_low, w_key)
        + contract_cols(value_grad_low, w_value)
    )
    grad_tokens = tokens_direct + group_scatter(input_part.astype(jnp.bfloat16), "tp")
    factors = (hidden_group, query_low, key_low, value_grad_low, heads_low, branch_one_group)
    return grad_tokens, factors, grad_scale_qk


def per_device(
    tokens,
    parents,
    slot_segment,
    w_query,
    w_key,
    w_value,
    w_attn_out,
    w_up,
    w_gate,
    w_down,
    alpha_attn,
    alpha_mlp,
    scale_qk,
    scale_up,
    scale_gate,
    cotangent,
):
    local_heads = w_query.shape[1]
    vectors = (alpha_attn, alpha_mlp, scale_qk) + hidden_scales(scale_up, scale_gate)

    def spread_gather(own_block):
        return lax.all_gather(own_block, SPREAD, axis=0, tiled=True)

    packed = spread_gather(jnp.concatenate([w_query, w_key, w_value, w_attn_out.T], axis=1))
    gathered = (
        packed[:, :local_heads],
        packed[:, local_heads : 2 * local_heads],
        packed[:, 2 * local_heads : 3 * local_heads],
        packed[:, 3 * local_heads :],
    )
    micros = range(tokens.shape[0])
    groups = [group_gather(tokens[m, 0], "tp") for m in micros]
    shards, groups = lax.optimization_barrier((hidden_shards(w_up, w_gate, w_down), groups))
    hidden_gathered = hidden_weights(shards)
    front = [
        forward_attention(gathered, vectors, groups[m], parents[m, 0], slot_segment[m, 0])
        for m in micros
    ]
    mid = [
        feed_forward(hidden_gathered, vectors, tokens[m, 0], front[m][0], cotangent[m, 0])
        for m in micros
    ]
    tops = [group_gather(mid[m][2].astype(jnp.bfloat16), "tp") for m in micros]

    def stack(pick):
        return jnp.concatenate([pick(m) for m in micros], axis=0)

    mixed_all, top_all, hidden_all, up_all, gate_all = (
        stack(lambda m: mid[m][3][place]) for place in range(5)
    )
    products = [
        contract_rows(former, latter).astype(jnp.bfloat16)
        for former, latter in (
            (up_all, hidden_all),
            (gate_all, hidden_all),
            (mixed_all, top_all),
        )
    ]
    products, tops[-1] = lax.optimization_barrier((products, tops[-1]))
    back = [
        backward_attention(gathered, vectors, front[m][1], tops[m], mid[m][1]) for m in micros
    ]
    tokens_all, query_all, key_all, value_all, heads_all, branch_all = (
        stack(lambda m: back[m][1][place]) for place in range(6)
    )

    grad_u, grad_g, grad_d = hidden_weight_grads(products)
    attention_product = jnp.concatenate(
        [
            contract_rows(tokens_all, query_all),
            contract_rows(tokens_all, key_all),
            contract_rows(tokens_all, value_all),
            contract_rows(branch_all, heads_all),
        ],
        axis=1,
    )
    grad_attention = owner_scatter(attention_product.astype(jnp.bfloat16))
    grad_q, grad_k, grad_v, grad_o = jnp.split(grad_attention, 4, axis=1)

    sum_attn, sum_mlp, sum_up, sum_gate = (
        sum(mid[m][4][place] for m in micros) for place in range(4)
    )
    sum_qk = butterfly(sum(back[m][2] for m in micros), SPREAD)
    width = sum_attn.shape[0]
    alphas = butterfly(jnp.concatenate([sum_attn, sum_mlp]), SPREAD + ("tp",))
    sum_up, sum_gate = hidden_scale_grads(jnp.stack([sum_up, sum_gate]))
    return (
        jnp.stack([mid[m][0] for m in micros])[:, None],
        jnp.stack([back[m][0] for m in micros])[:, None],
        grad_q,
        grad_k,
        grad_v,
        grad_o.T,
        grad_u.T,
        grad_g.T,
        grad_d,
        alphas[:width],
        alphas[width:],
        sum_qk,
        sum_up,
        sum_gate,
    )


def solution(mesh):
    return jax.shard_map(
        per_device,
        mesh=mesh,
        in_specs=(
            P(None, "shard", ("ctx", "tp"), None),
            P(None, "shard", None),
            P(None, "shard", None),
            P(("shard", "ctx"), "tp"),
            P(("shard", "ctx"), "tp"),
            P(("shard", "ctx"), "tp"),
            P("tp", ("shard", "ctx")),
            P(("shard", "ctx"), "tp"),
            P(("shard", "ctx"), "tp"),
            P("tp", ("shard", "ctx")),
            P(),
            P(),
            P("tp"),
            P("tp"),
            P("tp"),
            P(None, "shard", ("ctx", "tp"), None),
        ),
        out_specs=(
            P(None, "shard", ("ctx", "tp"), None),
            P(None, "shard", ("ctx", "tp"), None),
            P(("shard", "ctx"), "tp"),
            P(("shard", "ctx"), "tp"),
            P(("shard", "ctx"), "tp"),
            P("tp", ("shard", "ctx")),
            P(("shard", "ctx"), "tp"),
            P(("shard", "ctx"), "tp"),
            P("tp", ("shard", "ctx")),
            P(),
            P(),
            P("tp"),
            P("tp"),
            P("tp"),
        ),
        check_vma=False,
    )
```

```python
import math

import jax
import jax.numpy as jnp
from jax import lax
from jax.experimental import pallas as pl
from jax.experimental.pallas import tpu as pltpu
from jax.sharding import PartitionSpec as P

D = 1280
HDIM = 64
SEG = 64
SEGS = 40
TREE_TOK = 2560


EPSILON = 1e-06
HIGHEST = lax.Precision.HIGHEST
SPREAD = ("shard", "ctx")


def unit_rows(values):
    return values * lax.rsqrt(jnp.sum(values * values, axis=-1, keepdims=True) + EPSILON)


def contract_rows(former, latter):
    return lax.dot_general(
        former, latter, (((0,), (0,)), ((), ())), preferred_element_type=jnp.float32
    )


def contract_cols(former, latter):
    return lax.dot_general(
        former, latter, (((1,), (1,)), ((), ())), preferred_element_type=jnp.float32
    )


def mix_rows(residual, branch, mixing):
    return unit_rows(residual + mixing * (unit_rows(branch) - residual))


def swap(value, axis, bit):
    size = lax.axis_size(axis)
    return lax.ppermute(value, axis, [(place, place ^ bit) for place in range(size)])


def add_low(former, latter):
    return (former.astype(jnp.float32) + latter.astype(jnp.float32)).astype(jnp.bfloat16)


def butterfly(value, axes):
    for axis in axes:
        bit = 1
        while bit < lax.axis_size(axis):
            value = value + swap(value, axis, bit)
            bit *= 2
    return value


def group_order(axis):
    size = lax.axis_size(axis)
    places = jnp.arange(size, dtype=jnp.int32)
    return places ^ lax.axis_index(axis) if size == 4 else places


def group_gather(own_block, axis):
    if lax.axis_size(axis) != 4:
        return [lax.all_gather(own_block, axis, axis=0, tiled=True)]
    across = swap(own_block, axis, 2)
    beside = swap(own_block, axis, 1)
    return [own_block, beside, across, swap(across, axis, 1)]


def group_scatter(pieces, axis):
    if lax.axis_size(axis) != 4:
        return [lax.psum_scatter(pieces[0], axis, scatter_dimension=0, tiled=True)]
    own, beside, across, far = pieces
    far = swap(far, axis, 1)
    beside = swap(beside, axis, 1)
    return [own, beside, swap(add_low(across, far), axis, 2)]


def total_wide(parts):
    return sum(part.astype(jnp.float32) for part in parts)


def in_plane():
    return (lax.axis_size("shard"), lax.axis_size("ctx"), lax.axis_size("tp")) == (2, 4, 4)


def hop(value, bits):
    return lax.ppermute(value, SPREAD, [(place, place ^ bits) for place in range(8)])


def hidden_gather(own_block):
    if not in_plane():
        return group_gather(own_block, "tp")
    return [own_block] + [hop(own_block, bits) for bits in (2, 4, 6)]


def hidden_scatter(pieces):
    if not in_plane():
        return group_scatter(pieces, "tp")
    return [pieces[0]] + [hop(piece, bits) for piece, bits in zip(pieces[1:], (2, 4, 6))]


def hidden_shards(w_up, w_gate, w_down):
    if not in_plane():
        return jnp.stack([w_up.T, w_gate.T, w_down])
    rows, hidden = w_up.shape
    part = hidden // 8
    packed = jnp.stack(
        [
            w_up.reshape(rows, 8, part).transpose(1, 2, 0),
            w_gate.reshape(rows, 8, part).transpose(1, 2, 0),
            w_down.reshape(8, part, rows),
        ],
        axis=1,
    )
    packed = lax.all_to_all(packed, SPREAD, 0, 0)
    return packed.transpose(1, 2, 0, 3).reshape(3, part, 8 * rows)


def hidden_weights(matrices):
    if not in_plane():
        return [
            [lax.all_gather(matrices[place], SPREAD, axis=1, tiled=True)] for place in range(3)
        ]
    lines = [lax.all_gather(matrices[place], "tp", axis=0, tiled=True) for place in range(3)]
    return [[line, swap(line, "ctx", 1)] for line in lines]


def hidden_scales(*scales):
    if not in_plane():
        return scales
    part = scales[0].shape[0] // 8
    first = lax.axis_index(SPREAD) * part
    own = jnp.stack([lax.dynamic_slice_in_dim(scale, first, part) for scale in scales])
    line = jnp.concatenate(group_gather(own[None], "tp"), axis=0)
    line = jnp.take(line, group_order("tp"), axis=0)
    both = jnp.concatenate([line, swap(line, "ctx", 1)], axis=0)
    return tuple(both[:, place].reshape(-1) for place in range(len(scales)))


def core_sums(products):
    if not in_plane():
        return products
    half = products[0].shape[0] // 2
    return [add_low(product[:half], swap(product[half:], "ctx", 1)) for product in products]


def hidden_weight_grads(lines):
    if not in_plane():
        return [
            lax.psum_scatter(line, SPREAD, scatter_dimension=1, tiled=True).astype(jnp.float32)
            for line in lines
        ]
    sums = [lax.psum_scatter(line, "tp", scatter_dimension=0, tiled=True) for line in lines]
    part, width = sums[0].shape
    packed = jnp.stack([total.reshape(part, 8, width // 8).transpose(1, 0, 2) for total in sums], 1)
    packed = lax.all_to_all(packed, SPREAD, 0, 0).astype(jnp.float32)
    return [packed[:, place].reshape(8 * part, width // 8) for place in range(3)]


def hidden_scale_grads(sums):
    if not in_plane():
        return butterfly(sums, SPREAD)
    count, hidden = sums.shape
    parts = sums.reshape(count, 2, 4, hidden // 8)
    line = butterfly(parts[:, 0] + swap(parts[:, 1], "ctx", 1), ("tp",))
    line = lax.dynamic_index_in_dim(line, lax.axis_index("tp"), 1, keepdims=False)
    blank = jnp.zeros((count, 8, hidden // 8), jnp.float32)
    place = lax.axis_index(SPREAD)
    spread_out = lax.dynamic_update_slice_in_dim(blank, line[:, None], place, 1)
    return butterfly(spread_out, SPREAD).reshape(count, hidden)


def owner_scatter(product_low):
    if lax.axis_size("ctx") != 4 or lax.axis_size("shard") != 2:
        return lax.psum_scatter(
            product_low, ("shard", "ctx"), scatter_dimension=0, tiled=True
        ).astype(jnp.float32)
    place = lax.axis_index("ctx")
    core, along = place % 2, place // 2
    plane = lax.axis_index("shard")
    rows, width = product_low.shape
    blocks = product_low.reshape(2, 2, 2, rows // 8, width)

    def pick(value, index, axis):
        return lax.dynamic_index_in_dim(value, index, axis, keepdims=False)

    blocks = add_low(pick(blocks, core, 2), swap(pick(blocks, 1 - core, 2), "ctx", 1))
    former, latter = blocks[..., : width // 2], blocks[..., width // 2 :]
    former_in = swap(pick(former, 1 - along, 1), "ctx", 2)
    latter_in = swap(pick(latter, 1 - plane, 0), "shard", 1)
    former = add_low(pick(former, along, 1), former_in)
    latter = add_low(pick(latter, plane, 0), latter_in)
    former_in = swap(pick(former, 1 - plane, 0), "shard", 1)
    latter_in = swap(pick(latter, 1 - along, 0), "ctx", 2)
    return jnp.concatenate(
        [
            pick(former, plane, 0).astype(jnp.float32) + former_in.astype(jnp.float32),
            pick(latter, along, 0).astype(jnp.float32) + latter_in.astype(jnp.float32),
        ],
        axis=1,
    )


def row_labels(slots, group_size):
    tree_rows = group_size * lax.axis_size("ctx")
    chunk = group_size // lax.axis_size("tp")
    within = (group_order("tp")[:, None] * chunk + jnp.arange(chunk, dtype=jnp.int32)).reshape(-1)
    keys = (group_order("ctx")[:, None] * group_size + within[None, :]).reshape(-1)
    onehot = (keys[:, None] // SEG == jnp.arange(tree_rows // SEG, dtype=jnp.int32)[None, :])
    segment = jnp.sum(jnp.where(onehot, slots[None, :], 0), axis=1)
    offset = keys % SEG
    if lax.axis_size("ctx") != 4:
        first = lax.axis_index("ctx") * group_size
    else:
        first = 0
    return (
        lax.dynamic_slice_in_dim(segment, first, group_size),
        lax.dynamic_slice_in_dim(offset, first, group_size),
        segment,
        offset,
    )


LOG2_SCALE = math.sqrt(HDIM) * math.log2(math.e)
LANES = 128
KEY_TILE = 256


def copies(sources, targets, sems):
    moves = [
        pltpu.make_async_copy(source, target, sems.at[place])
        for place, (source, target) in enumerate(zip(sources, targets))
    ]
    for move in moves:
        move.start()
    return moves


def row_blocks(ref, count):
    rows = ref.shape[0] // count
    return [ref.at[pl.ds(place * rows, rows)] for place in range(count)]


ANYWHERE = pl.BlockSpec(memory_space=pl.ANY)


def half_kept(value, unit, axis):
    place = lax.broadcasted_iota(jnp.int32, value.shape, axis)
    inside = (place >= HDIM) if unit % 2 else (place < HDIM)
    return jnp.where(inside, value, jnp.zeros_like(value))


def seen_tile(hot_ref, side_ref):
    hot = hot_ref[...]
    strict = jnp.dot(hot, side_ref[0], preferred_element_type=jnp.float32)
    same = jnp.dot(hot, side_ref[1], preferred_element_type=jnp.float32)
    before = jnp.dot(hot, side_ref[2], preferred_element_type=jnp.float32)
    return (strict + same * before).astype(jnp.bfloat16)


def pair_of(unit):
    return slice(unit // 2 * LANES, unit // 2 * LANES + LANES)


def attend_body(count, query_ref, *refs):
    pieces, refs = refs[:count], refs[count:]
    (hot_ref, side_ref, weight_ref, out_ref, scale_ref), refs = refs[:5], refs[5:]
    outs, (tree_ref, turned_ref, sum_ref, sems) = refs[:-4], refs[-4:]
    heads = query_ref.shape[1] // HDIM
    step = pl.program_id(0)

    @pl.when(step == 0)
    def prepare():
        moves = copies(pieces, row_blocks(tree_ref, count), sems)
        turned = query_ref[...].astype(jnp.float32).T.astype(jnp.bfloat16)
        blank = jnp.zeros((HDIM, turned.shape[1]), jnp.bfloat16)
        for head in range(heads):
            own = turned[head * HDIM : (head + 1) * HDIM]
            halves = [blank, own] if head % 2 else [own, blank]
            turned_ref[head] = jnp.concatenate(halves, axis=0)
        sum_ref[...] = jnp.zeros_like(sum_ref)
        for move in moves:
            move.wait()

    tree = tree_ref[pl.ds(step * KEY_TILE, KEY_TILE)]
    values_turned = tree[:, heads * HDIM :].astype(jnp.float32).T.astype(jnp.bfloat16)
    seen = seen_tile(hot_ref, side_ref)
    ones = jnp.ones((sum_ref.shape[1] - HDIM, tree.shape[0]), jnp.bfloat16)
    for head in range(heads):
        scores = jnp.dot(tree[:, pair_of(head)], turned_ref[head], preferred_element_type=jnp.float32)
        lifted = jnp.exp2(scores * LOG2_SCALE).astype(jnp.bfloat16) * seen
        own = jnp.concatenate([values_turned[head * HDIM : (head + 1) * HDIM], ones], axis=0)
        sum_ref[head] += jnp.dot(own, lifted, preferred_element_type=jnp.float32)

    @pl.when(step == pl.num_programs(0) - 1)
    def finish():
        parts = []
        for head in range(heads):
            inverse = 1.0 / sum_ref[head, HDIM : HDIM + 1]
            scale_ref[head : head + 1] = inverse
            parts.append(sum_ref[head, :HDIM] * inverse)
        low = jnp.concatenate(parts, axis=0).T.astype(jnp.bfloat16)
        out_ref[...] = low
        width = low.shape[1]
        rows = low.shape[0] // len(outs)
        for place, out in enumerate(outs):
            out[...] = contract_cols(
                low[place * rows : (place + 1) * rows], weight_ref[:, 3 * width :]
            ).astype(jnp.bfloat16)


def attend(query, pieces, hot, side, weight, count_out):
    rows, features = query.shape
    wide = weight.shape[0]
    count, width = len(pieces), pieces[0].shape[1]
    keys = pieces[0].shape[0] * count
    heads = features // HDIM
    whole = lambda step: (0, 0)
    return pl.pallas_call(
        lambda *refs: attend_body(count, *refs),
        grid=(keys // KEY_TILE,),
        in_specs=[pl.BlockSpec((rows, features), whole)]
        + [ANYWHERE] * count
        + [
            pl.BlockSpec((KEY_TILE, LANES), lambda step: (step, 0)),
            pl.BlockSpec((3, LANES, rows), lambda step: (0, 0, 0)),
            pl.BlockSpec(weight.shape, whole),
        ],
        out_specs=[
            pl.BlockSpec((rows, features), whole),
            pl.BlockSpec((8, rows), whole),
        ]
        + [pl.BlockSpec((rows // count_out, wide), whole)] * count_out,
        out_shape=[
            jax.ShapeDtypeStruct((rows, features), jnp.bfloat16),
            jax.ShapeDtypeStruct((8, rows), jnp.float32),
        ]
        + [jax.ShapeDtypeStruct((rows // count_out, wide), jnp.bfloat16)] * count_out,
        scratch_shapes=[
            pltpu.VMEM((keys, width), jnp.bfloat16),
            pltpu.VMEM((heads, LANES, rows), jnp.bfloat16),
            pltpu.VMEM((heads, HDIM + 16, rows), jnp.float32),
            pltpu.SemaphoreType.DMA((count,)),
        ],
        compiler_params=pltpu.CompilerParams(vmem_limit_bytes=48 << 20),
        name="attend",
    )(query, *pieces, hot, side, weight)


def attend_grad_body(count, tops, query_ref, heads_ref, *refs):
    pieces, refs = refs[:count], refs[count:]
    top_refs, refs = refs[:tops], refs[tops:]
    (hot_ref, side_ref, scale_ref, weight_ref, query_out), refs = refs[:5], refs[5:]
    outs, refs = refs[:count], refs[count:]
    group_out, tree_ref, tree_out, group, turned_ref, plain_ref, delta_ref, sum_ref = refs[:8]
    sems, top_sems, group_sem = refs[8:]
    heads = heads_ref.shape[1] // HDIM
    units = 2 * heads
    step = pl.program_id(0)

    @pl.when(step == 0)
    def prepare():
        moves = copies(pieces, row_blocks(tree_ref, count), sems)
        gathers = copies(top_refs, row_blocks(group, tops), top_sems)
        for gather in gathers:
            gather.wait()
        keep = pltpu.make_async_copy(group, group_out, group_sem)
        keep.start()
        features = query_ref.shape[1]
        upstream = jnp.dot(
            group[...], weight_ref[:, 3 * features :], preferred_element_type=jnp.float32
        )
        both = jnp.concatenate([query_ref[...], upstream.astype(jnp.bfloat16)], axis=1)
        turned = both.astype(jnp.float32).T
        kept = heads_ref[...].astype(jnp.float32).T
        blank = jnp.zeros((HDIM, turned.shape[1]), jnp.bfloat16)
        for unit in range(units):
            own = turned[unit * HDIM : (unit + 1) * HDIM].astype(jnp.bfloat16)
            halves = [blank, own] if unit % 2 else [own, blank]
            turned_ref[unit] = jnp.concatenate(halves, axis=0)
            plain_ref[unit] = half_kept(both[:, pair_of(unit)], unit, 1)
        for head in range(heads):
            rows = slice(head * HDIM, (head + 1) * HDIM)
            pulled = turned[(heads + head) * HDIM : (heads + head + 1) * HDIM]
            delta_ref[head : head + 1] = jnp.sum(kept[rows] * pulled, axis=0, keepdims=True)
        sum_ref[...] = jnp.zeros_like(sum_ref)
        for move in moves:
            move.wait()
        keep.wait()

    here = pl.ds(step * KEY_TILE, KEY_TILE)
    tree = tree_ref[here]
    keys_turned = tree[:, : heads * HDIM].astype(jnp.float32).T.astype(jnp.bfloat16)
    seen = seen_tile(hot_ref, side_ref)
    weights, slopes = [], []
    for head in range(heads):
        scores = jnp.dot(tree[:, pair_of(head)], turned_ref[head], preferred_element_type=jnp.float32)
        weight = jnp.exp2(scores * LOG2_SCALE) * scale_ref[head : head + 1]
        pull = jnp.dot(
            tree[:, pair_of(heads + head)], turned_ref[heads + head], preferred_element_type=jnp.float32
        )
        slope = (weight * (pull - delta_ref[head : head + 1])).astype(jnp.bfloat16) * seen
        rows = slice(head * HDIM, (head + 1) * HDIM)
        sum_ref[rows] += jnp.dot(keys_turned[rows], slope, preferred_element_type=jnp.float32)
        weights.append(weight.astype(jnp.bfloat16) * seen)
        slopes.append(slope)
    terms = slopes + weights
    score_scale = math.sqrt(HDIM)
    for pair in range(heads):
        total = 0.0
        for unit in (2 * pair, 2 * pair + 1):
            part = jnp.dot(terms[unit], plain_ref[unit], preferred_element_type=jnp.float32)
            total = total + (part * score_scale if unit < heads else part)
        tree_out[here, pair * LANES : (pair + 1) * LANES] = total.astype(jnp.bfloat16)

    @pl.when(step == pl.num_programs(0) - 1)
    def finish():
        moves = copies(row_blocks(tree_out, count), outs, sems)
        query_out[...] = sum_ref[...].T * score_scale
        for move in moves:
            move.wait()


def attend_grad(query, tops, outs, pieces, hot, side, scale, weight):
    rows, features = query.shape
    wide = weight.shape[0]
    count, width = len(pieces), pieces[0].shape[1]
    keys = pieces[0].shape[0] * count
    heads = features // HDIM
    whole = lambda step: (0, 0)
    return pl.pallas_call(
        lambda *refs: attend_grad_body(count, len(tops), *refs),
        grid=(keys // KEY_TILE,),
        in_specs=[pl.BlockSpec((rows, features), whole)] * 2
        + [ANYWHERE] * (count + len(tops))
        + [
            pl.BlockSpec((KEY_TILE, LANES), lambda step: (step, 0)),
            pl.BlockSpec((3, LANES, rows), lambda step: (0, 0, 0)),
            pl.BlockSpec((8, rows), whole),
            pl.BlockSpec(weight.shape, whole),
        ],
        out_specs=[pl.BlockSpec((rows, features), whole)] + [ANYWHERE] * (count + 1),
        out_shape=[jax.ShapeDtypeStruct((rows, features), jnp.float32)]
        + [jax.ShapeDtypeStruct(piece.shape, jnp.bfloat16) for piece in pieces]
        + [jax.ShapeDtypeStruct((rows, wide), jnp.bfloat16)],
        scratch_shapes=[
            pltpu.VMEM((keys, width), jnp.bfloat16),
            pltpu.VMEM((keys, width), jnp.bfloat16),
            pltpu.VMEM((rows, wide), jnp.bfloat16),
            pltpu.VMEM((2 * heads, LANES, rows), jnp.bfloat16),
            pltpu.VMEM((2 * heads, rows, LANES), jnp.bfloat16),
            pltpu.VMEM((8, rows), jnp.float32),
            pltpu.VMEM((features, rows), jnp.float32),
            pltpu.SemaphoreType.DMA((count,)),
            pltpu.SemaphoreType.DMA((len(tops),)),
            pltpu.SemaphoreType.DMA,
        ],
        compiler_params=pltpu.CompilerParams(vmem_limit_bytes=56 << 20),
        name="attend_grad",
    )(query, outs, *pieces, *tops, hot, side, scale, weight)


def seen_factors(reachable, seg_query, off_query, segment, offset):
    segs = reachable.shape[0]
    labels = jnp.arange(LANES, dtype=jnp.int32)
    key_mark = jnp.where(labels < HDIM, segment[:, None], offset[:, None] + HDIM)
    hot = (key_mark == labels[None, :]).astype(jnp.bfloat16)
    query_hot = (labels[:, None] == seg_query[None, :]).astype(jnp.float32)
    wide = jnp.zeros((LANES, LANES), jnp.float32).at[:segs, :segs].set(reachable.T - jnp.eye(segs, dtype=jnp.float32))
    strict = jnp.dot(wide, query_hot, preferred_element_type=jnp.float32)
    same = query_hot
    before = ((labels[:, None] >= HDIM) & (labels[:, None] - HDIM <= off_query[None, :])).astype(jnp.float32)
    return hot, jnp.stack([strict, same, before]).astype(jnp.bfloat16)


def head_marks(features):
    row = lax.broadcasted_iota(jnp.int32, (features, LANES), 0) // HDIM
    column = lax.broadcasted_iota(jnp.int32, (features, LANES), 1)
    return (row == column).astype(jnp.float32)


def over_heads(values, marks):
    sums = jnp.dot(values, marks, precision=HIGHEST, preferred_element_type=jnp.float32)
    return sums, lambda heads: lax.dot_general(
        heads, marks, (((1,), (1,)), ((), ())), precision=HIGHEST, preferred_element_type=jnp.float32
    )


def project_body(count, *refs):
    pieces, refs = refs[:count], refs[count:]
    weight_ref, scale_ref, query_out, tree_out, raw_out, group_out, group, sems, group_sem = refs
    both = raw_out.shape[1]
    features = both // 2
    step = pl.program_id(0)
    keep = pltpu.make_async_copy(group, group_out, group_sem)

    @pl.when(step == 0)
    def assemble():
        moves = copies(pieces, row_blocks(group, count), sems)
        for move in moves:
            move.wait()
        keep.start()

    @pl.when(step == pl.num_programs(0) - 1)
    def kept():
        keep.wait()

    tile = query_out.shape[0]
    product = jnp.dot(
        group[pl.ds(step * tile, tile)], weight_ref[:, : 3 * features], preferred_element_type=jnp.float32
    )
    raw = product[:, :both]
    sums, spread_heads = over_heads(raw * raw, head_marks(both))
    unit = raw * spread_heads(lax.rsqrt(sums + EPSILON))
    scaled = (unit * scale_ref[...]).astype(jnp.bfloat16)
    raw_out[...] = raw
    query_out[...] = scaled[:, :features]
    tree_out[...] = jnp.concatenate(
        [scaled[:, features:], product[:, both:].astype(jnp.bfloat16)], axis=1
    )


def project(pieces, weight, scale):
    count, width = len(pieces), pieces[0].shape[1]
    rows = pieces[0].shape[0] * count
    features = weight.shape[1] // 4
    tile = rows // 4
    whole = lambda step: (0, 0)
    block = lambda columns: pl.BlockSpec((tile, columns), lambda step: (step, 0))
    return pl.pallas_call(
        lambda *refs: project_body(count, *refs),
        grid=(4,),
        in_specs=[ANYWHERE] * count
        + [
            pl.BlockSpec(weight.shape, whole),
            pl.BlockSpec((1, 2 * features), whole),
        ],
        out_specs=[block(features), block(2 * features), block(2 * features), ANYWHERE],
        out_shape=[
            jax.ShapeDtypeStruct((rows, features), jnp.bfloat16),
            jax.ShapeDtypeStruct((rows, 2 * features), jnp.bfloat16),
            jax.ShapeDtypeStruct((rows, 2 * features), jnp.float32),
            jax.ShapeDtypeStruct((rows, width), jnp.bfloat16),
        ],
        scratch_shapes=[
            pltpu.VMEM((rows, width), jnp.bfloat16),
            pltpu.SemaphoreType.DMA((count,)),
            pltpu.SemaphoreType.DMA,
        ],
        compiler_params=pltpu.CompilerParams(vmem_limit_bytes=40 << 20),
        name="project",
    )(*pieces, weight, scale)


def project_grad_body(count, query_ref, *refs):
    tree_refs, refs = refs[:count], refs[count:]
    (raw_ref, weight_ref, scale_ref, low_out, scale_out), part_outs = refs[:5], refs[5:]
    step = pl.program_id(0)
    both = raw_ref.shape[1]
    features = both // 2
    tree = sum(ref[...].astype(jnp.float32) for ref in tree_refs)
    upstream = jnp.concatenate([query_ref[...], tree[:, :features]], axis=1)
    raw = raw_ref[...]
    marks = head_marks(both)
    sums, spread_heads = over_heads(raw * raw, marks)
    inverse = spread_heads(lax.rsqrt(sums + EPSILON))
    unit = raw * inverse
    scale_out[...] = jnp.sum(upstream * unit, axis=0, keepdims=True)[None]
    pulled = upstream * scale_ref[...]
    inner = spread_heads(over_heads(unit * pulled, marks)[0])
    grads = inverse * (pulled - unit * inner)
    low = jnp.concatenate([grads, tree[:, features:]], axis=1).astype(jnp.bfloat16)
    low_out[...] = low
    part = contract_cols(low, weight_ref[:, : 3 * features]).astype(jnp.bfloat16)
    for place, part_out in enumerate(part_outs):

        @pl.when((step == place) | (len(part_outs) == 1))
        def store():
            part_out[...] = part


def project_grad(query_grad, tree_parts, raw, weight, scale, count_out):
    rows, both = raw.shape
    width = weight.shape[0]
    features = both // 2
    tile = rows // 4
    whole = lambda step: (0, 0)
    block = lambda columns: pl.BlockSpec((tile, columns), lambda step: (step, 0))
    return pl.pallas_call(
        lambda *refs: project_grad_body(len(tree_parts), *refs),
        grid=(4,),
        in_specs=[block(features)]
        + [block(both) for part in tree_parts]
        + [block(both), pl.BlockSpec(weight.shape, whole), pl.BlockSpec((1, both), whole)],
        out_specs=[
            block(3 * features),
            pl.BlockSpec((1, 1, both), lambda step: (step, 0, 0)),
        ]
        + ([block(width)] if count_out == 1 else [pl.BlockSpec((tile, width), whole)] * 4),
        out_shape=[
            jax.ShapeDtypeStruct((rows, 3 * features), jnp.bfloat16),
            jax.ShapeDtypeStruct((4, 1, both), jnp.float32),
        ]
        + [jax.ShapeDtypeStruct((rows // count_out, width), jnp.bfloat16)] * count_out,
        compiler_params=pltpu.CompilerParams(vmem_limit_bytes=40 << 20),
        name="project_grad",
    )(query_grad, *tree_parts, raw, weight, scale)


def gated(up, gate, scale_up, scale_gate):
    raw = gate * (scale_gate * math.sqrt(D))
    curve = 1.0 / (1.0 + jnp.exp(-raw))
    return raw, curve, raw * curve, up * scale_up


def hidden_body(count, halves, *refs):
    pieces, refs = refs[:count], refs[count:]
    weights, refs = refs[: 3 * halves], refs[3 * halves :]
    scale_ref, refs = refs[0], refs[1:]
    outs, refs = refs[:count], refs[count:]
    group_out, up_out, gate_out, mixed_out, group, matrices, total, sems, out_sem = refs
    half = up_out.shape[1] // halves
    moves = copies(pieces, row_blocks(group, count), sems)
    loads = [
        pltpu.make_async_copy(weights[place], matrices.at[place], sems.at[count + place])
        for place in range(3 * halves)
    ]
    for load in loads:
        load.start()
    for move in moves:
        move.wait()
    keep = pltpu.make_async_copy(group, group_out, out_sem)
    keep.start()
    for place in range(halves):
        columns = slice(place * half, (place + 1) * half)
        for matrix in range(3):
            loads[matrix * halves + place].wait()
        tokens = group[...]
        up = contract_cols(tokens, matrices[place])
        gate = contract_cols(tokens, matrices[halves + place])
        up_out[:, columns] = up.astype(jnp.bfloat16)
        gate_out[:, columns] = gate.astype(jnp.bfloat16)
        raw, curve, silu, scaled = gated(up, gate, scale_ref[0:1, columns], scale_ref[1:2, columns])
        mixed = (scaled * silu).astype(jnp.bfloat16)
        mixed_out[:, columns] = mixed
        part = jnp.dot(mixed, matrices[2 * halves + place], preferred_element_type=jnp.float32)
        total[...] = part if place == 0 else total[...] + part
    rows = group.shape[0] // count
    for place in range(count):
        outs[place][...] = total[place * rows : (place + 1) * rows].astype(jnp.bfloat16)
    keep.wait()


def hidden_forward(pieces, weights, scales):
    count, halves = len(pieces), len(weights[0])
    rows, width = pieces[0].shape[0] * count, pieces[0].shape[1]
    half = weights[0][0].shape[0]
    hidden = half * halves
    low = lambda columns: jax.ShapeDtypeStruct((rows, columns), jnp.bfloat16)
    vmem = pl.BlockSpec(memory_space=pltpu.VMEM)
    return pl.pallas_call(
        lambda *refs: hidden_body(count, halves, *refs),
        in_specs=[ANYWHERE] * (count + 3 * halves) + [vmem],
        out_specs=[vmem] * count + [ANYWHERE] + [vmem] * 3,
        out_shape=[jax.ShapeDtypeStruct(piece.shape, jnp.bfloat16) for piece in pieces]
        + [low(width), low(hidden), low(hidden), low(hidden)],
        scratch_shapes=[
            pltpu.VMEM((rows, width), jnp.bfloat16),
            pltpu.VMEM((3 * halves, half, width), jnp.bfloat16),
            pltpu.VMEM((rows, width), jnp.float32),
            pltpu.SemaphoreType.DMA((count + 3 * halves,)),
            pltpu.SemaphoreType.DMA,
        ],
        compiler_params=pltpu.CompilerParams(vmem_limit_bytes=52 << 20),
        name="hidden",
    )(*pieces, *[matrix for parts in weights for matrix in parts], jnp.stack(scales))


def hidden_grad_body(count, halves, *refs):
    pieces, refs = refs[:count], refs[count:]
    weights, refs = refs[: 3 * halves], refs[3 * halves :]
    scale_ref, up_ref, gate_ref = refs[:3]
    outs, refs = refs[3 : 3 + count], refs[3 + count :]
    group_out, up_out, gate_out, scale_out, group, matrices, total, sems, out_sem = refs
    half = up_out.shape[1] // halves
    moves = copies(pieces, row_blocks(group, count), sems)
    loads = [
        pltpu.make_async_copy(weights[place], matrices.at[place], sems.at[count + place])
        for place in range(3 * halves)
    ]
    for load in loads:
        load.start()
    for move in moves:
        move.wait()
    keep = pltpu.make_async_copy(group, group_out, out_sem)
    keep.start()
    for place in range(halves):
        columns = slice(place * half, (place + 1) * half)
        for matrix in range(3):
            loads[matrix * halves + place].wait()
        pulled = contract_cols(group[...], matrices[2 * halves + place])
        pulled = pulled.astype(jnp.bfloat16).astype(jnp.float32)
        up = up_ref[:, columns].astype(jnp.float32)
        gate = gate_ref[:, columns].astype(jnp.float32)
        scale_up, scale_gate = scale_ref[0:1, columns], scale_ref[1:2, columns]
        raw, curve, silu, scaled = gated(up, gate, scale_up, scale_gate)
        curved = pulled * silu
        up_low = (curved * scale_up).astype(jnp.bfloat16)
        bent = pulled * scaled * (curve * (1.0 + raw * (1.0 - curve)))
        gate_low = (bent * (scale_gate * math.sqrt(D))).astype(jnp.bfloat16)
        scale_out[0:1, columns] = jnp.sum(curved * up, axis=0, keepdims=True)
        scale_out[1:2, columns] = jnp.sum(bent * gate, axis=0, keepdims=True) * math.sqrt(D)
        up_out[:, columns] = up_low
        gate_out[:, columns] = gate_low
        part = jnp.dot(up_low, matrices[place], preferred_element_type=jnp.float32)
        part = part + jnp.dot(gate_low, matrices[halves + place], preferred_element_type=jnp.float32)
        total[...] = part if place == 0 else total[...] + part
    rows = group.shape[0] // count
    for place in range(count):
        outs[place][...] = total[place * rows : (place + 1) * rows].astype(jnp.bfloat16)
    keep.wait()


def hidden_backward(pieces, weights, scales, up, gate):
    count, halves = len(pieces), len(weights[0])
    rows, width = pieces[0].shape[0] * count, pieces[0].shape[1]
    half = weights[0][0].shape[0]
    hidden = half * halves
    low = lambda columns: jax.ShapeDtypeStruct((rows, columns), jnp.bfloat16)
    vmem = pl.BlockSpec(memory_space=pltpu.VMEM)
    return pl.pallas_call(
        lambda *refs: hidden_grad_body(count, halves, *refs),
        in_specs=[ANYWHERE] * (count + 3 * halves) + [vmem] * 3,
        out_specs=[vmem] * count + [ANYWHERE] + [vmem] * 3,
        out_shape=[jax.ShapeDtypeStruct(piece.shape, jnp.bfloat16) for piece in pieces]
        + [low(width), low(hidden), low(hidden), jax.ShapeDtypeStruct((8, hidden), jnp.float32)],
        scratch_shapes=[
            pltpu.VMEM((rows, width), jnp.bfloat16),
            pltpu.VMEM((3 * halves, half, width), jnp.bfloat16),
            pltpu.VMEM((rows, width), jnp.float32),
            pltpu.SemaphoreType.DMA((count + 3 * halves,)),
            pltpu.SemaphoreType.DMA,
        ],
        compiler_params=pltpu.CompilerParams(vmem_limit_bytes=56 << 20),
        name="hidden_grad",
    )(*pieces, *[matrix for parts in weights for matrix in parts], jnp.stack(scales), up, gate)


def visibility(parents, slots, group_size):
    labels = jnp.arange(SEGS, dtype=jnp.int32)
    linked = (parents[:, None] == labels[None, :]).astype(jnp.float32)
    reachable = jnp.maximum(linked, jnp.eye(SEGS, dtype=jnp.float32))
    for doubling in range(SEGS.bit_length()):
        reachable = jnp.minimum(jnp.dot(reachable, reachable, precision=HIGHEST), 1.0)
    return seen_factors(reachable, *row_labels(slots, group_size))


def forward_attention(packed, scale_both, pieces, parents, slots):
    rows = pieces[0].shape[0] * len(pieces)
    seen = visibility(parents, slots, rows)
    queries, tree_own, raw, group = project(pieces, packed, scale_both)
    tree = group_gather(tree_own, "ctx")
    heads_low, inverse, *parts = attend(queries, tree, *seen, packed, len(pieces))
    return group_scatter(parts, "tp"), (group, seen, queries, tree, raw, heads_low, inverse)


def feed_forward(weights, scales, alphas, tokens_own, branch_parts, cotangent_own):
    alpha_attn, alpha_mlp = alphas
    tokens_wide = tokens_own.astype(jnp.float32)
    branch_one = total_wide(branch_parts)
    hidden_one, pull_in = jax.vjp(mix_rows, tokens_wide, branch_one, alpha_attn)
    pieces = hidden_gather(hidden_one.astype(jnp.bfloat16))
    count = len(pieces)
    outs = hidden_forward(pieces, weights, scales)
    hidden_group, up, gate, mixed = outs[count:]
    branch_two = total_wide(hidden_scatter(outs[:count]))
    output_wide, pull_out = jax.vjp(mix_rows, hidden_one, branch_two, alpha_mlp)
    upstream = cotangent_own.astype(jnp.float32)
    hidden_direct, branch_two_grad, grad_alpha_mlp = pull_out(upstream)
    pieces = hidden_gather(branch_two_grad.astype(jnp.bfloat16))
    outs = hidden_backward(pieces, weights, scales, up, gate)
    top_group, up_low, gate_low, scale_sums = outs[count:]
    hidden_grad = hidden_direct + total_wide(hidden_scatter(outs[:count]))
    tokens_direct, branch_one_grad, grad_alpha_attn = pull_in(hidden_grad)
    tops = group_gather(branch_one_grad.astype(jnp.bfloat16), "tp")
    factors = ((up_low, hidden_group), (gate_low, hidden_group), (mixed, top_group))
    sums = (jnp.concatenate([grad_alpha_attn, grad_alpha_mlp]), scale_sums[:2])
    return output_wide.astype(jnp.bfloat16), tokens_direct, tops, factors, sums


def backward_attention(packed, scale_both, kept, tops, tokens_direct):
    group, seen, queries, tree, raw, heads_low, inverse = kept
    query_grads, *rest = attend_grad(
        queries, tops, heads_low, tree, *seen, inverse, packed
    )
    tree_grads, top_group = rest[:-1], rest[-1]
    tree_parts = group_scatter(tree_grads, "ctx")
    low, scale_sums, *parts = project_grad(
        query_grads, tree_parts, raw, packed, scale_both, len(tops)
    )
    grad_tokens = tokens_direct + total_wide(group_scatter(parts, "tp"))
    features = queries.shape[1]
    scale_sum = jnp.sum(scale_sums, axis=(0, 1))
    return grad_tokens, ((group, low), (top_group, heads_low)), (
        scale_sum[:features] + scale_sum[features:]
    )


def joint_product(factors):
    formers, latters = zip(*factors)
    return contract_rows(jnp.concatenate(formers, axis=0), jnp.concatenate(latters, axis=0))


def per_device(
    tokens,
    parents,
    slot_segment,
    w_query,
    w_key,
    w_value,
    w_attn_out,
    w_up,
    w_gate,
    w_down,
    alpha_attn,
    alpha_mlp,
    scale_qk,
    scale_up,
    scale_gate,
    cotangent,
):
    width = tokens.shape[-1]
    micros = range(tokens.shape[0])
    groups = [group_gather(tokens[m, 0], "tp") for m in micros]
    packed = lax.all_gather(
        jnp.concatenate([w_query, w_key, w_value, w_attn_out.T], axis=1),
        SPREAD,
        axis=0,
        tiled=True,
    )
    shards, groups = lax.optimization_barrier((hidden_shards(w_up, w_gate, w_down), groups))
    weights = hidden_weights(shards)
    scales = hidden_scales(scale_up, scale_gate)
    scale_both = jnp.concatenate([scale_qk, scale_qk])[None]
    front = [
        forward_attention(packed, scale_both, groups[m], parents[m, 0], slot_segment[m, 0])
        for m in micros
    ]
    mid = [
        feed_forward(
            weights, scales, (alpha_attn, alpha_mlp), tokens[m, 0], front[m][0], cotangent[m, 0]
        )
        for m in micros
    ]
    lines = core_sums(
        [
            joint_product([mid[m][3][place] for m in micros]).astype(jnp.bfloat16)
            for place in range(3)
        ]
    )
    tops = [mid[m][2] for m in micros]
    lines, tops[-1] = lax.optimization_barrier((lines, tops[-1]))
    grad_u, grad_g, grad_d = hidden_weight_grads(lines)
    back = [
        backward_attention(packed, scale_both, front[m][1], tops[m], mid[m][1]) for m in micros
    ]
    grad_attention = owner_scatter(
        jnp.concatenate(
            [joint_product([back[m][1][place] for m in micros]) for place in range(2)], axis=1
        ).astype(jnp.bfloat16)
    )
    grad_q, grad_k, grad_v, grad_o = jnp.split(grad_attention, 4, axis=1)
    sum_qk = butterfly(sum(back[m][2] for m in micros), SPREAD)
    alphas = butterfly(sum(mid[m][4][0] for m in micros), SPREAD + ("tp",))
    sum_up, sum_gate = hidden_scale_grads(sum(mid[m][4][1] for m in micros))
    return (
        jnp.stack([mid[m][0] for m in micros])[:, None],
        jnp.stack([back[m][0] for m in micros])[:, None],
        grad_q,
        grad_k,
        grad_v,
        grad_o.T,
        grad_u.T,
        grad_g.T,
        grad_d,
        alphas[:width],
        alphas[width:],
        sum_qk,
        sum_up,
        sum_gate,
    )


def solution(mesh):
    return jax.shard_map(
        per_device,
        mesh=mesh,
        in_specs=(
            P(None, "shard", ("ctx", "tp"), None),
            P(None, "shard", None),
            P(None, "shard", None),
            P(("shard", "ctx"), "tp"),
            P(("shard", "ctx"), "tp"),
            P(("shard", "ctx"), "tp"),
            P("tp", ("shard", "ctx")),
            P(("shard", "ctx"), "tp"),
            P(("shard", "ctx"), "tp"),
            P("tp", ("shard", "ctx")),
            P(),
            P(),
            P("tp"),
            P("tp"),
            P("tp"),
            P(None, "shard", ("ctx", "tp"), None),
        ),
        out_specs=(
            P(None, "shard", ("ctx", "tp"), None),
            P(None, "shard", ("ctx", "tp"), None),
            P(("shard", "ctx"), "tp"),
            P(("shard", "ctx"), "tp"),
            P(("shard", "ctx"), "tp"),
            P("tp", ("shard", "ctx")),
            P(("shard", "ctx"), "tp"),
            P(("shard", "ctx"), "tp"),
            P("tp", ("shard", "ctx")),
            P(),
            P(),
            P("tp"),
            P("tp"),
            P("tp"),
        ),
        check_vma=False,
    )
```

```python
import math

import jax
import jax.numpy as jnp
from jax import lax
from jax.experimental import pallas as pl
from jax.experimental.pallas import tpu as pltpu
from jax.sharding import PartitionSpec as P

D = 1280
HDIM = 64
SEG = 64
SEGS = 40
TREE_TOK = 2560


EPSILON = 1e-06
HIGHEST = lax.Precision.HIGHEST
SPREAD = ("shard", "ctx")


def unit_rows(values):
    return values * lax.rsqrt(jnp.sum(values * values, axis=-1, keepdims=True) + EPSILON)


def contract_rows(former, latter):
    return lax.dot_general(
        former, latter, (((0,), (0,)), ((), ())), preferred_element_type=jnp.float32
    )


def contract_cols(former, latter):
    return lax.dot_general(
        former, latter, (((1,), (1,)), ((), ())), preferred_element_type=jnp.float32
    )


def mix_rows(residual, branch, mixing):
    return unit_rows(residual + mixing * (unit_rows(branch) - residual))


def swap(value, axis, bit):
    size = lax.axis_size(axis)
    return lax.ppermute(value, axis, [(place, place ^ bit) for place in range(size)])


def after(value, *others):
    for other in others:
        value = value + (other[(slice(0, 1),) * other.ndim].reshape(()) * 0).astype(value.dtype)
    return value


def add_low(former, latter):
    return (former.astype(jnp.float32) + latter.astype(jnp.float32)).astype(jnp.bfloat16)


def butterfly(value, axes):
    for axis in axes:
        bit = 1
        while bit < lax.axis_size(axis):
            value = value + swap(value, axis, bit)
            bit *= 2
    return value


def group_order(axis):
    size = lax.axis_size(axis)
    places = jnp.arange(size, dtype=jnp.int32)
    return places ^ lax.axis_index(axis) if size == 4 else places


def group_gather(own_block, axis):
    if lax.axis_size(axis) != 4:
        return [lax.all_gather(own_block, axis, axis=0, tiled=True)]
    across = swap(own_block, axis, 2)
    beside = swap(own_block, axis, 1)
    return [own_block, beside, across, swap(across, axis, 1)]


def group_scatter(pieces, axis):
    if lax.axis_size(axis) != 4:
        return [lax.psum_scatter(pieces[0], axis, scatter_dimension=0, tiled=True)]
    return [pieces[0]] + [swap(piece, axis, bits) for piece, bits in zip(pieces[1:], (1, 2, 3))]


def total_wide(parts):
    return sum(part.astype(jnp.float32) for part in parts)


def in_plane():
    return (lax.axis_size("shard"), lax.axis_size("ctx"), lax.axis_size("tp")) == (2, 4, 4)


def hop(value, bits):
    return lax.ppermute(value, SPREAD, [(place, place ^ bits) for place in range(8)])


def hidden_gather(own_block):
    if not in_plane():
        return group_gather(own_block, "tp")
    return [own_block] + [hop(own_block, bits) for bits in (2, 4, 6)]


def hidden_scatter(pieces):
    if not in_plane():
        return group_scatter(pieces, "tp")
    return [pieces[0]] + [hop(piece, bits) for piece, bits in zip(pieces[1:], (2, 4, 6))]


def hidden_shards(w_up, w_gate, w_down):
    if not in_plane():
        return jnp.stack([w_up.T, w_gate.T, w_down])
    rows, hidden = w_up.shape
    part = hidden // 8
    packed = jnp.stack(
        [
            w_up.reshape(rows, 8, part).transpose(1, 2, 0),
            w_gate.reshape(rows, 8, part).transpose(1, 2, 0),
            w_down.reshape(8, part, rows),
        ],
        axis=1,
    )
    packed = lax.all_to_all(packed, SPREAD, 0, 0)
    return packed.transpose(1, 2, 0, 3).reshape(3, part, 8 * rows)


def hidden_weights(matrices):
    if not in_plane():
        return [
            [lax.all_gather(matrices[place], SPREAD, axis=1, tiled=True)] for place in range(3)
        ]
    lines = [lax.all_gather(matrices[place], "tp", axis=0, tiled=True) for place in range(3)]
    return [[line, swap(line, "ctx", 1)] for line in lines]


def hidden_scales(*scales):
    if not in_plane():
        return scales
    part = scales[0].shape[0] // 8
    first = lax.axis_index(SPREAD) * part
    own = jnp.stack([lax.dynamic_slice_in_dim(scale, first, part) for scale in scales])
    line = jnp.concatenate(group_gather(own[None], "tp"), axis=0)
    line = jnp.take(line, group_order("tp"), axis=0)
    both = jnp.concatenate([line, swap(line, "ctx", 1)], axis=0)
    return tuple(both[:, place].reshape(-1) for place in range(len(scales)))


def core_sums(products):
    if not in_plane():
        return products
    half = products[0].shape[0] // 2
    return [add_low(product[:half], swap(product[half:], "ctx", 1)) for product in products]


def hidden_line_sums(lines):
    if not in_plane():
        return lines
    return [lax.psum_scatter(line, "tp", scatter_dimension=0, tiled=True) for line in lines]


def hidden_spread(sums):
    if not in_plane():
        return jnp.stack(
            [lax.psum_scatter(total, SPREAD, scatter_dimension=1, tiled=True) for total in sums]
        )
    part, width = sums[0].shape
    packed = jnp.stack([total.reshape(part, 8, width // 8).transpose(1, 0, 2) for total in sums], 1)
    return lax.all_to_all(packed, SPREAD, 0, 0)


def hidden_weight_grads(spread_sums):
    wide = spread_sums.astype(jnp.float32)
    if not in_plane():
        return [wide[place] for place in range(3)]
    return [wide[:, place].reshape(-1, wide.shape[-1]) for place in range(3)]


def vector_sums(alphas, hidden_sums):
    count, hidden = hidden_sums.shape
    if not in_plane():
        return jnp.concatenate([butterfly(alphas, ("tp",)), hidden_sums.reshape(-1)])
    parts = hidden_sums.reshape(count, 2, 4, hidden // 8)
    line = (parts[:, 0] + swap(parts[:, 1], "ctx", 1)).reshape(-1)
    width = alphas.shape[0]
    both = butterfly(jnp.concatenate([alphas, line]), ("tp",))
    line = both[width:].reshape(count, 4, hidden // 8)
    line = lax.dynamic_index_in_dim(line, lax.axis_index("tp"), 1, keepdims=True)
    blank = jnp.zeros((count, 8, hidden // 8), jnp.float32)
    placed = lax.dynamic_update_slice_in_dim(blank, line, lax.axis_index(SPREAD), 1)
    return jnp.concatenate([both[:width], placed.reshape(-1)])


def owner_scatter(product_low):
    count = lax.axis_size(SPREAD)
    rows, width = product_low.shape
    blocks = lax.all_to_all(product_low.reshape(count, rows // count, width), SPREAD, 0, 0)
    return jnp.sum(blocks.astype(jnp.float32), axis=0)


def row_labels(slots, group_size):
    tree_rows = group_size * lax.axis_size("ctx")
    chunk = group_size // lax.axis_size("tp")
    within = (group_order("tp")[:, None] * chunk + jnp.arange(chunk, dtype=jnp.int32)).reshape(-1)
    keys = (group_order("ctx")[:, None] * group_size + within[None, :]).reshape(-1)
    onehot = (keys[:, None] // SEG == jnp.arange(tree_rows // SEG, dtype=jnp.int32)[None, :])
    segment = jnp.sum(jnp.where(onehot, slots[None, :], 0), axis=1)
    offset = keys % SEG
    if lax.axis_size("ctx") != 4:
        first = lax.axis_index("ctx") * group_size
    else:
        first = 0
    return (
        lax.dynamic_slice_in_dim(segment, first, group_size),
        lax.dynamic_slice_in_dim(offset, first, group_size),
        segment,
        offset,
    )


LOG2_SCALE = math.sqrt(HDIM) * math.log2(math.e)
LANES = 128
KEY_TILE = 256


def copies(sources, targets, sems):
    moves = [
        pltpu.make_async_copy(source, target, sems.at[place])
        for place, (source, target) in enumerate(zip(sources, targets))
    ]
    for move in moves:
        move.start()
    return moves


def row_blocks(ref, count):
    rows = ref.shape[0] // count
    return [ref.at[pl.ds(place * rows, rows)] for place in range(count)]


def core_time(micros):
    return pl.CostEstimate(flops=int(micros * 1.15e9), transcendentals=0, bytes_accessed=1 << 20)


ANYWHERE = pl.BlockSpec(memory_space=pl.ANY)


def half_kept(value, unit, axis):
    place = lax.broadcasted_iota(jnp.int32, value.shape, axis)
    inside = (place >= HDIM) if unit % 2 else (place < HDIM)
    return jnp.where(inside, value, jnp.zeros_like(value))


def seen_tile(hot_ref, side_ref):
    hot = hot_ref[...]
    strict = jnp.dot(hot, side_ref[0], preferred_element_type=jnp.float32)
    same = jnp.dot(hot, side_ref[1], preferred_element_type=jnp.float32)
    before = jnp.dot(hot, side_ref[2], preferred_element_type=jnp.float32)
    return (strict + same * before).astype(jnp.bfloat16)


def pair_of(unit):
    return slice(unit // 2 * LANES, unit // 2 * LANES + LANES)


def attend_body(count, query_ref, *refs):
    pieces, refs = refs[:count], refs[count:]
    (hot_ref, side_ref, weight_ref, out_ref, scale_ref), refs = refs[:5], refs[5:]
    outs, (tree_ref, turned_ref, sum_ref, sems) = refs[:-4], refs[-4:]
    heads = query_ref.shape[1] // HDIM
    step = pl.program_id(0)

    @pl.when(step == 0)
    def prepare():
        moves = copies(pieces, row_blocks(tree_ref, count), sems)
        turned = query_ref[...].astype(jnp.float32).T.astype(jnp.bfloat16)
        blank = jnp.zeros((HDIM, turned.shape[1]), jnp.bfloat16)
        for head in range(heads):
            own = turned[head * HDIM : (head + 1) * HDIM]
            halves = [blank, own] if head % 2 else [own, blank]
            turned_ref[head] = jnp.concatenate(halves, axis=0)
        sum_ref[...] = jnp.zeros_like(sum_ref)
        for move in moves:
            move.wait()

    tree = tree_ref[pl.ds(step * KEY_TILE, KEY_TILE)]
    values_turned = tree[:, heads * HDIM :].astype(jnp.float32).T.astype(jnp.bfloat16)
    seen = seen_tile(hot_ref, side_ref)
    ones = jnp.ones((sum_ref.shape[1] - HDIM, tree.shape[0]), jnp.bfloat16)
    for head in range(heads):
        scores = jnp.dot(tree[:, pair_of(head)], turned_ref[head], preferred_element_type=jnp.float32)
        lifted = jnp.exp2(scores * LOG2_SCALE).astype(jnp.bfloat16) * seen
        own = jnp.concatenate([values_turned[head * HDIM : (head + 1) * HDIM], ones], axis=0)
        sum_ref[head] += jnp.dot(own, lifted, preferred_element_type=jnp.float32)

    @pl.when(step == pl.num_programs(0) - 1)
    def finish():
        parts = []
        for head in range(heads):
            inverse = 1.0 / sum_ref[head, HDIM : HDIM + 1]
            scale_ref[head : head + 1] = inverse
            parts.append(sum_ref[head, :HDIM] * inverse)
        low = jnp.concatenate(parts, axis=0).T.astype(jnp.bfloat16)
        out_ref[...] = low
        width = low.shape[1]
        rows = low.shape[0] // len(outs)
        for place, out in enumerate(outs):
            out[...] = contract_cols(
                low[place * rows : (place + 1) * rows], weight_ref[:, 3 * width :]
            ).astype(jnp.bfloat16)


def attend(query, pieces, hot, side, weight, count_out):
    rows, features = query.shape
    wide = weight.shape[0]
    count, width = len(pieces), pieces[0].shape[1]
    keys = pieces[0].shape[0] * count
    heads = features // HDIM
    whole = lambda step: (0, 0)
    return pl.pallas_call(
        lambda *refs: attend_body(count, *refs),
        grid=(keys // KEY_TILE,),
        in_specs=[pl.BlockSpec((rows, features), whole)]
        + [ANYWHERE] * count
        + [
            pl.BlockSpec((KEY_TILE, LANES), lambda step: (step, 0)),
            pl.BlockSpec((3, LANES, rows), lambda step: (0, 0, 0)),
            pl.BlockSpec(weight.shape, whole),
        ],
        out_specs=[
            pl.BlockSpec((rows, features), whole),
            pl.BlockSpec((8, rows), whole),
        ]
        + [pl.BlockSpec((rows // count_out, wide), whole)] * count_out,
        out_shape=[
            jax.ShapeDtypeStruct((rows, features), jnp.bfloat16),
            jax.ShapeDtypeStruct((8, rows), jnp.float32),
        ]
        + [jax.ShapeDtypeStruct((rows // count_out, wide), jnp.bfloat16)] * count_out,
        scratch_shapes=[
            pltpu.VMEM((keys, width), jnp.bfloat16),
            pltpu.VMEM((heads, LANES, rows), jnp.bfloat16),
            pltpu.VMEM((heads, HDIM + 16, rows), jnp.float32),
            pltpu.SemaphoreType.DMA((count,)),
        ],
        compiler_params=pltpu.CompilerParams(vmem_limit_bytes=48 << 20),
        cost_estimate=core_time(23),
        name="attend",
    )(query, *pieces, hot, side, weight)


def attend_grad_body(count, tops, query_ref, heads_ref, *refs):
    pieces, refs = refs[:count], refs[count:]
    top_refs, refs = refs[:tops], refs[tops:]
    (hot_ref, side_ref, scale_ref, weight_ref, query_out), refs = refs[:5], refs[5:]
    outs, refs = refs[:count], refs[count:]
    group_out, tree_ref, tree_out, group, turned_ref, plain_ref, delta_ref, sum_ref = refs[:8]
    sems, top_sems, group_sem = refs[8:]
    heads = heads_ref.shape[1] // HDIM
    units = 2 * heads
    step = pl.program_id(0)

    @pl.when(step == 0)
    def prepare():
        moves = copies(pieces, row_blocks(tree_ref, count), sems)
        gathers = copies(top_refs, row_blocks(group, tops), top_sems)
        for gather in gathers:
            gather.wait()
        keep = pltpu.make_async_copy(group, group_out, group_sem)
        keep.start()
        features = query_ref.shape[1]
        upstream = jnp.dot(
            group[...], weight_ref[:, 3 * features :], preferred_element_type=jnp.float32
        )
        both = jnp.concatenate([query_ref[...], upstream.astype(jnp.bfloat16)], axis=1)
        turned = both.astype(jnp.float32).T
        kept = heads_ref[...].astype(jnp.float32).T
        blank = jnp.zeros((HDIM, turned.shape[1]), jnp.bfloat16)
        for unit in range(units):
            own = turned[unit * HDIM : (unit + 1) * HDIM].astype(jnp.bfloat16)
            halves = [blank, own] if unit % 2 else [own, blank]
            turned_ref[unit] = jnp.concatenate(halves, axis=0)
            plain_ref[unit] = half_kept(both[:, pair_of(unit)], unit, 1)
        for head in range(heads):
            rows = slice(head * HDIM, (head + 1) * HDIM)
            pulled = turned[(heads + head) * HDIM : (heads + head + 1) * HDIM]
            delta_ref[head : head + 1] = jnp.sum(kept[rows] * pulled, axis=0, keepdims=True)
        sum_ref[...] = jnp.zeros_like(sum_ref)
        for move in moves:
            move.wait()
        keep.wait()

    here = pl.ds(step * KEY_TILE, KEY_TILE)
    tree = tree_ref[here]
    keys_turned = tree[:, : heads * HDIM].astype(jnp.float32).T.astype(jnp.bfloat16)
    seen = seen_tile(hot_ref, side_ref)
    weights, slopes = [], []
    for head in range(heads):
        scores = jnp.dot(tree[:, pair_of(head)], turned_ref[head], preferred_element_type=jnp.float32)
        weight = jnp.exp2(scores * LOG2_SCALE) * scale_ref[head : head + 1]
        pull = jnp.dot(
            tree[:, pair_of(heads + head)], turned_ref[heads + head], preferred_element_type=jnp.float32
        )
        slope = (weight * (pull - delta_ref[head : head + 1])).astype(jnp.bfloat16) * seen
        rows = slice(head * HDIM, (head + 1) * HDIM)
        sum_ref[rows] += jnp.dot(keys_turned[rows], slope, preferred_element_type=jnp.float32)
        weights.append(weight.astype(jnp.bfloat16) * seen)
        slopes.append(slope)
    terms = slopes + weights
    score_scale = math.sqrt(HDIM)
    for pair in range(heads):
        total = 0.0
        for unit in (2 * pair, 2 * pair + 1):
            part = jnp.dot(terms[unit], plain_ref[unit], preferred_element_type=jnp.float32)
            total = total + (part * score_scale if unit < heads else part)
        tree_out[here, pair * LANES : (pair + 1) * LANES] = total.astype(jnp.bfloat16)

    @pl.when(step == pl.num_programs(0) - 1)
    def finish():
        moves = copies(row_blocks(tree_out, count), outs, sems)
        query_out[...] = sum_ref[...].T * score_scale
        for move in moves:
            move.wait()


def attend_grad(query, tops, outs, pieces, hot, side, scale, weight):
    rows, features = query.shape
    wide = weight.shape[0]
    count, width = len(pieces), pieces[0].shape[1]
    keys = pieces[0].shape[0] * count
    heads = features // HDIM
    whole = lambda step: (0, 0)
    return pl.pallas_call(
        lambda *refs: attend_grad_body(count, len(tops), *refs),
        grid=(keys // KEY_TILE,),
        in_specs=[pl.BlockSpec((rows, features), whole)] * 2
        + [ANYWHERE] * (count + len(tops))
        + [
            pl.BlockSpec((KEY_TILE, LANES), lambda step: (step, 0)),
            pl.BlockSpec((3, LANES, rows), lambda step: (0, 0, 0)),
            pl.BlockSpec((8, rows), whole),
            pl.BlockSpec(weight.shape, whole),
        ],
        out_specs=[pl.BlockSpec((rows, features), whole)] + [ANYWHERE] * (count + 1),
        out_shape=[jax.ShapeDtypeStruct((rows, features), jnp.float32)]
        + [jax.ShapeDtypeStruct(piece.shape, jnp.bfloat16) for piece in pieces]
        + [jax.ShapeDtypeStruct((rows, wide), jnp.bfloat16)],
        scratch_shapes=[
            pltpu.VMEM((keys, width), jnp.bfloat16),
            pltpu.VMEM((keys, width), jnp.bfloat16),
            pltpu.VMEM((rows, wide), jnp.bfloat16),
            pltpu.VMEM((2 * heads, LANES, rows), jnp.bfloat16),
            pltpu.VMEM((2 * heads, rows, LANES), jnp.bfloat16),
            pltpu.VMEM((8, rows), jnp.float32),
            pltpu.VMEM((features, rows), jnp.float32),
            pltpu.SemaphoreType.DMA((count,)),
            pltpu.SemaphoreType.DMA((len(tops),)),
            pltpu.SemaphoreType.DMA,
        ],
        compiler_params=pltpu.CompilerParams(vmem_limit_bytes=56 << 20),
        cost_estimate=core_time(38),
        name="attend_grad",
    )(query, outs, *pieces, *tops, hot, side, scale, weight)


def seen_factors(reachable, seg_query, off_query, segment, offset):
    segs = reachable.shape[0]
    labels = jnp.arange(LANES, dtype=jnp.int32)
    key_mark = jnp.where(labels < HDIM, segment[:, None], offset[:, None] + HDIM)
    hot = (key_mark == labels[None, :]).astype(jnp.bfloat16)
    query_hot = (labels[:, None] == seg_query[None, :]).astype(jnp.float32)
    wide = jnp.zeros((LANES, LANES), jnp.float32).at[:segs, :segs].set(reachable.T - jnp.eye(segs, dtype=jnp.float32))
    strict = jnp.dot(wide, query_hot, preferred_element_type=jnp.float32)
    same = query_hot
    before = ((labels[:, None] >= HDIM) & (labels[:, None] - HDIM <= off_query[None, :])).astype(jnp.float32)
    return hot, jnp.stack([strict, same, before]).astype(jnp.bfloat16)


def head_marks(features):
    row = lax.broadcasted_iota(jnp.int32, (features, LANES), 0) // HDIM
    column = lax.broadcasted_iota(jnp.int32, (features, LANES), 1)
    return (row == column).astype(jnp.float32)


def over_heads(values, marks):
    sums = jnp.dot(values, marks, precision=HIGHEST, preferred_element_type=jnp.float32)
    return sums, lambda heads: lax.dot_general(
        heads, marks, (((1,), (1,)), ((), ())), precision=HIGHEST, preferred_element_type=jnp.float32
    )


def project_body(count, *refs):
    pieces, refs = refs[:count], refs[count:]
    weight_ref, scale_ref, query_out, tree_out, raw_out, group_out, group, sems, group_sem = refs
    both = raw_out.shape[1]
    features = both // 2
    step = pl.program_id(0)
    keep = pltpu.make_async_copy(group, group_out, group_sem)

    @pl.when(step == 0)
    def assemble():
        moves = copies(pieces, row_blocks(group, count), sems)
        for move in moves:
            move.wait()
        keep.start()

    @pl.when(step == pl.num_programs(0) - 1)
    def kept():
        keep.wait()

    tile = query_out.shape[0]
    product = jnp.dot(
        group[pl.ds(step * tile, tile)], weight_ref[:, : 3 * features], preferred_element_type=jnp.float32
    )
    raw = product[:, :both]
    sums, spread_heads = over_heads(raw * raw, head_marks(both))
    unit = raw * spread_heads(lax.rsqrt(sums + EPSILON))
    scaled = (unit * scale_ref[...]).astype(jnp.bfloat16)
    raw_out[...] = raw
    query_out[...] = scaled[:, :features]
    tree_out[...] = jnp.concatenate(
        [scaled[:, features:], product[:, both:].astype(jnp.bfloat16)], axis=1
    )


def project(pieces, weight, scale):
    count, width = len(pieces), pieces[0].shape[1]
    rows = pieces[0].shape[0] * count
    features = weight.shape[1] // 4
    tile = rows // 4
    whole = lambda step: (0, 0)
    block = lambda columns: pl.BlockSpec((tile, columns), lambda step: (step, 0))
    return pl.pallas_call(
        lambda *refs: project_body(count, *refs),
        grid=(4,),
        in_specs=[ANYWHERE] * count
        + [
            pl.BlockSpec(weight.shape, whole),
            pl.BlockSpec((1, 2 * features), whole),
        ],
        out_specs=[block(features), block(2 * features), block(2 * features), ANYWHERE],
        out_shape=[
            jax.ShapeDtypeStruct((rows, features), jnp.bfloat16),
            jax.ShapeDtypeStruct((rows, 2 * features), jnp.bfloat16),
            jax.ShapeDtypeStruct((rows, 2 * features), jnp.float32),
            jax.ShapeDtypeStruct((rows, width), jnp.bfloat16),
        ],
        scratch_shapes=[
            pltpu.VMEM((rows, width), jnp.bfloat16),
            pltpu.SemaphoreType.DMA((count,)),
            pltpu.SemaphoreType.DMA,
        ],
        compiler_params=pltpu.CompilerParams(vmem_limit_bytes=40 << 20),
        cost_estimate=core_time(9),
        name="project",
    )(*pieces, weight, scale)


def project_grad_body(count, query_ref, *refs):
    tree_refs, refs = refs[:count], refs[count:]
    (raw_ref, weight_ref, scale_ref, low_out, scale_out), part_outs = refs[:5], refs[5:]
    step = pl.program_id(0)
    both = raw_ref.shape[1]
    features = both // 2
    tree = sum(ref[...].astype(jnp.float32) for ref in tree_refs)
    upstream = jnp.concatenate([query_ref[...], tree[:, :features]], axis=1)
    raw = raw_ref[...]
    marks = head_marks(both)
    sums, spread_heads = over_heads(raw * raw, marks)
    inverse = spread_heads(lax.rsqrt(sums + EPSILON))
    unit = raw * inverse
    scale_out[...] = jnp.sum(upstream * unit, axis=0, keepdims=True)[None]
    pulled = upstream * scale_ref[...]
    inner = spread_heads(over_heads(unit * pulled, marks)[0])
    grads = inverse * (pulled - unit * inner)
    low = jnp.concatenate([grads, tree[:, features:]], axis=1).astype(jnp.bfloat16)
    low_out[...] = low
    part = contract_cols(low, weight_ref[:, : 3 * features]).astype(jnp.bfloat16)
    for place, part_out in enumerate(part_outs):

        @pl.when((step == place) | (len(part_outs) == 1))
        def store():
            part_out[...] = part


def project_grad(query_grad, tree_parts, raw, weight, scale, count_out):
    rows, both = raw.shape
    width = weight.shape[0]
    features = both // 2
    tile = rows // 4
    whole = lambda step: (0, 0)
    block = lambda columns: pl.BlockSpec((tile, columns), lambda step: (step, 0))
    return pl.pallas_call(
        lambda *refs: project_grad_body(len(tree_parts), *refs),
        grid=(4,),
        in_specs=[block(features)]
        + [block(both) for part in tree_parts]
        + [block(both), pl.BlockSpec(weight.shape, whole), pl.BlockSpec((1, both), whole)],
        out_specs=[
            block(3 * features),
            pl.BlockSpec((1, 1, both), lambda step: (step, 0, 0)),
        ]
        + ([block(width)] if count_out == 1 else [pl.BlockSpec((tile, width), whole)] * 4),
        out_shape=[
            jax.ShapeDtypeStruct((rows, 3 * features), jnp.bfloat16),
            jax.ShapeDtypeStruct((4, 1, both), jnp.float32),
        ]
        + [jax.ShapeDtypeStruct((rows // count_out, width), jnp.bfloat16)] * count_out,
        compiler_params=pltpu.CompilerParams(vmem_limit_bytes=40 << 20),
        cost_estimate=core_time(14),
        name="project_grad",
    )(query_grad, *tree_parts, raw, weight, scale)


def gated(up, gate, scale_up, scale_gate):
    raw = gate * (scale_gate * math.sqrt(D))
    curve = 1.0 / (1.0 + jnp.exp(-raw))
    return raw, curve, raw * curve, up * scale_up


def hidden_body(count, halves, *refs):
    pieces, refs = refs[:count], refs[count:]
    weights, refs = refs[: 3 * halves], refs[3 * halves :]
    scale_ref, refs = refs[0], refs[1:]
    outs, refs = refs[:count], refs[count:]
    group_out, up_out, gate_out, mixed_out, group, matrices, total, sems, out_sem = refs
    half = up_out.shape[1] // halves
    moves = copies(pieces, row_blocks(group, count), sems)
    loads = [
        pltpu.make_async_copy(weights[place], matrices.at[place], sems.at[count + place])
        for place in range(3 * halves)
    ]
    for load in loads:
        load.start()
    for move in moves:
        move.wait()
    keep = pltpu.make_async_copy(group, group_out, out_sem)
    keep.start()
    for place in range(halves):
        columns = slice(place * half, (place + 1) * half)
        for matrix in range(3):
            loads[matrix * halves + place].wait()
        tokens = group[...]
        up = contract_cols(tokens, matrices[place])
        gate = contract_cols(tokens, matrices[halves + place])
        up_out[:, columns] = up.astype(jnp.bfloat16)
        gate_out[:, columns] = gate.astype(jnp.bfloat16)
        raw, curve, silu, scaled = gated(up, gate, scale_ref[0:1, columns], scale_ref[1:2, columns])
        mixed = (scaled * silu).astype(jnp.bfloat16)
        mixed_out[:, columns] = mixed
        part = jnp.dot(mixed, matrices[2 * halves + place], preferred_element_type=jnp.float32)
        total[...] = part if place == 0 else total[...] + part
    rows = group.shape[0] // count
    for place in range(count):
        outs[place][...] = total[place * rows : (place + 1) * rows].astype(jnp.bfloat16)
    keep.wait()


def hidden_forward(pieces, weights, scales):
    count, halves = len(pieces), len(weights[0])
    rows, width = pieces[0].shape[0] * count, pieces[0].shape[1]
    half = weights[0][0].shape[0]
    hidden = half * halves
    low = lambda columns: jax.ShapeDtypeStruct((rows, columns), jnp.bfloat16)
    vmem = pl.BlockSpec(memory_space=pltpu.VMEM)
    return pl.pallas_call(
        lambda *refs: hidden_body(count, halves, *refs),
        in_specs=[ANYWHERE] * (count + 3 * halves) + [vmem],
        out_specs=[vmem] * count + [ANYWHERE] + [vmem] * 3,
        out_shape=[jax.ShapeDtypeStruct(piece.shape, jnp.bfloat16) for piece in pieces]
        + [low(width), low(hidden), low(hidden), low(hidden)],
        scratch_shapes=[
            pltpu.VMEM((rows, width), jnp.bfloat16),
            pltpu.VMEM((3 * halves, half, width), jnp.bfloat16),
            pltpu.VMEM((rows, width), jnp.float32),
            pltpu.SemaphoreType.DMA((count + 3 * halves,)),
            pltpu.SemaphoreType.DMA,
        ],
        compiler_params=pltpu.CompilerParams(vmem_limit_bytes=52 << 20),
        cost_estimate=core_time(16),
        name="hidden",
    )(*pieces, *[matrix for parts in weights for matrix in parts], jnp.stack(scales))


def hidden_grad_body(count, halves, *refs):
    pieces, refs = refs[:count], refs[count:]
    weights, refs = refs[: 3 * halves], refs[3 * halves :]
    scale_ref, up_ref, gate_ref = refs[:3]
    outs, refs = refs[3 : 3 + count], refs[3 + count :]
    group_out, up_out, gate_out, scale_out, group, matrices, total, sems, out_sem = refs
    half = up_out.shape[1] // halves
    moves = copies(pieces, row_blocks(group, count), sems)
    loads = [
        pltpu.make_async_copy(weights[place], matrices.at[place], sems.at[count + place])
        for place in range(3 * halves)
    ]
    for load in loads:
        load.start()
    for move in moves:
        move.wait()
    keep = pltpu.make_async_copy(group, group_out, out_sem)
    keep.start()
    for place in range(halves):
        columns = slice(place * half, (place + 1) * half)
        for matrix in range(3):
            loads[matrix * halves + place].wait()
        pulled = contract_cols(group[...], matrices[2 * halves + place])
        pulled = pulled.astype(jnp.bfloat16).astype(jnp.float32)
        up = up_ref[:, columns].astype(jnp.float32)
        gate = gate_ref[:, columns].astype(jnp.float32)
        scale_up, scale_gate = scale_ref[0:1, columns], scale_ref[1:2, columns]
        raw, curve, silu, scaled = gated(up, gate, scale_up, scale_gate)
        curved = pulled * silu
        up_low = (curved * scale_up).astype(jnp.bfloat16)
        bent = pulled * scaled * (curve * (1.0 + raw * (1.0 - curve)))
        gate_low = (bent * (scale_gate * math.sqrt(D))).astype(jnp.bfloat16)
        scale_out[0:1, columns] = jnp.sum(curved * up, axis=0, keepdims=True)
        scale_out[1:2, columns] = jnp.sum(bent * gate, axis=0, keepdims=True) * math.sqrt(D)
        up_out[:, columns] = up_low
        gate_out[:, columns] = gate_low
        part = jnp.dot(up_low, matrices[place], preferred_element_type=jnp.float32)
        part = part + jnp.dot(gate_low, matrices[halves + place], preferred_element_type=jnp.float32)
        total[...] = part if place == 0 else total[...] + part
    rows = group.shape[0] // count
    for place in range(count):
        outs[place][...] = total[place * rows : (place + 1) * rows].astype(jnp.bfloat16)
    keep.wait()


def hidden_backward(pieces, weights, scales, up, gate):
    count, halves = len(pieces), len(weights[0])
    rows, width = pieces[0].shape[0] * count, pieces[0].shape[1]
    half = weights[0][0].shape[0]
    hidden = half * halves
    low = lambda columns: jax.ShapeDtypeStruct((rows, columns), jnp.bfloat16)
    vmem = pl.BlockSpec(memory_space=pltpu.VMEM)
    return pl.pallas_call(
        lambda *refs: hidden_grad_body(count, halves, *refs),
        in_specs=[ANYWHERE] * (count + 3 * halves) + [vmem] * 3,
        out_specs=[vmem] * count + [ANYWHERE] + [vmem] * 3,
        out_shape=[jax.ShapeDtypeStruct(piece.shape, jnp.bfloat16) for piece in pieces]
        + [low(width), low(hidden), low(hidden), jax.ShapeDtypeStruct((8, hidden), jnp.float32)],
        scratch_shapes=[
            pltpu.VMEM((rows, width), jnp.bfloat16),
            pltpu.VMEM((3 * halves, half, width), jnp.bfloat16),
            pltpu.VMEM((rows, width), jnp.float32),
            pltpu.SemaphoreType.DMA((count + 3 * halves,)),
            pltpu.SemaphoreType.DMA,
        ],
        compiler_params=pltpu.CompilerParams(vmem_limit_bytes=56 << 20),
        cost_estimate=core_time(19),
        name="hidden_grad",
    )(*pieces, *[matrix for parts in weights for matrix in parts], jnp.stack(scales), up, gate)


def visibility(parents, slots, group_size):
    labels = jnp.arange(SEGS, dtype=jnp.int32)
    linked = (parents[:, None] == labels[None, :]).astype(jnp.float32)
    reachable = jnp.maximum(linked, jnp.eye(SEGS, dtype=jnp.float32))
    for doubling in range(SEGS.bit_length()):
        reachable = jnp.minimum(jnp.dot(reachable, reachable, precision=HIGHEST), 1.0)
    return seen_factors(reachable, *row_labels(slots, group_size))


def forward_attention(packed, scale_both, pieces, parents, slots):
    rows = pieces[0].shape[0] * len(pieces)
    seen = visibility(parents, slots, rows)
    queries, tree_own, raw, group = project(pieces, packed, scale_both)
    tree = group_gather(tree_own, "ctx")
    heads_low, inverse, *parts = attend(queries, tree, *seen, packed, len(pieces))
    return group_scatter(parts, "tp"), (group, seen, queries, tree, raw, heads_low, inverse)


def feed_forward(weights, scales, alphas, tokens_own, branch_parts, cotangent_own):
    alpha_attn, alpha_mlp = alphas
    tokens_wide = tokens_own.astype(jnp.float32)
    branch_one = total_wide(branch_parts)
    hidden_one, pull_in = jax.vjp(mix_rows, tokens_wide, branch_one, alpha_attn)
    pieces = hidden_gather(hidden_one.astype(jnp.bfloat16))
    count = len(pieces)
    outs = hidden_forward(pieces, weights, scales)
    hidden_group, up, gate, mixed = outs[count:]
    branch_two = total_wide(hidden_scatter(outs[:count]))
    output_wide, pull_out = jax.vjp(mix_rows, hidden_one, branch_two, alpha_mlp)
    upstream = cotangent_own.astype(jnp.float32)
    hidden_direct, branch_two_grad, grad_alpha_mlp = pull_out(upstream)
    pieces = hidden_gather(branch_two_grad.astype(jnp.bfloat16))
    outs = hidden_backward(pieces, weights, scales, up, gate)
    top_group, up_low, gate_low, scale_sums = outs[count:]
    hidden_grad = hidden_direct + total_wide(hidden_scatter(outs[:count]))
    tokens_direct, branch_one_grad, grad_alpha_attn = pull_in(hidden_grad)
    tops = group_gather(branch_one_grad.astype(jnp.bfloat16), "tp")
    factors = ((up_low, hidden_group), (gate_low, hidden_group), (mixed, top_group))
    sums = (jnp.concatenate([grad_alpha_attn, grad_alpha_mlp]), scale_sums[:2])
    return output_wide.astype(jnp.bfloat16), tokens_direct, tops, factors, sums


def backward_attention(packed, scale_both, kept, tops, tokens_direct):
    group, seen, queries, tree, raw, heads_low, inverse = kept
    query_grads, *rest = attend_grad(
        queries, tops, heads_low, tree, *seen, inverse, packed
    )
    tree_grads, top_group = rest[:-1], rest[-1]
    tree_parts = group_scatter(tree_grads, "ctx")
    low, scale_sums, *parts = project_grad(
        query_grads, tree_parts, raw, packed, scale_both, len(tops)
    )
    grad_tokens = tokens_direct + total_wide(group_scatter(parts, "tp"))
    features = queries.shape[1]
    scale_sum = jnp.sum(scale_sums, axis=(0, 1))
    return grad_tokens, ((group, low), (top_group, heads_low)), (
        scale_sum[:features] + scale_sum[features:]
    )


def joint_product(factors):
    formers, latters = zip(*factors)
    return contract_rows(jnp.concatenate(formers, axis=0), jnp.concatenate(latters, axis=0))


def per_device(
    tokens,
    parents,
    slot_segment,
    w_query,
    w_key,
    w_value,
    w_attn_out,
    w_up,
    w_gate,
    w_down,
    alpha_attn,
    alpha_mlp,
    scale_qk,
    scale_up,
    scale_gate,
    cotangent,
):
    width = tokens.shape[-1]
    micros = range(tokens.shape[0])
    groups = [group_gather(tokens[m, 0], "tp") for m in micros]
    packed = lax.all_gather(
        jnp.concatenate([w_query, w_key, w_value, w_attn_out.T], axis=1),
        SPREAD,
        axis=0,
        tiled=True,
    )
    scales = hidden_scales(scale_up, scale_gate)
    scale_both = jnp.concatenate([scale_qk, scale_qk])[None]
    first = groups[0][-1]
    shards = hidden_shards(after(w_up, first), after(w_gate, first), after(w_down, first))
    weights = hidden_weights(shards)
    scale_early = after(scale_both, *scales)
    front = [
        forward_attention(packed, scale_early, groups[m], parents[m, 0], slot_segment[m, 0])
        for m in micros
    ]
    mid = [
        feed_forward(
            weights, scales, (alpha_attn, alpha_mlp), tokens[m, 0], front[m][0], cotangent[m, 0]
        )
        for m in micros
    ]
    lines = core_sums(
        [
            joint_product([mid[m][3][place] for m in micros]).astype(jnp.bfloat16)
            for place in range(3)
        ]
    )
    vectors = vector_sums(
        sum(mid[m][4][0] for m in micros), sum(mid[m][4][1] for m in micros)
    )
    line_sums = hidden_line_sums(lines)
    spread_sums = hidden_spread(line_sums)
    waits = [after(scale_both, *line_sums), after(scale_both, spread_sums)]
    back = [
        backward_attention(packed, waits[min(m, 1)], front[m][1], mid[m][2], mid[m][1])
        for m in micros
    ]
    grad_u, grad_g, grad_d = hidden_weight_grads(spread_sums)
    grad_attention = owner_scatter(
        jnp.concatenate(
            [joint_product([back[m][1][place] for m in micros]) for place in range(2)], axis=1
        ).astype(jnp.bfloat16)
    )
    grad_q, grad_k, grad_v, grad_o = jnp.split(grad_attention, 4, axis=1)
    sums = butterfly(jnp.concatenate([vectors, sum(back[m][2] for m in micros)]), SPREAD)
    sum_alphas, sum_hidden, sum_qk = jnp.split(sums, [2 * width, sums.shape[0] - scale_qk.shape[0]])
    sum_up, sum_gate = jnp.split(sum_hidden, 2)
    return (
        jnp.stack([mid[m][0] for m in micros])[:, None],
        jnp.stack([back[m][0] for m in micros])[:, None],
        grad_q,
        grad_k,
        grad_v,
        grad_o.T,
        grad_u.T,
        grad_g.T,
        grad_d,
        sum_alphas[:width],
        sum_alphas[width:],
        sum_qk,
        sum_up,
        sum_gate,
    )


def solution(mesh):
    return jax.shard_map(
        per_device,
        mesh=mesh,
        in_specs=(
            P(None, "shard", ("ctx", "tp"), None),
            P(None, "shard", None),
            P(None, "shard", None),
            P(("shard", "ctx"), "tp"),
            P(("shard", "ctx"), "tp"),
            P(("shard", "ctx"), "tp"),
            P("tp", ("shard", "ctx")),
            P(("shard", "ctx"), "tp"),
            P(("shard", "ctx"), "tp"),
            P("tp", ("shard", "ctx")),
            P(),
            P(),
            P("tp"),
            P("tp"),
            P("tp"),
            P(None, "shard", ("ctx", "tp"), None),
        ),
        out_specs=(
            P(None, "shard", ("ctx", "tp"), None),
            P(None, "shard", ("ctx", "tp"), None),
            P(("shard", "ctx"), "tp"),
            P(("shard", "ctx"), "tp"),
            P(("shard", "ctx"), "tp"),
            P("tp", ("shard", "ctx")),
            P(("shard", "ctx"), "tp"),
            P(("shard", "ctx"), "tp"),
            P("tp", ("shard", "ctx")),
            P(),
            P(),
            P("tp"),
            P("tp"),
            P("tp"),
        ),
        check_vma=False,
    )
```

```python
import math

import jax
import jax.numpy as jnp
from jax import lax
from jax.experimental import pallas as pl
from jax.experimental.pallas import tpu as pltpu
from jax.sharding import PartitionSpec as P

D = 1280
HDIM = 64
SEG = 64
SEGS = 40
TREE_TOK = 2560


EPSILON = 1e-06
HIGHEST = lax.Precision.HIGHEST
SPREAD = ("shard", "ctx")


def unit_rows(values):
    return values * lax.rsqrt(jnp.sum(values * values, axis=-1, keepdims=True) + EPSILON)


def contract_rows(former, latter):
    return lax.dot_general(
        former, latter, (((0,), (0,)), ((), ())), preferred_element_type=jnp.float32
    )


def contract_cols(former, latter):
    return lax.dot_general(
        former, latter, (((1,), (1,)), ((), ())), preferred_element_type=jnp.float32
    )


def mix_rows(residual, branch, mixing):
    return unit_rows(residual + mixing * (unit_rows(branch) - residual))


def swap(value, axis, bit):
    size = lax.axis_size(axis)
    return lax.ppermute(value, axis, [(place, place ^ bit) for place in range(size)])


def after(value, *others):
    for other in others:
        value = value + (other[(slice(0, 1),) * other.ndim].reshape(()) * 0).astype(value.dtype)
    return value


def add_low(former, latter):
    return (former.astype(jnp.float32) + latter.astype(jnp.float32)).astype(jnp.bfloat16)


def butterfly(value, axes):
    for axis in axes:
        bit = 1
        while bit < lax.axis_size(axis):
            value = value + swap(value, axis, bit)
            bit *= 2
    return value


def group_order(axis):
    size = lax.axis_size(axis)
    places = jnp.arange(size, dtype=jnp.int32)
    return places ^ lax.axis_index(axis) if size == 4 else places


def group_gather(own_block, axis, gates=None):
    if lax.axis_size(axis) != 4:
        return [lax.all_gather(own_block, axis, axis=0, tiled=True)]
    across = swap(own_block, axis, 2)
    beside = swap(own_block, axis, 1)
    source = across if gates is None else after(across, beside, *gates)
    return [own_block, beside, across, swap(source, axis, 1)]


def group_scatter(pieces, axis, hops=2):
    if lax.axis_size(axis) != 4:
        parts = [lax.psum_scatter(pieces[0], axis, scatter_dimension=0, tiled=True)]
        return parts, parts[0]
    own, beside, across, far = pieces
    if hops == 1:
        parts = [swap(piece, axis, bits) for piece, bits in zip(pieces[1:], (1, 2, 3))]
        return [own] + parts, parts[0]
    far = swap(far, axis, 1)
    across = swap(add_low(across, far), axis, 2)
    return [own, swap(after(beside, far), axis, 1), across], far


def total_wide(parts):
    return sum(part.astype(jnp.float32) for part in parts)


def in_plane():
    return (lax.axis_size("shard"), lax.axis_size("ctx"), lax.axis_size("tp")) == (2, 4, 4)


def hop(value, bits):
    return lax.ppermute(value, SPREAD, [(place, place ^ bits) for place in range(8)])


def hidden_gather(own_block):
    if not in_plane():
        return group_gather(own_block, "tp")
    return [own_block] + [hop(own_block, bits) for bits in (2, 4, 6)]


def hidden_scatter(pieces):
    if not in_plane():
        return group_scatter(pieces, "tp")[0]
    return [pieces[0]] + [hop(piece, bits) for piece, bits in zip(pieces[1:], (2, 4, 6))]


def hidden_blocks(w_up, w_gate, w_down):
    if not in_plane():
        return jnp.stack([w_up.T, w_gate.T, w_down])
    rows, hidden = w_up.shape
    part = hidden // 8
    packed = jnp.stack(
        [
            w_up.reshape(rows, 8, part).transpose(1, 2, 0),
            w_gate.reshape(rows, 8, part).transpose(1, 2, 0),
            w_down.reshape(8, part, rows),
        ],
        axis=1,
    )
    return lax.all_to_all(packed, SPREAD, 0, 0)


def hidden_shards(blocks):
    if not in_plane():
        return blocks
    rows = blocks.shape[2]
    return blocks.transpose(1, 2, 0, 3).reshape(3, rows, -1)


def hidden_weights(shards):
    if not in_plane():
        return [lax.all_gather(shards, SPREAD, axis=2, tiled=True)[None]]
    line = lax.all_gather(shards, "tp", axis=0)
    return [line, swap(line, "ctx", 1)]


def hidden_scales(*scales):
    if not in_plane():
        return scales
    part = scales[0].shape[0] // 8
    first = lax.axis_index(SPREAD) * part
    own = jnp.stack([lax.dynamic_slice_in_dim(scale, first, part) for scale in scales])
    line = jnp.concatenate(group_gather(own[None], "tp"), axis=0)
    line = jnp.take(line, group_order("tp"), axis=0)
    both = jnp.concatenate([line, swap(line, "ctx", 1)], axis=0)
    return tuple(both[:, place].reshape(-1) for place in range(len(scales)))


def core_sums(products):
    if not in_plane():
        return products
    half = products[0].shape[0] // 2
    return [add_low(product[:half], swap(product[half:], "ctx", 1)) for product in products]


def hidden_line_sums(lines):
    if not in_plane():
        return lines
    return [lax.psum_scatter(line, "tp", scatter_dimension=0, tiled=True) for line in lines]


def hidden_spread(sums):
    if not in_plane():
        return jnp.stack(
            [lax.psum_scatter(total, SPREAD, scatter_dimension=1, tiled=True) for total in sums]
        )
    part, width = sums[0].shape
    packed = jnp.stack([total.reshape(part, 8, width // 8).transpose(1, 0, 2) for total in sums], 1)
    return lax.all_to_all(packed, SPREAD, 0, 0)


def hidden_weight_grads(spread_sums):
    wide = spread_sums.astype(jnp.float32)
    if not in_plane():
        return [wide[place] for place in range(3)]
    return [wide[:, place].reshape(-1, wide.shape[-1]) for place in range(3)]


def vector_sums(alphas, hidden_sums):
    count, hidden = hidden_sums.shape
    if not in_plane():
        return jnp.concatenate([butterfly(alphas, ("tp",)), hidden_sums.reshape(-1)])
    parts = hidden_sums.reshape(count, 2, 4, hidden // 8)
    line = (parts[:, 0] + swap(parts[:, 1], "ctx", 1)).reshape(-1)
    width = alphas.shape[0]
    both = butterfly(jnp.concatenate([alphas, line]), ("tp",))
    line = both[width:].reshape(count, 4, hidden // 8)
    line = lax.dynamic_index_in_dim(line, lax.axis_index("tp"), 1, keepdims=True)
    blank = jnp.zeros((count, 8, hidden // 8), jnp.float32)
    placed = lax.dynamic_update_slice_in_dim(blank, line, lax.axis_index(SPREAD), 1)
    return jnp.concatenate([both[:width], placed.reshape(-1)])


def owner_scatter(product_low):
    if not in_plane():
        total = lax.psum_scatter(product_low, SPREAD, scatter_dimension=0, tiled=True)
        return total.astype(jnp.float32)
    place = lax.axis_index("ctx")
    core, along, plane = place % 2, place // 2, lax.axis_index("shard")
    rows, width = product_low.shape
    blocks = product_low.reshape(4, 2, rows // 8, width)

    def of_core(which):
        return lax.dynamic_index_in_dim(blocks, which, 1, keepdims=False)

    blocks = add_low(of_core(core), swap(of_core(1 - core), "ctx", 1))
    chip = plane * 2 + along

    def of_chip(bits):
        return lax.dynamic_index_in_dim(blocks, chip ^ bits, 0, keepdims=False)

    return total_wide([of_chip(0)] + [hop(of_chip(bits), 2 * bits) for bits in (1, 2, 3)])


def row_labels(slots, group_size):
    tree_rows = group_size * lax.axis_size("ctx")
    chunk = group_size // lax.axis_size("tp")
    within = (group_order("tp")[:, None] * chunk + jnp.arange(chunk, dtype=jnp.int32)).reshape(-1)
    keys = (group_order("ctx")[:, None] * group_size + within[None, :]).reshape(-1)
    onehot = (keys[:, None] // SEG == jnp.arange(tree_rows // SEG, dtype=jnp.int32)[None, :])
    segment = jnp.sum(jnp.where(onehot, slots[None, :], 0), axis=1)
    offset = keys % SEG
    if lax.axis_size("ctx") != 4:
        first = lax.axis_index("ctx") * group_size
    else:
        first = 0
    return (
        lax.dynamic_slice_in_dim(segment, first, group_size),
        lax.dynamic_slice_in_dim(offset, first, group_size),
        segment,
        offset,
    )


LOG2_SCALE = math.sqrt(HDIM) * math.log2(math.e)
LANES = 128
KEY_TILE = 256


def copies(sources, targets, sems):
    moves = [
        pltpu.make_async_copy(source, target, sems.at[place])
        for place, (source, target) in enumerate(zip(sources, targets))
    ]
    for move in moves:
        move.start()
    return moves


def row_blocks(ref, count):
    rows = ref.shape[0] // count
    return [ref.at[pl.ds(place * rows, rows)] for place in range(count)]


ANYWHERE = pl.BlockSpec(memory_space=pl.ANY)


def half_kept(value, unit, axis):
    place = lax.broadcasted_iota(jnp.int32, value.shape, axis)
    inside = (place >= HDIM) if unit % 2 else (place < HDIM)
    return jnp.where(inside, value, jnp.zeros_like(value))


def seen_tile(hot_ref, side_ref):
    hot = hot_ref[...]
    strict = jnp.dot(hot, side_ref[0], preferred_element_type=jnp.float32)
    same = jnp.dot(hot, side_ref[1], preferred_element_type=jnp.float32)
    before = jnp.dot(hot, side_ref[2], preferred_element_type=jnp.float32)
    return (strict + same * before).astype(jnp.bfloat16)


def pair_of(unit):
    return slice(unit // 2 * LANES, unit // 2 * LANES + LANES)


def attend_body(count, query_ref, *refs):
    pieces, refs = refs[:count], refs[count:]
    (hot_ref, side_ref, weight_ref, out_ref, scale_ref), refs = refs[:5], refs[5:]
    outs, (tree_ref, turned_ref, sum_ref, sems) = refs[:-4], refs[-4:]
    heads = query_ref.shape[1] // HDIM
    step = pl.program_id(0)

    @pl.when(step == 0)
    def prepare():
        moves = copies(pieces, row_blocks(tree_ref, count), sems)
        turned = query_ref[...].astype(jnp.float32).T.astype(jnp.bfloat16)
        blank = jnp.zeros((HDIM, turned.shape[1]), jnp.bfloat16)
        for head in range(heads):
            own = turned[head * HDIM : (head + 1) * HDIM]
            halves = [blank, own] if head % 2 else [own, blank]
            turned_ref[head] = jnp.concatenate(halves, axis=0)
        sum_ref[...] = jnp.zeros_like(sum_ref)
        for move in moves:
            move.wait()

    tree = tree_ref[pl.ds(step * KEY_TILE, KEY_TILE)]
    values_turned = tree[:, heads * HDIM :].astype(jnp.float32).T.astype(jnp.bfloat16)
    seen = seen_tile(hot_ref, side_ref)
    ones = jnp.ones((sum_ref.shape[1] - HDIM, tree.shape[0]), jnp.bfloat16)
    for head in range(heads):
        scores = jnp.dot(tree[:, pair_of(head)], turned_ref[head], preferred_element_type=jnp.float32)
        lifted = jnp.exp2(scores * LOG2_SCALE).astype(jnp.bfloat16) * seen
        own = jnp.concatenate([values_turned[head * HDIM : (head + 1) * HDIM], ones], axis=0)
        sum_ref[head] += jnp.dot(own, lifted, preferred_element_type=jnp.float32)

    @pl.when(step == pl.num_programs(0) - 1)
    def finish():
        parts = []
        for head in range(heads):
            inverse = 1.0 / sum_ref[head, HDIM : HDIM + 1]
            scale_ref[head : head + 1] = inverse
            parts.append(sum_ref[head, :HDIM] * inverse)
        low = jnp.concatenate(parts, axis=0).T.astype(jnp.bfloat16)
        out_ref[...] = low
        width = low.shape[1]
        rows = low.shape[0] // len(outs)
        for place, out in enumerate(outs):
            out[...] = contract_cols(
                low[place * rows : (place + 1) * rows], weight_ref[:, 3 * width :]
            ).astype(jnp.bfloat16)


def attend(query, pieces, hot, side, weight, count_out):
    rows, features = query.shape
    wide = weight.shape[0]
    count, width = len(pieces), pieces[0].shape[1]
    keys = pieces[0].shape[0] * count
    heads = features // HDIM
    whole = lambda step: (0, 0)
    return pl.pallas_call(
        lambda *refs: attend_body(count, *refs),
        grid=(keys // KEY_TILE,),
        in_specs=[pl.BlockSpec((rows, features), whole)]
        + [ANYWHERE] * count
        + [
            pl.BlockSpec((KEY_TILE, LANES), lambda step: (step, 0)),
            pl.BlockSpec((3, LANES, rows), lambda step: (0, 0, 0)),
            pl.BlockSpec(weight.shape, whole),
        ],
        out_specs=[
            pl.BlockSpec((rows, features), whole),
            pl.BlockSpec((8, rows), whole),
        ]
        + [pl.BlockSpec((rows // count_out, wide), whole)] * count_out,
        out_shape=[
            jax.ShapeDtypeStruct((rows, features), jnp.bfloat16),
            jax.ShapeDtypeStruct((8, rows), jnp.float32),
        ]
        + [jax.ShapeDtypeStruct((rows // count_out, wide), jnp.bfloat16)] * count_out,
        scratch_shapes=[
            pltpu.VMEM((keys, width), jnp.bfloat16),
            pltpu.VMEM((heads, LANES, rows), jnp.bfloat16),
            pltpu.VMEM((heads, HDIM + 16, rows), jnp.float32),
            pltpu.SemaphoreType.DMA((count,)),
        ],
        compiler_params=pltpu.CompilerParams(vmem_limit_bytes=48 << 20),
        name="attend",
    )(query, *pieces, hot, side, weight)


def attend_grad_body(count, tops, query_ref, heads_ref, *refs):
    pieces, refs = refs[:count], refs[count:]
    top_refs, refs = refs[:tops], refs[tops:]
    (hot_ref, side_ref, scale_ref, weight_ref, query_out), refs = refs[:5], refs[5:]
    outs, refs = refs[:count], refs[count:]
    group_out, tree_ref, tree_out, group, turned_ref, plain_ref, delta_ref, sum_ref = refs[:8]
    sems, top_sems, group_sem = refs[8:]
    heads = heads_ref.shape[1] // HDIM
    units = 2 * heads
    step = pl.program_id(0)

    @pl.when(step == 0)
    def prepare():
        moves = copies(pieces, row_blocks(tree_ref, count), sems)
        gathers = copies(top_refs, row_blocks(group, tops), top_sems)
        for gather in gathers:
            gather.wait()
        keep = pltpu.make_async_copy(group, group_out, group_sem)
        keep.start()
        features = query_ref.shape[1]
        upstream = jnp.dot(
            group[...], weight_ref[:, 3 * features :], preferred_element_type=jnp.float32
        )
        both = jnp.concatenate([query_ref[...], upstream.astype(jnp.bfloat16)], axis=1)
        turned = both.astype(jnp.float32).T
        kept = heads_ref[...].astype(jnp.float32).T
        blank = jnp.zeros((HDIM, turned.shape[1]), jnp.bfloat16)
        for unit in range(units):
            own = turned[unit * HDIM : (unit + 1) * HDIM].astype(jnp.bfloat16)
            halves = [blank, own] if unit % 2 else [own, blank]
            turned_ref[unit] = jnp.concatenate(halves, axis=0)
            plain_ref[unit] = half_kept(both[:, pair_of(unit)], unit, 1)
        for head in range(heads):
            rows = slice(head * HDIM, (head + 1) * HDIM)
            pulled = turned[(heads + head) * HDIM : (heads + head + 1) * HDIM]
            delta_ref[head : head + 1] = jnp.sum(kept[rows] * pulled, axis=0, keepdims=True)
        sum_ref[...] = jnp.zeros_like(sum_ref)
        for move in moves:
            move.wait()
        keep.wait()

    here = pl.ds(step * KEY_TILE, KEY_TILE)
    tree = tree_ref[here]
    keys_turned = tree[:, : heads * HDIM].astype(jnp.float32).T.astype(jnp.bfloat16)
    seen = seen_tile(hot_ref, side_ref)
    weights, slopes = [], []
    for head in range(heads):
        scores = jnp.dot(tree[:, pair_of(head)], turned_ref[head], preferred_element_type=jnp.float32)
        weight = jnp.exp2(scores * LOG2_SCALE) * scale_ref[head : head + 1]
        pull = jnp.dot(
            tree[:, pair_of(heads + head)], turned_ref[heads + head], preferred_element_type=jnp.float32
        )
        slope = (weight * (pull - delta_ref[head : head + 1])).astype(jnp.bfloat16) * seen
        rows = slice(head * HDIM, (head + 1) * HDIM)
        sum_ref[rows] += jnp.dot(keys_turned[rows], slope, preferred_element_type=jnp.float32)
        weights.append(weight.astype(jnp.bfloat16) * seen)
        slopes.append(slope)
    terms = slopes + weights
    score_scale = math.sqrt(HDIM)
    for pair in range(heads):
        total = 0.0
        for unit in (2 * pair, 2 * pair + 1):
            part = jnp.dot(terms[unit], plain_ref[unit], preferred_element_type=jnp.float32)
            total = total + (part * score_scale if unit < heads else part)
        tree_out[here, pair * LANES : (pair + 1) * LANES] = total.astype(jnp.bfloat16)

    @pl.when(step == pl.num_programs(0) - 1)
    def finish():
        moves = copies(row_blocks(tree_out, count), outs, sems)
        query_out[...] = sum_ref[...].T * score_scale
        for move in moves:
            move.wait()


def attend_grad(query, tops, outs, pieces, hot, side, scale, weight):
    rows, features = query.shape
    wide = weight.shape[0]
    count, width = len(pieces), pieces[0].shape[1]
    keys = pieces[0].shape[0] * count
    heads = features // HDIM
    whole = lambda step: (0, 0)
    return pl.pallas_call(
        lambda *refs: attend_grad_body(count, len(tops), *refs),
        grid=(keys // KEY_TILE,),
        in_specs=[pl.BlockSpec((rows, features), whole)] * 2
        + [ANYWHERE] * (count + len(tops))
        + [
            pl.BlockSpec((KEY_TILE, LANES), lambda step: (step, 0)),
            pl.BlockSpec((3, LANES, rows), lambda step: (0, 0, 0)),
            pl.BlockSpec((8, rows), whole),
            pl.BlockSpec(weight.shape, whole),
        ],
        out_specs=[pl.BlockSpec((rows, features), whole)] + [ANYWHERE] * (count + 1),
        out_shape=[jax.ShapeDtypeStruct((rows, features), jnp.float32)]
        + [jax.ShapeDtypeStruct(piece.shape, jnp.bfloat16) for piece in pieces]
        + [jax.ShapeDtypeStruct((rows, wide), jnp.bfloat16)],
        scratch_shapes=[
            pltpu.VMEM((keys, width), jnp.bfloat16),
            pltpu.VMEM((keys, width), jnp.bfloat16),
            pltpu.VMEM((rows, wide), jnp.bfloat16),
            pltpu.VMEM((2 * heads, LANES, rows), jnp.bfloat16),
            pltpu.VMEM((2 * heads, rows, LANES), jnp.bfloat16),
            pltpu.VMEM((8, rows), jnp.float32),
            pltpu.VMEM((features, rows), jnp.float32),
            pltpu.SemaphoreType.DMA((count,)),
            pltpu.SemaphoreType.DMA((len(tops),)),
            pltpu.SemaphoreType.DMA,
        ],
        compiler_params=pltpu.CompilerParams(vmem_limit_bytes=56 << 20),
        name="attend_grad",
    )(query, outs, *pieces, *tops, hot, side, scale, weight)


def seen_factors(reachable, seg_query, off_query, segment, offset):
    segs = reachable.shape[0]
    labels = jnp.arange(LANES, dtype=jnp.int32)
    key_mark = jnp.where(labels < HDIM, segment[:, None], offset[:, None] + HDIM)
    hot = (key_mark == labels[None, :]).astype(jnp.bfloat16)
    query_hot = (labels[:, None] == seg_query[None, :]).astype(jnp.float32)
    wide = jnp.zeros((LANES, LANES), jnp.float32).at[:segs, :segs].set(reachable.T - jnp.eye(segs, dtype=jnp.float32))
    strict = jnp.dot(wide, query_hot, preferred_element_type=jnp.float32)
    same = query_hot
    before = ((labels[:, None] >= HDIM) & (labels[:, None] - HDIM <= off_query[None, :])).astype(jnp.float32)
    return hot, jnp.stack([strict, same, before]).astype(jnp.bfloat16)


def head_marks(features):
    row = lax.broadcasted_iota(jnp.int32, (features, LANES), 0) // HDIM
    column = lax.broadcasted_iota(jnp.int32, (features, LANES), 1)
    return (row == column).astype(jnp.float32)


def over_heads(values, marks):
    sums = jnp.dot(values, marks, precision=HIGHEST, preferred_element_type=jnp.float32)
    return sums, lambda heads: lax.dot_general(
        heads, marks, (((1,), (1,)), ((), ())), precision=HIGHEST, preferred_element_type=jnp.float32
    )


def project_body(count, *refs):
    pieces, refs = refs[:count], refs[count:]
    weight_ref, scale_ref, query_out, tree_out, raw_out, group_out, group, sems, group_sem = refs
    both = raw_out.shape[1]
    features = both // 2
    step = pl.program_id(0)
    keep = pltpu.make_async_copy(group, group_out, group_sem)

    @pl.when(step == 0)
    def assemble():
        moves = copies(pieces, row_blocks(group, count), sems)
        for move in moves:
            move.wait()
        keep.start()

    @pl.when(step == pl.num_programs(0) - 1)
    def kept():
        keep.wait()

    tile = query_out.shape[0]
    product = jnp.dot(
        group[pl.ds(step * tile, tile)], weight_ref[:, : 3 * features], preferred_element_type=jnp.float32
    )
    raw = product[:, :both]
    sums, spread_heads = over_heads(raw * raw, head_marks(both))
    unit = raw * spread_heads(lax.rsqrt(sums + EPSILON))
    scaled = (unit * scale_ref[...]).astype(jnp.bfloat16)
    raw_out[...] = raw
    query_out[...] = scaled[:, :features]
    tree_out[...] = jnp.concatenate(
        [scaled[:, features:], product[:, both:].astype(jnp.bfloat16)], axis=1
    )


def project(pieces, weight, scale):
    count, width = len(pieces), pieces[0].shape[1]
    rows = pieces[0].shape[0] * count
    features = weight.shape[1] // 4
    tile = rows // 4
    whole = lambda step: (0, 0)
    block = lambda columns: pl.BlockSpec((tile, columns), lambda step: (step, 0))
    return pl.pallas_call(
        lambda *refs: project_body(count, *refs),
        grid=(4,),
        in_specs=[ANYWHERE] * count
        + [
            pl.BlockSpec(weight.shape, whole),
            pl.BlockSpec((1, 2 * features), whole),
        ],
        out_specs=[block(features), block(2 * features), block(2 * features), ANYWHERE],
        out_shape=[
            jax.ShapeDtypeStruct((rows, features), jnp.bfloat16),
            jax.ShapeDtypeStruct((rows, 2 * features), jnp.bfloat16),
            jax.ShapeDtypeStruct((rows, 2 * features), jnp.float32),
            jax.ShapeDtypeStruct((rows, width), jnp.bfloat16),
        ],
        scratch_shapes=[
            pltpu.VMEM((rows, width), jnp.bfloat16),
            pltpu.SemaphoreType.DMA((count,)),
            pltpu.SemaphoreType.DMA,
        ],
        compiler_params=pltpu.CompilerParams(vmem_limit_bytes=40 << 20),
        name="project",
    )(*pieces, weight, scale)


def project_grad_body(count, query_ref, *refs):
    tree_refs, refs = refs[:count], refs[count:]
    (raw_ref, weight_ref, scale_ref, low_out, scale_out), part_outs = refs[:5], refs[5:]
    step = pl.program_id(0)
    both = raw_ref.shape[1]
    features = both // 2
    tree = sum(ref[...].astype(jnp.float32) for ref in tree_refs)
    upstream = jnp.concatenate([query_ref[...], tree[:, :features]], axis=1)
    raw = raw_ref[...]
    marks = head_marks(both)
    sums, spread_heads = over_heads(raw * raw, marks)
    inverse = spread_heads(lax.rsqrt(sums + EPSILON))
    unit = raw * inverse
    scale_out[...] = jnp.sum(upstream * unit, axis=0, keepdims=True)[None]
    pulled = upstream * scale_ref[...]
    inner = spread_heads(over_heads(unit * pulled, marks)[0])
    grads = inverse * (pulled - unit * inner)
    low = jnp.concatenate([grads, tree[:, features:]], axis=1).astype(jnp.bfloat16)
    low_out[...] = low
    part = contract_cols(low, weight_ref[:, : 3 * features]).astype(jnp.bfloat16)
    for place, part_out in enumerate(part_outs):

        @pl.when((step == place) | (len(part_outs) == 1))
        def store():
            part_out[...] = part


def project_grad(query_grad, tree_parts, raw, weight, scale, count_out):
    rows, both = raw.shape
    width = weight.shape[0]
    features = both // 2
    tile = rows // 4
    whole = lambda step: (0, 0)
    block = lambda columns: pl.BlockSpec((tile, columns), lambda step: (step, 0))
    return pl.pallas_call(
        lambda *refs: project_grad_body(len(tree_parts), *refs),
        grid=(4,),
        in_specs=[block(features)]
        + [block(both) for part in tree_parts]
        + [block(both), pl.BlockSpec(weight.shape, whole), pl.BlockSpec((1, both), whole)],
        out_specs=[
            block(3 * features),
            pl.BlockSpec((1, 1, both), lambda step: (step, 0, 0)),
        ]
        + ([block(width)] if count_out == 1 else [pl.BlockSpec((tile, width), whole)] * 4),
        out_shape=[
            jax.ShapeDtypeStruct((rows, 3 * features), jnp.bfloat16),
            jax.ShapeDtypeStruct((4, 1, both), jnp.float32),
        ]
        + [jax.ShapeDtypeStruct((rows // count_out, width), jnp.bfloat16)] * count_out,
        compiler_params=pltpu.CompilerParams(vmem_limit_bytes=40 << 20),
        name="project_grad",
    )(query_grad, *tree_parts, raw, weight, scale)


def gated(up, gate, scale_up, scale_gate):
    raw = gate * (scale_gate * math.sqrt(D))
    curve = 1.0 / (1.0 + jnp.exp(-raw))
    return raw, curve, raw * curve, up * scale_up


def hidden_body(count, halves, *refs):
    pieces, refs = refs[:count], refs[count:]
    weights, refs = refs[:halves], refs[halves:]
    scale_ref, refs = refs[0], refs[1:]
    outs, refs = refs[:count], refs[count:]
    group_out, up_out, gate_out, mixed_out, group, matrices, total, sems, out_sem = refs
    half = up_out.shape[1] // halves
    moves = copies(pieces, row_blocks(group, count), sems)
    loads = [
        pltpu.make_async_copy(
            weights[place % halves].at[:, place // halves], matrices.at[place], sems.at[count + place]
        )
        for place in range(3 * halves)
    ]
    for load in loads:
        load.start()
    for move in moves:
        move.wait()
    keep = pltpu.make_async_copy(group, group_out, out_sem)
    keep.start()
    for place in range(halves):
        columns = slice(place * half, (place + 1) * half)
        for matrix in range(3):
            loads[matrix * halves + place].wait()
        tokens = group[...]
        up = contract_cols(tokens, matrices[place].reshape(half, -1))
        gate = contract_cols(tokens, matrices[halves + place].reshape(half, -1))
        up_out[:, columns] = up.astype(jnp.bfloat16)
        gate_out[:, columns] = gate.astype(jnp.bfloat16)
        raw, curve, silu, scaled = gated(up, gate, scale_ref[0:1, columns], scale_ref[1:2, columns])
        mixed = (scaled * silu).astype(jnp.bfloat16)
        mixed_out[:, columns] = mixed
        part = jnp.dot(
            mixed, matrices[2 * halves + place].reshape(half, -1), preferred_element_type=jnp.float32
        )
        total[...] = part if place == 0 else total[...] + part
    rows = group.shape[0] // count
    for place in range(count):
        outs[place][...] = total[place * rows : (place + 1) * rows].astype(jnp.bfloat16)
    keep.wait()


def hidden_forward(pieces, weights, scales):
    count, halves = len(pieces), len(weights)
    rows, width = pieces[0].shape[0] * count, pieces[0].shape[1]
    half = weights[0].shape[0] * weights[0].shape[2]
    hidden = half * halves
    low = lambda columns: jax.ShapeDtypeStruct((rows, columns), jnp.bfloat16)
    vmem = pl.BlockSpec(memory_space=pltpu.VMEM)
    return pl.pallas_call(
        lambda *refs: hidden_body(count, halves, *refs),
        in_specs=[ANYWHERE] * (count + halves) + [vmem],
        out_specs=[vmem] * count + [ANYWHERE] + [vmem] * 3,
        out_shape=[jax.ShapeDtypeStruct(piece.shape, jnp.bfloat16) for piece in pieces]
        + [low(width), low(hidden), low(hidden), low(hidden)],
        scratch_shapes=[
            pltpu.VMEM((rows, width), jnp.bfloat16),
            pltpu.VMEM((3 * halves, weights[0].shape[0]) + weights[0].shape[2:], jnp.bfloat16),
            pltpu.VMEM((rows, width), jnp.float32),
            pltpu.SemaphoreType.DMA((count + 3 * halves,)),
            pltpu.SemaphoreType.DMA,
        ],
        compiler_params=pltpu.CompilerParams(vmem_limit_bytes=52 << 20),
        name="hidden",
    )(*pieces, *weights, jnp.stack(scales))


def hidden_grad_body(count, halves, *refs):
    pieces, refs = refs[:count], refs[count:]
    weights, refs = refs[:halves], refs[halves:]
    scale_ref, up_ref, gate_ref = refs[:3]
    outs, refs = refs[3 : 3 + count], refs[3 + count :]
    group_out, up_out, gate_out, scale_out, group, matrices, total, sems, out_sem = refs
    half = up_out.shape[1] // halves
    moves = copies(pieces, row_blocks(group, count), sems)
    loads = [
        pltpu.make_async_copy(
            weights[place % halves].at[:, place // halves], matrices.at[place], sems.at[count + place]
        )
        for place in range(3 * halves)
    ]
    for load in loads:
        load.start()
    for move in moves:
        move.wait()
    keep = pltpu.make_async_copy(group, group_out, out_sem)
    keep.start()
    for place in range(halves):
        columns = slice(place * half, (place + 1) * half)
        for matrix in range(3):
            loads[matrix * halves + place].wait()
        pulled = contract_cols(group[...], matrices[2 * halves + place].reshape(half, -1))
        pulled = pulled.astype(jnp.bfloat16).astype(jnp.float32)
        up = up_ref[:, columns].astype(jnp.float32)
        gate = gate_ref[:, columns].astype(jnp.float32)
        scale_up, scale_gate = scale_ref[0:1, columns], scale_ref[1:2, columns]
        raw, curve, silu, scaled = gated(up, gate, scale_up, scale_gate)
        curved = pulled * silu
        up_low = (curved * scale_up).astype(jnp.bfloat16)
        bent = pulled * scaled * (curve * (1.0 + raw * (1.0 - curve)))
        gate_low = (bent * (scale_gate * math.sqrt(D))).astype(jnp.bfloat16)
        scale_out[0:1, columns] = jnp.sum(curved * up, axis=0, keepdims=True)
        scale_out[1:2, columns] = jnp.sum(bent * gate, axis=0, keepdims=True) * math.sqrt(D)
        up_out[:, columns] = up_low
        gate_out[:, columns] = gate_low
        part = jnp.dot(
            up_low, matrices[place].reshape(half, -1), preferred_element_type=jnp.float32
        )
        part = part + jnp.dot(
            gate_low, matrices[halves + place].reshape(half, -1), preferred_element_type=jnp.float32
        )
        total[...] = part if place == 0 else total[...] + part
    rows = group.shape[0] // count
    for place in range(count):
        outs[place][...] = total[place * rows : (place + 1) * rows].astype(jnp.bfloat16)
    keep.wait()


def hidden_backward(pieces, weights, scales, up, gate):
    count, halves = len(pieces), len(weights)
    rows, width = pieces[0].shape[0] * count, pieces[0].shape[1]
    half = weights[0].shape[0] * weights[0].shape[2]
    hidden = half * halves
    low = lambda columns: jax.ShapeDtypeStruct((rows, columns), jnp.bfloat16)
    vmem = pl.BlockSpec(memory_space=pltpu.VMEM)
    return pl.pallas_call(
        lambda *refs: hidden_grad_body(count, halves, *refs),
        in_specs=[ANYWHERE] * (count + halves) + [vmem] * 3,
        out_specs=[vmem] * count + [ANYWHERE] + [vmem] * 3,
        out_shape=[jax.ShapeDtypeStruct(piece.shape, jnp.bfloat16) for piece in pieces]
        + [low(width), low(hidden), low(hidden), jax.ShapeDtypeStruct((8, hidden), jnp.float32)],
        scratch_shapes=[
            pltpu.VMEM((rows, width), jnp.bfloat16),
            pltpu.VMEM((3 * halves, weights[0].shape[0]) + weights[0].shape[2:], jnp.bfloat16),
            pltpu.VMEM((rows, width), jnp.float32),
            pltpu.SemaphoreType.DMA((count + 3 * halves,)),
            pltpu.SemaphoreType.DMA,
        ],
        compiler_params=pltpu.CompilerParams(vmem_limit_bytes=56 << 20),
        name="hidden_grad",
    )(*pieces, *weights, jnp.stack(scales), up, gate)


def visibility(parents, slots, group_size):
    labels = jnp.arange(SEGS, dtype=jnp.int32)
    linked = (parents[:, None] == labels[None, :]).astype(jnp.float32)
    reachable = jnp.maximum(linked, jnp.eye(SEGS, dtype=jnp.float32))
    for doubling in range(SEGS.bit_length()):
        reachable = jnp.minimum(jnp.dot(reachable, reachable, precision=HIGHEST), 1.0)
    return seen_factors(reachable, *row_labels(slots, group_size))


def prepare_attention(packed, scale_both, pieces, parents, slots):
    rows = pieces[0].shape[0] * len(pieces)
    queries, tree_own, raw, group = project(pieces, packed, scale_both)
    return visibility(parents, slots, rows), queries, group_gather(tree_own, "ctx"), raw, group


def forward_attention(packed, prepared, count):
    seen, queries, tree, raw, group = prepared
    heads_low, inverse, *parts = attend(queries, tree, *seen, packed, count)
    return group_scatter(parts, "tp")[0], (group, seen, queries, tree, raw, heads_low, inverse)


def first_mix(tokens_own, branch_parts, alpha_attn, gates):
    tokens_wide = tokens_own.astype(jnp.float32)
    hidden_one, pull_in = jax.vjp(
        mix_rows, tokens_wide, total_wide(branch_parts), after(alpha_attn, *gates)
    )
    hidden_low = hidden_one.astype(jnp.bfloat16)
    return (hidden_one, pull_in), hidden_low, hidden_gather(hidden_low)


def second_mix(hidden_one, branch_parts, alpha_mlp, cotangent_own, gates):
    output_wide, pull_out = jax.vjp(
        mix_rows, hidden_one, total_wide(branch_parts), after(alpha_mlp, *gates)
    )
    hidden_direct, branch_grad, grad_alpha_mlp = pull_out(cotangent_own.astype(jnp.float32))
    branch_low = branch_grad.astype(jnp.bfloat16)
    kept = (output_wide.astype(jnp.bfloat16), hidden_direct, grad_alpha_mlp)
    return kept, branch_low, hidden_gather(branch_low)


def third_mix(pull_in, hidden_parts, hidden_direct, gates):
    hidden_grad = total_wide(hidden_parts) + after(hidden_direct, *gates)
    tokens_direct, branch_grad, grad_alpha_attn = pull_in(hidden_grad)
    return tokens_direct, branch_grad.astype(jnp.bfloat16), grad_alpha_attn


def backward_attention(packed, kept, tops, hops):
    group, seen, queries, tree, raw, heads_low, inverse = kept
    query_grads, *rest = attend_grad(queries, tops, heads_low, tree, *seen, inverse, packed)
    tree_parts, first = group_scatter(rest[:-1], "ctx", hops)
    return query_grads, tree_parts, (rest[-1], heads_low)


def backward_projection(packed, scale_both, kept, attended, tokens_direct, hops):
    group, raw = kept[0], kept[4]
    query_grads, tree_parts, heads_factors = attended
    count = lax.axis_size("tp") if lax.axis_size("tp") == 4 else 1
    low, scale_sums, *parts = project_grad(
        query_grads, tree_parts, raw, packed, scale_both, count
    )
    own_parts, first = group_scatter(parts, "tp", hops)
    grad_tokens = tokens_direct + total_wide(own_parts)
    features = scale_both.shape[1] // 2
    scale_sum = jnp.sum(scale_sums, axis=(0, 1))
    scale_sum = scale_sum[:features] + scale_sum[features:]
    return grad_tokens, ((group, low), heads_factors), scale_sum, first


def joint_product(factors):
    formers, latters = zip(*factors)
    return contract_rows(jnp.concatenate(formers, axis=0), jnp.concatenate(latters, axis=0))


def per_device(
    tokens,
    parents,
    slot_segment,
    w_query,
    w_key,
    w_value,
    w_attn_out,
    w_up,
    w_gate,
    w_down,
    alpha_attn,
    alpha_mlp,
    scale_qk,
    scale_up,
    scale_gate,
    cotangent,
):
    width = tokens.shape[-1]
    micros = range(tokens.shape[0])
    last = tokens.shape[0] - 1
    groups = [group_gather(tokens[0, 0], "tp")]
    packed = lax.all_gather(
        jnp.concatenate([w_query, w_key, w_value, w_attn_out.T], axis=1),
        SPREAD,
        axis=0,
        tiled=True,
    )
    scales = hidden_scales(scale_up, scale_gate)
    scale_both = jnp.concatenate([scale_qk, scale_qk])[None]
    blocks = hidden_blocks(w_up, w_gate, w_down)
    prepared = []
    gates = scales
    for m in micros:
        early = after(scale_both, *gates)
        prepared.append(
            prepare_attention(packed, early, groups[m], parents[m, 0], slot_segment[m, 0])
        )
        if m == last:
            break
        ahead = groups[m][len(groups[m]) // 2]
        groups.append(group_gather(after(tokens[m + 1, 0], ahead), "tp", prepared[m][1:2]))
        if m == 0:
            shards = hidden_shards(after(blocks, groups[1][-1]))
        tree = prepared[m][2]
        gates = (tree[len(tree) // 2], shards)
    if last == 0:
        shards = hidden_shards(blocks)
    weights = hidden_weights(shards)
    front = [forward_attention(packed, prepared[m], len(groups[m])) for m in micros]
    gates = ()
    opened, forwards, mixed, backwards, closed, tops = [], [], [], [], [], []
    for m in micros:
        kept, mark, pieces = first_mix(tokens[m, 0], front[m][0], alpha_attn, gates)
        gates = (mark,)
        count = len(pieces)
        outs = hidden_forward(pieces, weights, scales)
        opened.append(kept)
        forwards.append((hidden_scatter(outs[:count]), outs[count:]))
    for m in micros:
        kept, mark, pieces = second_mix(
            opened[m][0], forwards[m][0], alpha_mlp, cotangent[m, 0], gates
        )
        gates = (mark,)
        up, gate = forwards[m][1][1:3]
        outs = hidden_backward(pieces, weights, scales, up, gate)
        mixed.append(kept)
        backwards.append((hidden_scatter(outs[:count]), outs[count:]))
    joined = []
    for m in micros:
        hidden_group, hidden_mixed = forwards[m][1][0], forwards[m][1][3]
        top_group, up_low, gate_low = backwards[m][1][:3]
        joined.append(((up_low, hidden_group), (gate_low, hidden_group), (hidden_mixed, top_group)))
    products = [
        joint_product([joined[m][place] for m in micros]).astype(jnp.bfloat16)
        for place in range(3)
    ]
    for m in micros:
        closed.append(
            third_mix(
                opened[m][1],
                backwards[m][0],
                mixed[m][1],
                gates,
            )
        )
        gates = (closed[-1][1],)
        tops.append(group_gather(closed[-1][1], "tp", products if m == last else ()))
    lines = core_sums(products)
    line_sums = hidden_line_sums([after(line, *[top[-1] for top in tops]) for line in lines])
    spread_sums = hidden_spread(line_sums)
    attended = [backward_attention(packed, front[m][1], tops[m], 1) for m in micros]
    vectors = vector_sums(
        after(
            sum(jnp.concatenate([closed[m][2], mixed[m][2]]) for m in micros), attended[-1][0]
        ),
        sum(backwards[m][1][3][:2] for m in micros),
    )
    gates = ()
    back = []
    for m in micros:
        back.append(
            backward_projection(
                packed,
                after(scale_both, *gates),
                front[m][1],
                attended[m],
                closed[m][0],
                1 if m == last else 2,
            )
        )
        gates = (back[-1][3], spread_sums, vectors)
    product = jnp.concatenate(
        [joint_product([back[m][1][place] for m in micros]) for place in range(2)], axis=1
    )
    grad_attention = owner_scatter(product.astype(jnp.bfloat16))
    grad_q, grad_k, grad_v, grad_o = jnp.split(grad_attention, 4, axis=1)
    grad_u, grad_g, grad_d = hidden_weight_grads(spread_sums)
    sums = butterfly(jnp.concatenate([vectors, sum(back[m][2] for m in micros)]), SPREAD)
    sum_alphas, sum_hidden, sum_qk = jnp.split(sums, [2 * width, sums.shape[0] - scale_qk.shape[0]])
    sum_up, sum_gate = jnp.split(sum_hidden, 2)
    return (
        jnp.stack([mixed[m][0] for m in micros])[:, None],
        jnp.stack([back[m][0] for m in micros])[:, None],
        grad_q,
        grad_k,
        grad_v,
        grad_o.T,
        grad_u.T,
        grad_g.T,
        grad_d,
        sum_alphas[:width],
        sum_alphas[width:],
        sum_qk,
        sum_up,
        sum_gate,
    )


def solution(mesh):
    return jax.shard_map(
        per_device,
        mesh=mesh,
        in_specs=(
            P(None, "shard", ("ctx", "tp"), None),
            P(None, "shard", None),
            P(None, "shard", None),
            P(("shard", "ctx"), "tp"),
            P(("shard", "ctx"), "tp"),
            P(("shard", "ctx"), "tp"),
            P("tp", ("shard", "ctx")),
            P(("shard", "ctx"), "tp"),
            P(("shard", "ctx"), "tp"),
            P("tp", ("shard", "ctx")),
            P(),
            P(),
            P("tp"),
            P("tp"),
            P("tp"),
            P(None, "shard", ("ctx", "tp"), None),
        ),
        out_specs=(
            P(None, "shard", ("ctx", "tp"), None),
            P(None, "shard", ("ctx", "tp"), None),
            P(("shard", "ctx"), "tp"),
            P(("shard", "ctx"), "tp"),
            P(("shard", "ctx"), "tp"),
            P("tp", ("shard", "ctx")),
            P(("shard", "ctx"), "tp"),
            P(("shard", "ctx"), "tp"),
            P("tp", ("shard", "ctx")),
            P(),
            P(),
            P("tp"),
            P("tp"),
            P("tp"),
        ),
        check_vma=False,
    )
```

```python
import math

import jax
import jax.numpy as jnp
from jax import lax
from jax.experimental import pallas as pl
from jax.experimental.pallas import tpu as pltpu
from jax.sharding import PartitionSpec as P

D = 1280
HDIM = 64
SEG = 64
SEGS = 40
TREE_TOK = 2560


EPSILON = 1e-06
HIGHEST = lax.Precision.HIGHEST
SPREAD = ("shard", "ctx")


def unit_rows(values):
    return values * lax.rsqrt(jnp.sum(values * values, axis=-1, keepdims=True) + EPSILON)


def contract_rows(former, latter):
    return lax.dot_general(
        former, latter, (((0,), (0,)), ((), ())), preferred_element_type=jnp.float32
    )


def contract_cols(former, latter):
    return lax.dot_general(
        former, latter, (((1,), (1,)), ((), ())), preferred_element_type=jnp.float32
    )


def mix_rows(residual, branch, mixing):
    return unit_rows(residual + mixing * (unit_rows(branch) - residual))


def swap(value, axis, bit):
    size = lax.axis_size(axis)
    return lax.ppermute(value, axis, [(place, place ^ bit) for place in range(size)])


def after(value, *others):
    for other in others:
        value = value + (other[(slice(0, 1),) * other.ndim].reshape(()) * 0).astype(value.dtype)
    return value


def add_low(former, latter):
    return (former.astype(jnp.float32) + latter.astype(jnp.float32)).astype(jnp.bfloat16)


def butterfly(value, axes):
    for axis in axes:
        bit = 1
        while bit < lax.axis_size(axis):
            value = value + swap(value, axis, bit)
            bit *= 2
    return value


def group_order(axis):
    size = lax.axis_size(axis)
    places = jnp.arange(size, dtype=jnp.int32)
    return places ^ lax.axis_index(axis) if size == 4 else places


def group_gather(own_block, axis, gates=None):
    if lax.axis_size(axis) != 4:
        return [lax.all_gather(own_block, axis, axis=0, tiled=True)]
    across = swap(own_block, axis, 2)
    beside = swap(own_block, axis, 1)
    source = across if gates is None else after(across, beside, *gates)
    return [own_block, beside, across, swap(source, axis, 1)]


def group_scatter(pieces, axis, hops=2):
    if lax.axis_size(axis) != 4:
        parts = [lax.psum_scatter(pieces[0], axis, scatter_dimension=0, tiled=True)]
        return parts, parts[0]
    own, beside, across, far = pieces
    if hops == 1:
        parts = [swap(piece, axis, bits) for piece, bits in zip(pieces[1:], (1, 2, 3))]
        return [own] + parts, parts[0]
    far = swap(far, axis, 1)
    across = swap(add_low(across, far), axis, 2)
    return [own, swap(after(beside, far), axis, 1), across], far


def total_wide(parts):
    return sum(part.astype(jnp.float32) for part in parts)


def in_plane():
    return (lax.axis_size("shard"), lax.axis_size("ctx"), lax.axis_size("tp")) == (2, 4, 4)


def hop(value, bits):
    return lax.ppermute(value, SPREAD, [(place, place ^ bits) for place in range(8)])


def hidden_gather(own_block):
    if not in_plane():
        return group_gather(own_block, "tp")
    return [own_block] + [hop(own_block, bits) for bits in (2, 4, 6)]


def hidden_scatter(pieces):
    if not in_plane():
        return group_scatter(pieces, "tp")[0]
    return [pieces[0]] + [hop(piece, bits) for piece, bits in zip(pieces[1:], (2, 4, 6))]


def hidden_blocks(w_up, w_gate, w_down):
    if not in_plane():
        return jnp.stack([w_up.T, w_gate.T, w_down])
    rows, hidden = w_up.shape
    part = hidden // 8
    packed = jnp.stack(
        [
            w_up.reshape(rows, 8, part).transpose(1, 2, 0),
            w_gate.reshape(rows, 8, part).transpose(1, 2, 0),
            w_down.reshape(8, part, rows),
        ],
        axis=1,
    )
    return lax.all_to_all(packed, SPREAD, 0, 0)


def hidden_shards(blocks):
    if not in_plane():
        return blocks
    rows = blocks.shape[2]
    return blocks.transpose(1, 2, 0, 3).reshape(3, rows, -1)


def hidden_weights(shards):
    if not in_plane():
        return [lax.all_gather(shards, SPREAD, axis=2, tiled=True)[None]]
    line = lax.all_gather(shards, "tp", axis=0)
    return [line, swap(line, "ctx", 1)]


def hidden_scales(*scales):
    if not in_plane():
        return scales
    part = scales[0].shape[0] // 8
    first = lax.axis_index(SPREAD) * part
    own = jnp.stack([lax.dynamic_slice_in_dim(scale, first, part) for scale in scales])
    line = jnp.concatenate(group_gather(own[None], "tp"), axis=0)
    line = jnp.take(line, group_order("tp"), axis=0)
    both = jnp.concatenate([line, swap(line, "ctx", 1)], axis=0)
    return tuple(both[:, place].reshape(-1) for place in range(len(scales)))


def core_sums(products):
    if not in_plane():
        return products
    half = products[0].shape[0] // 2
    return [add_low(product[:half], swap(product[half:], "ctx", 1)) for product in products]


def hidden_line_sums(lines):
    if not in_plane():
        return lines
    return [lax.psum_scatter(line, "tp", scatter_dimension=0, tiled=True) for line in lines]


def hidden_pack(sums):
    if not in_plane():
        return jnp.stack(sums)
    part, width = sums[0].shape
    return jnp.stack([total.reshape(part, 8, width // 8).transpose(1, 0, 2) for total in sums], 1)


def hidden_spread(packed):
    if not in_plane():
        return lax.psum_scatter(packed, SPREAD, scatter_dimension=2, tiled=True)
    return lax.all_to_all(packed, SPREAD, 0, 0)


def hidden_weight_grads(spread_sums):
    wide = spread_sums.astype(jnp.float32)
    if not in_plane():
        return [wide[place] for place in range(3)]
    return [wide[:, place].reshape(-1, wide.shape[-1]) for place in range(3)]


def vector_sums(alphas, hidden_sums):
    count, hidden = hidden_sums.shape
    if not in_plane():
        return jnp.concatenate([butterfly(alphas, ("tp",)), hidden_sums.reshape(-1)])
    parts = hidden_sums.reshape(count, 2, 4, hidden // 8)
    line = (parts[:, 0] + swap(parts[:, 1], "ctx", 1)).reshape(-1)
    width = alphas.shape[0]
    both = butterfly(jnp.concatenate([alphas, line]), ("tp",))
    line = both[width:].reshape(count, 4, hidden // 8)
    line = lax.dynamic_index_in_dim(line, lax.axis_index("tp"), 1, keepdims=True)
    blank = jnp.zeros((count, 8, hidden // 8), jnp.float32)
    placed = lax.dynamic_update_slice_in_dim(blank, line, lax.axis_index(SPREAD), 1)
    return jnp.concatenate([both[:width], placed.reshape(-1)])


def owner_scatter(product_low):
    if not in_plane():
        total = lax.psum_scatter(product_low, SPREAD, scatter_dimension=0, tiled=True)
        return total.astype(jnp.float32)
    place = lax.axis_index("ctx")
    core, along, plane = place % 2, place // 2, lax.axis_index("shard")
    rows, width = product_low.shape
    blocks = product_low.reshape(4, 2, rows // 8, width)

    def of_core(which):
        return lax.dynamic_index_in_dim(blocks, which, 1, keepdims=False)

    blocks = add_low(of_core(core), swap(of_core(1 - core), "ctx", 1))
    chip = plane * 2 + along

    def of_chip(bits):
        return lax.dynamic_index_in_dim(blocks, chip ^ bits, 0, keepdims=False)

    return total_wide([of_chip(0)] + [hop(of_chip(bits), 2 * bits) for bits in (1, 2, 3)])


def row_labels(slots, group_size):
    tree_rows = group_size * lax.axis_size("ctx")
    chunk = group_size // lax.axis_size("tp")
    within = (group_order("tp")[:, None] * chunk + jnp.arange(chunk, dtype=jnp.int32)).reshape(-1)
    keys = (group_order("ctx")[:, None] * group_size + within[None, :]).reshape(-1)
    onehot = (keys[:, None] // SEG == jnp.arange(tree_rows // SEG, dtype=jnp.int32)[None, :])
    segment = jnp.sum(jnp.where(onehot, slots[None, :], 0), axis=1)
    offset = keys % SEG
    if lax.axis_size("ctx") != 4:
        first = lax.axis_index("ctx") * group_size
    else:
        first = 0
    return (
        lax.dynamic_slice_in_dim(segment, first, group_size),
        lax.dynamic_slice_in_dim(offset, first, group_size),
        segment,
        offset,
    )


LOG2_SCALE = math.sqrt(HDIM) * math.log2(math.e)
LANES = 128
KEY_TILE = 1280
GRAD_TILE = 640


def copies(sources, targets, sems):
    moves = [
        pltpu.make_async_copy(source, target, sems.at[place])
        for place, (source, target) in enumerate(zip(sources, targets))
    ]
    for move in moves:
        move.start()
    return moves


def row_blocks(ref, count):
    rows = ref.shape[0] // count
    return [ref.at[pl.ds(place * rows, rows)] for place in range(count)]


ANYWHERE = pl.BlockSpec(memory_space=pl.ANY)


def half_kept(value, unit, axis):
    place = lax.broadcasted_iota(jnp.int32, value.shape, axis)
    inside = (place >= HDIM) if unit % 2 else (place < HDIM)
    return jnp.where(inside, value, jnp.zeros_like(value))


def seen_tile(hot_ref, side_ref):
    hot = hot_ref[...]
    strict = jnp.dot(hot, side_ref[0], preferred_element_type=jnp.float32)
    same = jnp.dot(hot, side_ref[1], preferred_element_type=jnp.float32)
    before = jnp.dot(hot, side_ref[2], preferred_element_type=jnp.float32)
    return (strict + same * before).astype(jnp.bfloat16)


def pair_of(unit):
    return slice(unit // 2 * LANES, unit // 2 * LANES + LANES)


def attend_body(count, query_ref, *refs):
    pieces, refs = refs[:count], refs[count:]
    (hot_ref, side_ref, weight_ref, out_ref, scale_ref), refs = refs[:5], refs[5:]
    outs, (tree_ref, turned_ref, sum_ref, sems) = refs[:-4], refs[-4:]
    heads = query_ref.shape[1] // HDIM
    step = pl.program_id(0)

    @pl.when(step == 0)
    def prepare():
        moves = copies(pieces, row_blocks(tree_ref, count), sems)
        turned = query_ref[...].astype(jnp.float32).T.astype(jnp.bfloat16)
        blank = jnp.zeros((HDIM, turned.shape[1]), jnp.bfloat16)
        for head in range(heads):
            own = turned[head * HDIM : (head + 1) * HDIM]
            halves = [blank, own] if head % 2 else [own, blank]
            turned_ref[head] = jnp.concatenate(halves, axis=0)
        sum_ref[...] = jnp.zeros_like(sum_ref)
        for move in moves:
            move.wait()

    tree = tree_ref[pl.ds(step * KEY_TILE, KEY_TILE)]
    values_turned = tree[:, heads * HDIM :].astype(jnp.float32).T.astype(jnp.bfloat16)
    seen = seen_tile(hot_ref, side_ref)
    ones = jnp.ones((sum_ref.shape[1] - HDIM, tree.shape[0]), jnp.bfloat16)
    for head in range(heads):
        scores = jnp.dot(tree[:, pair_of(head)], turned_ref[head], preferred_element_type=jnp.float32)
        lifted = jnp.exp2(scores * LOG2_SCALE).astype(jnp.bfloat16) * seen
        own = jnp.concatenate([values_turned[head * HDIM : (head + 1) * HDIM], ones], axis=0)
        sum_ref[head] += jnp.dot(own, lifted, preferred_element_type=jnp.float32)

    @pl.when(step == pl.num_programs(0) - 1)
    def finish():
        parts = []
        for head in range(heads):
            inverse = 1.0 / sum_ref[head, HDIM : HDIM + 1]
            scale_ref[head : head + 1] = inverse
            parts.append(sum_ref[head, :HDIM] * inverse)
        low = jnp.concatenate(parts, axis=0).T.astype(jnp.bfloat16)
        out_ref[...] = low
        width = low.shape[1]
        rows = low.shape[0] // len(outs)
        for place, out in enumerate(outs):
            out[...] = contract_cols(
                low[place * rows : (place + 1) * rows], weight_ref[:, 3 * width :]
            ).astype(jnp.bfloat16)


def attend(query, pieces, hot, side, weight, count_out):
    rows, features = query.shape
    wide = weight.shape[0]
    count, width = len(pieces), pieces[0].shape[1]
    keys = pieces[0].shape[0] * count
    heads = features // HDIM
    whole = lambda step: (0, 0)
    return pl.pallas_call(
        lambda *refs: attend_body(count, *refs),
        grid=(keys // KEY_TILE,),
        in_specs=[pl.BlockSpec((rows, features), whole)]
        + [ANYWHERE] * count
        + [
            pl.BlockSpec((KEY_TILE, LANES), lambda step: (step, 0)),
            pl.BlockSpec((3, LANES, rows), lambda step: (0, 0, 0)),
            pl.BlockSpec(weight.shape, whole),
        ],
        out_specs=[
            pl.BlockSpec((rows, features), whole),
            pl.BlockSpec((8, rows), whole),
        ]
        + [pl.BlockSpec((rows // count_out, wide), whole)] * count_out,
        out_shape=[
            jax.ShapeDtypeStruct((rows, features), jnp.bfloat16),
            jax.ShapeDtypeStruct((8, rows), jnp.float32),
        ]
        + [jax.ShapeDtypeStruct((rows // count_out, wide), jnp.bfloat16)] * count_out,
        scratch_shapes=[
            pltpu.VMEM((keys, width), jnp.bfloat16),
            pltpu.VMEM((heads, LANES, rows), jnp.bfloat16),
            pltpu.VMEM((heads, HDIM + 16, rows), jnp.float32),
            pltpu.SemaphoreType.DMA((count,)),
        ],
        compiler_params=pltpu.CompilerParams(vmem_limit_bytes=48 << 20),
        name="attend",
    )(query, *pieces, hot, side, weight)


def attend_grad_body(count, tops, query_ref, heads_ref, *refs):
    pieces, refs = refs[:count], refs[count:]
    top_refs, refs = refs[:tops], refs[tops:]
    (hot_ref, side_ref, scale_ref, weight_ref, query_out), refs = refs[:5], refs[5:]
    outs, refs = refs[:count], refs[count:]
    group_out, tree_ref, tree_out, group, turned_ref, plain_ref, delta_ref, sum_ref = refs[:8]
    sems, top_sems, group_sem = refs[8:]
    heads = heads_ref.shape[1] // HDIM
    units = 2 * heads
    step = pl.program_id(0)

    @pl.when(step == 0)
    def prepare():
        moves = copies(pieces, row_blocks(tree_ref, count), sems)
        gathers = copies(top_refs, row_blocks(group, tops), top_sems)
        for gather in gathers:
            gather.wait()
        keep = pltpu.make_async_copy(group, group_out, group_sem)
        keep.start()
        features = query_ref.shape[1]
        upstream = jnp.dot(
            group[...], weight_ref[:, 3 * features :], preferred_element_type=jnp.float32
        )
        both = jnp.concatenate([query_ref[...], upstream.astype(jnp.bfloat16)], axis=1)
        turned = both.astype(jnp.float32).T
        kept = heads_ref[...].astype(jnp.float32).T
        blank = jnp.zeros((HDIM, turned.shape[1]), jnp.bfloat16)
        for unit in range(units):
            own = turned[unit * HDIM : (unit + 1) * HDIM].astype(jnp.bfloat16)
            halves = [blank, own] if unit % 2 else [own, blank]
            turned_ref[unit] = jnp.concatenate(halves, axis=0)
            plain_ref[unit] = half_kept(both[:, pair_of(unit)], unit, 1)
        for head in range(heads):
            rows = slice(head * HDIM, (head + 1) * HDIM)
            pulled = turned[(heads + head) * HDIM : (heads + head + 1) * HDIM]
            delta_ref[head : head + 1] = jnp.sum(kept[rows] * pulled, axis=0, keepdims=True)
        sum_ref[...] = jnp.zeros_like(sum_ref)
        for move in moves:
            move.wait()
        keep.wait()

    here = pl.ds(step * GRAD_TILE, GRAD_TILE)
    tree = tree_ref[here]
    keys_turned = tree[:, : heads * HDIM].astype(jnp.float32).T.astype(jnp.bfloat16)
    seen = seen_tile(hot_ref, side_ref)
    weights, slopes = [], []
    for head in range(heads):
        scores = jnp.dot(tree[:, pair_of(head)], turned_ref[head], preferred_element_type=jnp.float32)
        weight = jnp.exp2(scores * LOG2_SCALE) * scale_ref[head : head + 1]
        pull = jnp.dot(
            tree[:, pair_of(heads + head)], turned_ref[heads + head], preferred_element_type=jnp.float32
        )
        slope = (weight * (pull - delta_ref[head : head + 1])).astype(jnp.bfloat16) * seen
        rows = slice(head * HDIM, (head + 1) * HDIM)
        sum_ref[rows] += jnp.dot(keys_turned[rows], slope, preferred_element_type=jnp.float32)
        weights.append(weight.astype(jnp.bfloat16) * seen)
        slopes.append(slope)
    terms = slopes + weights
    score_scale = math.sqrt(HDIM)
    for pair in range(heads):
        total = 0.0
        for unit in (2 * pair, 2 * pair + 1):
            part = jnp.dot(terms[unit], plain_ref[unit], preferred_element_type=jnp.float32)
            total = total + (part * score_scale if unit < heads else part)
        tree_out[here, pair * LANES : (pair + 1) * LANES] = total.astype(jnp.bfloat16)

    @pl.when(step == pl.num_programs(0) - 1)
    def finish():
        moves = copies(row_blocks(tree_out, count), outs, sems)
        query_out[...] = sum_ref[...].T * score_scale
        for move in moves:
            move.wait()


def attend_grad(query, tops, outs, pieces, hot, side, scale, weight):
    rows, features = query.shape
    wide = weight.shape[0]
    count, width = len(pieces), pieces[0].shape[1]
    keys = pieces[0].shape[0] * count
    heads = features // HDIM
    whole = lambda step: (0, 0)
    return pl.pallas_call(
        lambda *refs: attend_grad_body(count, len(tops), *refs),
        grid=(keys // GRAD_TILE,),
        in_specs=[pl.BlockSpec((rows, features), whole)] * 2
        + [ANYWHERE] * (count + len(tops))
        + [
            pl.BlockSpec((GRAD_TILE, LANES), lambda step: (step, 0)),
            pl.BlockSpec((3, LANES, rows), lambda step: (0, 0, 0)),
            pl.BlockSpec((8, rows), whole),
            pl.BlockSpec(weight.shape, whole),
        ],
        out_specs=[pl.BlockSpec((rows, features), whole)] + [ANYWHERE] * (count + 1),
        out_shape=[jax.ShapeDtypeStruct((rows, features), jnp.float32)]
        + [jax.ShapeDtypeStruct(piece.shape, jnp.bfloat16) for piece in pieces]
        + [jax.ShapeDtypeStruct((rows, wide), jnp.bfloat16)],
        scratch_shapes=[
            pltpu.VMEM((keys, width), jnp.bfloat16),
            pltpu.VMEM((keys, width), jnp.bfloat16),
            pltpu.VMEM((rows, wide), jnp.bfloat16),
            pltpu.VMEM((2 * heads, LANES, rows), jnp.bfloat16),
            pltpu.VMEM((2 * heads, rows, LANES), jnp.bfloat16),
            pltpu.VMEM((8, rows), jnp.float32),
            pltpu.VMEM((features, rows), jnp.float32),
            pltpu.SemaphoreType.DMA((count,)),
            pltpu.SemaphoreType.DMA((len(tops),)),
            pltpu.SemaphoreType.DMA,
        ],
        compiler_params=pltpu.CompilerParams(vmem_limit_bytes=56 << 20),
        name="attend_grad",
    )(query, outs, *pieces, *tops, hot, side, scale, weight)


def seen_factors(reachable, seg_query, off_query, segment, offset):
    segs = reachable.shape[0]
    labels = jnp.arange(LANES, dtype=jnp.int32)
    key_mark = jnp.where(labels < HDIM, segment[:, None], offset[:, None] + HDIM)
    hot = (key_mark == labels[None, :]).astype(jnp.bfloat16)
    query_hot = (labels[:, None] == seg_query[None, :]).astype(jnp.float32)
    wide = jnp.zeros((LANES, LANES), jnp.float32).at[:segs, :segs].set(reachable.T - jnp.eye(segs, dtype=jnp.float32))
    strict = jnp.dot(wide, query_hot, preferred_element_type=jnp.float32)
    same = query_hot
    before = ((labels[:, None] >= HDIM) & (labels[:, None] - HDIM <= off_query[None, :])).astype(jnp.float32)
    return hot, jnp.stack([strict, same, before]).astype(jnp.bfloat16)


def head_marks(features):
    row = lax.broadcasted_iota(jnp.int32, (features, LANES), 0) // HDIM
    column = lax.broadcasted_iota(jnp.int32, (features, LANES), 1)
    return (row == column).astype(jnp.float32).astype(jnp.bfloat16)


def wide_dot(values, marks, axis):
    high = values.astype(jnp.bfloat16)
    rest = (values - high.astype(jnp.float32)).astype(jnp.bfloat16)
    dims = (((1,), (axis,)), ((), ()))
    return lax.dot_general(
        high, marks, dims, preferred_element_type=jnp.float32
    ) + lax.dot_general(rest, marks, dims, preferred_element_type=jnp.float32)


def over_heads(values, marks):
    return wide_dot(values, marks, 0), lambda heads: wide_dot(heads, marks, 1)


def project_body(count, *refs):
    pieces, refs = refs[:count], refs[count:]
    weight_ref, scale_ref, query_out, tree_out, raw_out, group_out, group, sems, group_sem = refs
    both = raw_out.shape[1]
    features = both // 2
    step = pl.program_id(0)
    keep = pltpu.make_async_copy(group, group_out, group_sem)

    @pl.when(step == 0)
    def assemble():
        moves = copies(pieces, row_blocks(group, count), sems)
        for move in moves:
            move.wait()
        keep.start()

    @pl.when(step == pl.num_programs(0) - 1)
    def kept():
        keep.wait()

    tile = query_out.shape[0]
    product = jnp.dot(
        group[pl.ds(step * tile, tile)], weight_ref[:, : 3 * features], preferred_element_type=jnp.float32
    )
    raw = product[:, :both]
    sums, spread_heads = over_heads(raw * raw, head_marks(both))
    unit = raw * spread_heads(lax.rsqrt(sums + EPSILON))
    scaled = (unit * scale_ref[...]).astype(jnp.bfloat16)
    raw_out[...] = raw
    query_out[...] = scaled[:, :features]
    tree_out[...] = jnp.concatenate(
        [scaled[:, features:], product[:, both:].astype(jnp.bfloat16)], axis=1
    )


def project(pieces, weight, scale):
    count, width = len(pieces), pieces[0].shape[1]
    rows = pieces[0].shape[0] * count
    features = weight.shape[1] // 4
    tile = rows // 4
    whole = lambda step: (0, 0)
    block = lambda columns: pl.BlockSpec((tile, columns), lambda step: (step, 0))
    return pl.pallas_call(
        lambda *refs: project_body(count, *refs),
        grid=(4,),
        in_specs=[ANYWHERE] * count
        + [
            pl.BlockSpec(weight.shape, whole),
            pl.BlockSpec((1, 2 * features), whole),
        ],
        out_specs=[block(features), block(2 * features), block(2 * features), ANYWHERE],
        out_shape=[
            jax.ShapeDtypeStruct((rows, features), jnp.bfloat16),
            jax.ShapeDtypeStruct((rows, 2 * features), jnp.bfloat16),
            jax.ShapeDtypeStruct((rows, 2 * features), jnp.float32),
            jax.ShapeDtypeStruct((rows, width), jnp.bfloat16),
        ],
        scratch_shapes=[
            pltpu.VMEM((rows, width), jnp.bfloat16),
            pltpu.SemaphoreType.DMA((count,)),
            pltpu.SemaphoreType.DMA,
        ],
        compiler_params=pltpu.CompilerParams(vmem_limit_bytes=40 << 20),
        name="project",
    )(*pieces, weight, scale)


def project_grad_body(count, query_ref, *refs):
    tree_refs, refs = refs[:count], refs[count:]
    (raw_ref, weight_ref, scale_ref, low_out, scale_out), part_outs = refs[:5], refs[5:]
    step = pl.program_id(0)
    both = raw_ref.shape[1]
    features = both // 2
    tree = sum(ref[...].astype(jnp.float32) for ref in tree_refs)
    upstream = jnp.concatenate([query_ref[...], tree[:, :features]], axis=1)
    raw = raw_ref[...]
    marks = head_marks(both)
    sums, spread_heads = over_heads(raw * raw, marks)
    inverse = spread_heads(lax.rsqrt(sums + EPSILON))
    unit = raw * inverse
    scale_out[...] = jnp.sum(upstream * unit, axis=0, keepdims=True)[None]
    pulled = upstream * scale_ref[...]
    inner = spread_heads(over_heads(unit * pulled, marks)[0])
    grads = inverse * (pulled - unit * inner)
    low = jnp.concatenate([grads, tree[:, features:]], axis=1).astype(jnp.bfloat16)
    low_out[...] = low
    part = contract_cols(low, weight_ref[:, : 3 * features]).astype(jnp.bfloat16)
    for place, part_out in enumerate(part_outs):

        @pl.when((step == place) | (len(part_outs) == 1))
        def store():
            part_out[...] = part


def project_grad(query_grad, tree_parts, raw, weight, scale, count_out):
    rows, both = raw.shape
    width = weight.shape[0]
    features = both // 2
    tile = rows // 4
    whole = lambda step: (0, 0)
    block = lambda columns: pl.BlockSpec((tile, columns), lambda step: (step, 0))
    return pl.pallas_call(
        lambda *refs: project_grad_body(len(tree_parts), *refs),
        grid=(4,),
        in_specs=[block(features)]
        + [block(both) for part in tree_parts]
        + [block(both), pl.BlockSpec(weight.shape, whole), pl.BlockSpec((1, both), whole)],
        out_specs=[
            block(3 * features),
            pl.BlockSpec((1, 1, both), lambda step: (step, 0, 0)),
        ]
        + ([block(width)] if count_out == 1 else [pl.BlockSpec((tile, width), whole)] * 4),
        out_shape=[
            jax.ShapeDtypeStruct((rows, 3 * features), jnp.bfloat16),
            jax.ShapeDtypeStruct((4, 1, both), jnp.float32),
        ]
        + [jax.ShapeDtypeStruct((rows // count_out, width), jnp.bfloat16)] * count_out,
        compiler_params=pltpu.CompilerParams(vmem_limit_bytes=40 << 20),
        name="project_grad",
    )(query_grad, *tree_parts, raw, weight, scale)


def gated(up, gate, scale_up, scale_gate):
    raw = gate * (scale_gate * math.sqrt(D))
    curve = 1.0 / (1.0 + jnp.exp(-raw))
    return raw, curve, raw * curve, up * scale_up


def hidden_body(count, halves, *refs):
    pieces, refs = refs[:count], refs[count:]
    weights, refs = refs[:halves], refs[halves:]
    scale_ref, refs = refs[0], refs[1:]
    outs, refs = refs[:count], refs[count:]
    group_out, up_out, gate_out, mixed_out, group, matrices, total, sems, out_sem = refs
    half = up_out.shape[1] // halves
    moves = copies(pieces, row_blocks(group, count), sems)
    loads = [
        pltpu.make_async_copy(
            weights[place % halves].at[:, place // halves], matrices.at[place], sems.at[count + place]
        )
        for place in range(3 * halves)
    ]
    for load in loads:
        load.start()
    for move in moves:
        move.wait()
    keep = pltpu.make_async_copy(group, group_out, out_sem)
    keep.start()
    for place in range(halves):
        columns = slice(place * half, (place + 1) * half)
        for matrix in range(3):
            loads[matrix * halves + place].wait()
        tokens = group[...]
        up = contract_cols(tokens, matrices[place].reshape(half, -1))
        gate = contract_cols(tokens, matrices[halves + place].reshape(half, -1))
        up_out[:, columns] = up.astype(jnp.bfloat16)
        gate_out[:, columns] = gate.astype(jnp.bfloat16)
        raw, curve, silu, scaled = gated(up, gate, scale_ref[0:1, columns], scale_ref[1:2, columns])
        mixed = (scaled * silu).astype(jnp.bfloat16)
        mixed_out[:, columns] = mixed
        part = jnp.dot(
            mixed, matrices[2 * halves + place].reshape(half, -1), preferred_element_type=jnp.float32
        )
        total[...] = part if place == 0 else total[...] + part
    rows = group.shape[0] // count
    for place in range(count):
        outs[place][...] = total[place * rows : (place + 1) * rows].astype(jnp.bfloat16)
    keep.wait()


def hidden_forward(pieces, weights, scales):
    count, halves = len(pieces), len(weights)
    rows, width = pieces[0].shape[0] * count, pieces[0].shape[1]
    half = weights[0].shape[0] * weights[0].shape[2]
    hidden = half * halves
    low = lambda columns: jax.ShapeDtypeStruct((rows, columns), jnp.bfloat16)
    vmem = pl.BlockSpec(memory_space=pltpu.VMEM)
    return pl.pallas_call(
        lambda *refs: hidden_body(count, halves, *refs),
        in_specs=[ANYWHERE] * (count + halves) + [vmem],
        out_specs=[vmem] * count + [ANYWHERE] + [vmem] * 3,
        out_shape=[jax.ShapeDtypeStruct(piece.shape, jnp.bfloat16) for piece in pieces]
        + [low(width), low(hidden), low(hidden), low(hidden)],
        scratch_shapes=[
            pltpu.VMEM((rows, width), jnp.bfloat16),
            pltpu.VMEM((3 * halves, weights[0].shape[0]) + weights[0].shape[2:], jnp.bfloat16),
            pltpu.VMEM((rows, width), jnp.float32),
            pltpu.SemaphoreType.DMA((count + 3 * halves,)),
            pltpu.SemaphoreType.DMA,
        ],
        compiler_params=pltpu.CompilerParams(vmem_limit_bytes=52 << 20),
        name="hidden",
    )(*pieces, *weights, jnp.stack(scales))


def hidden_grad_body(count, halves, *refs):
    pieces, refs = refs[:count], refs[count:]
    weights, refs = refs[:halves], refs[halves:]
    scale_ref, up_ref, gate_ref = refs[:3]
    outs, refs = refs[3 : 3 + count], refs[3 + count :]
    group_out, up_out, gate_out, scale_out, group, matrices, total, sems, out_sem = refs
    half = up_out.shape[1] // halves
    moves = copies(pieces, row_blocks(group, count), sems)
    loads = [
        pltpu.make_async_copy(
            weights[place % halves].at[:, place // halves], matrices.at[place], sems.at[count + place]
        )
        for place in range(3 * halves)
    ]
    for load in loads:
        load.start()
    for move in moves:
        move.wait()
    keep = pltpu.make_async_copy(group, group_out, out_sem)
    keep.start()
    for place in range(halves):
        columns = slice(place * half, (place + 1) * half)
        for matrix in range(3):
            loads[matrix * halves + place].wait()
        pulled = contract_cols(group[...], matrices[2 * halves + place].reshape(half, -1))
        pulled = pulled.astype(jnp.bfloat16).astype(jnp.float32)
        up = up_ref[:, columns].astype(jnp.float32)
        gate = gate_ref[:, columns].astype(jnp.float32)
        scale_up, scale_gate = scale_ref[0:1, columns], scale_ref[1:2, columns]
        raw, curve, silu, scaled = gated(up, gate, scale_up, scale_gate)
        curved = pulled * silu
        up_low = (curved * scale_up).astype(jnp.bfloat16)
        bent = pulled * scaled * (curve * (1.0 + raw * (1.0 - curve)))
        gate_low = (bent * (scale_gate * math.sqrt(D))).astype(jnp.bfloat16)
        scale_out[0:1, columns] = jnp.sum(curved * up, axis=0, keepdims=True)
        scale_out[1:2, columns] = jnp.sum(bent * gate, axis=0, keepdims=True) * math.sqrt(D)
        up_out[:, columns] = up_low
        gate_out[:, columns] = gate_low
        part = jnp.dot(
            up_low, matrices[place].reshape(half, -1), preferred_element_type=jnp.float32
        )
        part = part + jnp.dot(
            gate_low, matrices[halves + place].reshape(half, -1), preferred_element_type=jnp.float32
        )
        total[...] = part if place == 0 else total[...] + part
    rows = group.shape[0] // count
    for place in range(count):
        outs[place][...] = total[place * rows : (place + 1) * rows].astype(jnp.bfloat16)
    keep.wait()


def hidden_backward(pieces, weights, scales, up, gate):
    count, halves = len(pieces), len(weights)
    rows, width = pieces[0].shape[0] * count, pieces[0].shape[1]
    half = weights[0].shape[0] * weights[0].shape[2]
    hidden = half * halves
    low = lambda columns: jax.ShapeDtypeStruct((rows, columns), jnp.bfloat16)
    vmem = pl.BlockSpec(memory_space=pltpu.VMEM)
    return pl.pallas_call(
        lambda *refs: hidden_grad_body(count, halves, *refs),
        in_specs=[ANYWHERE] * (count + halves) + [vmem] * 3,
        out_specs=[vmem] * count + [ANYWHERE] + [vmem] * 3,
        out_shape=[jax.ShapeDtypeStruct(piece.shape, jnp.bfloat16) for piece in pieces]
        + [low(width), low(hidden), low(hidden), jax.ShapeDtypeStruct((8, hidden), jnp.float32)],
        scratch_shapes=[
            pltpu.VMEM((rows, width), jnp.bfloat16),
            pltpu.VMEM((3 * halves, weights[0].shape[0]) + weights[0].shape[2:], jnp.bfloat16),
            pltpu.VMEM((rows, width), jnp.float32),
            pltpu.SemaphoreType.DMA((count + 3 * halves,)),
            pltpu.SemaphoreType.DMA,
        ],
        compiler_params=pltpu.CompilerParams(vmem_limit_bytes=56 << 20),
        name="hidden_grad",
    )(*pieces, *weights, jnp.stack(scales), up, gate)


def visibility(parents, slots, group_size):
    labels = jnp.arange(SEGS, dtype=jnp.int32)
    linked = (parents[:, None] == labels[None, :]).astype(jnp.float32)
    reachable = jnp.maximum(linked, jnp.eye(SEGS, dtype=jnp.float32))
    for doubling in range(SEGS.bit_length()):
        reachable = jnp.minimum(jnp.dot(reachable, reachable, precision=HIGHEST), 1.0)
    return seen_factors(reachable, *row_labels(slots, group_size))


def prepare_attention(packed, scale_both, pieces, parents, slots):
    rows = pieces[0].shape[0] * len(pieces)
    queries, tree_own, raw, group = project(pieces, packed, scale_both)
    return visibility(parents, slots, rows), queries, group_gather(tree_own, "ctx"), raw, group


def forward_attention(packed, prepared, count):
    seen, queries, tree, raw, group = prepared
    heads_low, inverse, *parts = attend(queries, tree, *seen, packed, count)
    return group_scatter(parts, "tp")[0], (group, seen, queries, tree, raw, heads_low, inverse)


def first_mix(tokens_own, branch_parts, alpha_attn, gates):
    tokens_wide = tokens_own.astype(jnp.float32)
    hidden_one, pull_in = jax.vjp(
        mix_rows, tokens_wide, total_wide(branch_parts), after(alpha_attn, *gates)
    )
    hidden_low = hidden_one.astype(jnp.bfloat16)
    return (hidden_one, pull_in), hidden_low, hidden_gather(hidden_low)


def second_mix(hidden_one, branch_parts, alpha_mlp, cotangent_own, gates):
    output_wide, pull_out = jax.vjp(
        mix_rows, hidden_one, total_wide(branch_parts), after(alpha_mlp, *gates)
    )
    hidden_direct, branch_grad, grad_alpha_mlp = pull_out(cotangent_own.astype(jnp.float32))
    branch_low = branch_grad.astype(jnp.bfloat16)
    kept = (output_wide.astype(jnp.bfloat16), hidden_direct, grad_alpha_mlp)
    return kept, branch_low, hidden_gather(branch_low)


def third_mix(pull_in, hidden_parts, hidden_direct, gates):
    hidden_grad = total_wide(hidden_parts) + after(hidden_direct, *gates)
    tokens_direct, branch_grad, grad_alpha_attn = pull_in(hidden_grad)
    return tokens_direct, branch_grad.astype(jnp.bfloat16), grad_alpha_attn


def backward_attention(packed, kept, tops, hops):
    group, seen, queries, tree, raw, heads_low, inverse = kept
    query_grads, *rest = attend_grad(queries, tops, heads_low, tree, *seen, inverse, packed)
    tree_parts, first = group_scatter(rest[:-1], "ctx", hops)
    return query_grads, tree_parts, (rest[-1], heads_low)


def backward_projection(packed, scale_both, kept, attended, tokens_direct, hops):
    group, raw = kept[0], kept[4]
    query_grads, tree_parts, heads_factors = attended
    count = lax.axis_size("tp") if lax.axis_size("tp") == 4 else 1
    low, scale_sums, *parts = project_grad(
        query_grads, tree_parts, raw, packed, scale_both, count
    )
    own_parts, first = group_scatter(parts, "tp", hops)
    grad_tokens = tokens_direct + total_wide(own_parts)
    features = scale_both.shape[1] // 2
    scale_sum = jnp.sum(scale_sums, axis=(0, 1))
    scale_sum = scale_sum[:features] + scale_sum[features:]
    return grad_tokens, ((group, low), heads_factors), scale_sum, first


def joint_product(factors):
    formers, latters = zip(*factors)
    return contract_rows(jnp.concatenate(formers, axis=0), jnp.concatenate(latters, axis=0))


def per_device(
    tokens,
    parents,
    slot_segment,
    w_query,
    w_key,
    w_value,
    w_attn_out,
    w_up,
    w_gate,
    w_down,
    alpha_attn,
    alpha_mlp,
    scale_qk,
    scale_up,
    scale_gate,
    cotangent,
):
    width = tokens.shape[-1]
    micros = range(tokens.shape[0])
    last = tokens.shape[0] - 1
    groups = [group_gather(tokens[0, 0], "tp")]
    packed = lax.all_gather(
        jnp.concatenate([w_query, w_key, w_value, w_attn_out.T], axis=1),
        SPREAD,
        axis=0,
        tiled=True,
    )
    scales = hidden_scales(scale_up, scale_gate)
    scale_both = jnp.concatenate([scale_qk, scale_qk])[None]
    blocks = hidden_blocks(w_up, w_gate, w_down)
    prepared = []
    gates = scales
    for m in micros:
        early = after(scale_both, *gates)
        prepared.append(
            prepare_attention(packed, early, groups[m], parents[m, 0], slot_segment[m, 0])
        )
        if m == last:
            break
        ahead = groups[m][len(groups[m]) // 2]
        groups.append(group_gather(after(tokens[m + 1, 0], ahead), "tp", prepared[m][1:2]))
        if m == 0:
            shards = hidden_shards(after(blocks, groups[1][-1]))
        tree = prepared[m][2]
        gates = (tree[len(tree) // 2], shards)
    if last == 0:
        shards = hidden_shards(blocks)
    weights = hidden_weights(shards)
    front = [forward_attention(packed, prepared[m], len(groups[m])) for m in micros]
    gates = ()
    opened, forwards, mixed, backwards, closed, tops = [], [], [], [], [], []
    for m in micros:
        kept, mark, pieces = first_mix(tokens[m, 0], front[m][0], alpha_attn, gates)
        gates = (mark,)
        count = len(pieces)
        outs = hidden_forward(pieces, weights, scales)
        opened.append(kept)
        forwards.append((hidden_scatter(outs[:count]), outs[count:]))
    for m in micros:
        kept, mark, pieces = second_mix(
            opened[m][0], forwards[m][0], alpha_mlp, cotangent[m, 0], gates
        )
        gates = (mark,)
        up, gate = forwards[m][1][1:3]
        outs = hidden_backward(pieces, weights, scales, up, gate)
        mixed.append(kept)
        backwards.append((hidden_scatter(outs[:count]), outs[count:]))
    joined = []
    for m in micros:
        hidden_group, hidden_mixed = forwards[m][1][0], forwards[m][1][3]
        top_group, up_low, gate_low = backwards[m][1][:3]
        joined.append(((up_low, hidden_group), (gate_low, hidden_group), (hidden_mixed, top_group)))
    products = [
        joint_product([joined[m][place] for m in micros]).astype(jnp.bfloat16)
        for place in range(3)
    ]
    for m in micros:
        closed.append(
            third_mix(
                opened[m][1],
                backwards[m][0],
                mixed[m][1],
                gates,
            )
        )
        gates = (closed[-1][1],)
        tops.append(group_gather(closed[-1][1], "tp", products if m == last else ()))
    lines = core_sums(products)
    line_sums = hidden_line_sums([after(line, *[top[-1] for top in tops]) for line in lines])
    packed_sums = hidden_pack(line_sums)
    spread_sums = hidden_spread(packed_sums)
    attended = [backward_attention(packed, front[m][1], tops[m], 1) for m in micros]
    vectors = vector_sums(
        after(
            sum(jnp.concatenate([closed[m][2], mixed[m][2]]) for m in micros), attended[-1][0]
        ),
        sum(backwards[m][1][3][:2] for m in micros),
    )
    gates = ()
    back = []
    for m in micros:
        back.append(
            backward_projection(
                packed,
                after(scale_both, *gates),
                front[m][1],
                attended[m],
                closed[m][0],
                1 if m == last else 2,
            )
        )
        gates = (back[-1][3], packed_sums, vectors)
    product = jnp.concatenate(
        [joint_product([back[m][1][place] for m in micros]) for place in range(2)], axis=1
    )
    grad_attention = owner_scatter(product.astype(jnp.bfloat16))
    grad_q, grad_k, grad_v, grad_o = jnp.split(grad_attention, 4, axis=1)
    grad_u, grad_g, grad_d = hidden_weight_grads(spread_sums)
    sums = butterfly(jnp.concatenate([vectors, sum(back[m][2] for m in micros)]), SPREAD)
    sum_alphas, sum_hidden, sum_qk = jnp.split(sums, [2 * width, sums.shape[0] - scale_qk.shape[0]])
    sum_up, sum_gate = jnp.split(sum_hidden, 2)
    return (
        jnp.stack([mixed[m][0] for m in micros])[:, None],
        jnp.stack([back[m][0] for m in micros])[:, None],
        grad_q,
        grad_k,
        grad_v,
        grad_o.T,
        grad_u.T,
        grad_g.T,
        grad_d,
        sum_alphas[:width],
        sum_alphas[width:],
        sum_qk,
        sum_up,
        sum_gate,
    )


def solution(mesh):
    return jax.shard_map(
        per_device,
        mesh=mesh,
        in_specs=(
            P(None, "shard", ("ctx", "tp"), None),
            P(None, "shard", None),
            P(None, "shard", None),
            P(("shard", "ctx"), "tp"),
            P(("shard", "ctx"), "tp"),
            P(("shard", "ctx"), "tp"),
            P("tp", ("shard", "ctx")),
            P(("shard", "ctx"), "tp"),
            P(("shard", "ctx"), "tp"),
            P("tp", ("shard", "ctx")),
            P(),
            P(),
            P("tp"),
            P("tp"),
            P("tp"),
            P(None, "shard", ("ctx", "tp"), None),
        ),
        out_specs=(
            P(None, "shard", ("ctx", "tp"), None),
            P(None, "shard", ("ctx", "tp"), None),
            P(("shard", "ctx"), "tp"),
            P(("shard", "ctx"), "tp"),
            P(("shard", "ctx"), "tp"),
            P("tp", ("shard", "ctx")),
            P(("shard", "ctx"), "tp"),
            P(("shard", "ctx"), "tp"),
            P("tp", ("shard", "ctx")),
            P(),
            P(),
            P("tp"),
            P("tp"),
            P("tp"),
        ),
        check_vma=False,
    )
```

```python
import math

import jax
import jax.numpy as jnp
from jax import lax
from jax.experimental import pallas as pl
from jax.experimental.pallas import tpu as pltpu
from jax.sharding import PartitionSpec as P

D = 1280
HDIM = 64
SEG = 64
SEGS = 40
TREE_TOK = 2560


EPSILON = 1e-06
HIGHEST = lax.Precision.HIGHEST
SPREAD = ("shard", "ctx")


def unit_rows(values):
    return values * lax.rsqrt(jnp.sum(values * values, axis=-1, keepdims=True) + EPSILON)


def contract_rows(former, latter):
    return lax.dot_general(
        former, latter, (((0,), (0,)), ((), ())), preferred_element_type=jnp.float32
    )


def contract_cols(former, latter):
    return lax.dot_general(
        former, latter, (((1,), (1,)), ((), ())), preferred_element_type=jnp.float32
    )


def mix_rows(residual, branch, mixing):
    return unit_rows(residual + mixing * (unit_rows(branch) - residual))


def swap(value, axis, bit):
    size = lax.axis_size(axis)
    return lax.ppermute(value, axis, [(place, place ^ bit) for place in range(size)])


def after(value, *others):
    for other in others:
        value = value + (other[(slice(0, 1),) * other.ndim].reshape(()) * 0).astype(value.dtype)
    return value


def add_low(former, latter):
    return (former.astype(jnp.float32) + latter.astype(jnp.float32)).astype(jnp.bfloat16)


def butterfly(value, axes):
    for axis in axes:
        bit = 1
        while bit < lax.axis_size(axis):
            value = value + swap(value, axis, bit)
            bit *= 2
    return value


def group_order(axis):
    size = lax.axis_size(axis)
    places = jnp.arange(size, dtype=jnp.int32)
    return places ^ lax.axis_index(axis) if size == 4 else places


def group_gather(own_block, axis, gates=None):
    if lax.axis_size(axis) != 4:
        return [lax.all_gather(own_block, axis, axis=0, tiled=True)]
    across = swap(own_block, axis, 2)
    beside = swap(own_block, axis, 1)
    source = across if gates is None else after(across, beside, *gates)
    return [own_block, beside, across, swap(source, axis, 1)]


def group_scatter(pieces, axis, hops=2):
    if lax.axis_size(axis) != 4:
        parts = [lax.psum_scatter(pieces[0], axis, scatter_dimension=0, tiled=True)]
        return parts, parts[0]
    own, beside, across, far = pieces
    if hops == 1:
        parts = [swap(piece, axis, bits) for piece, bits in zip(pieces[1:], (1, 2, 3))]
        return [own] + parts, parts[0]
    far = swap(far, axis, 1)
    across = swap(add_low(across, far), axis, 2)
    return [own, swap(after(beside, far), axis, 1), across], far


def total_wide(parts):
    return sum(part.astype(jnp.float32) for part in parts)


def in_plane():
    return (lax.axis_size("shard"), lax.axis_size("ctx"), lax.axis_size("tp")) == (2, 4, 4)


def hop(value, bits):
    return lax.ppermute(value, SPREAD, [(place, place ^ bits) for place in range(8)])


def hidden_gather(own_block):
    if not in_plane():
        return group_gather(own_block, "tp")
    return [own_block] + [hop(own_block, bits) for bits in (2, 4, 6)]


def hidden_scatter(pieces):
    if not in_plane():
        return group_scatter(pieces, "tp")[0]
    return [pieces[0]] + [hop(piece, bits) for piece, bits in zip(pieces[1:], (2, 4, 6))]


def hidden_blocks(w_up, w_gate, w_down):
    if not in_plane():
        return jnp.stack([w_up.T, w_gate.T, w_down])
    rows, hidden = w_up.shape
    part = hidden // 8
    packed = jnp.stack(
        [
            w_up.reshape(rows, 8, part).transpose(1, 2, 0),
            w_gate.reshape(rows, 8, part).transpose(1, 2, 0),
            w_down.reshape(8, part, rows),
        ],
        axis=1,
    )
    return lax.all_to_all(packed, SPREAD, 0, 0)


def hidden_shards(blocks):
    if not in_plane():
        return blocks
    rows = blocks.shape[2]
    return blocks.transpose(1, 2, 0, 3).reshape(3, rows, -1)


def hidden_weights(shards):
    if not in_plane():
        return [lax.all_gather(shards, SPREAD, axis=2, tiled=True)[None]]
    line = lax.all_gather(shards, "tp", axis=0)
    return [line, swap(line, "ctx", 1)]


def hidden_scales(*scales):
    if not in_plane():
        return scales
    part = scales[0].shape[0] // 8
    first = lax.axis_index(SPREAD) * part
    own = jnp.stack([lax.dynamic_slice_in_dim(scale, first, part) for scale in scales])
    line = jnp.concatenate(group_gather(own[None], "tp"), axis=0)
    line = jnp.take(line, group_order("tp"), axis=0)
    both = jnp.concatenate([line, swap(line, "ctx", 1)], axis=0)
    return tuple(both[:, place].reshape(-1) for place in range(len(scales)))


def core_sums(products):
    if not in_plane():
        return products
    half = products[0].shape[0] // 2
    return [add_low(product[:half], swap(product[half:], "ctx", 1)) for product in products]


def hidden_line_sums(lines):
    if not in_plane():
        return lines
    return [lax.psum_scatter(line, "tp", scatter_dimension=0, tiled=True) for line in lines]


def hidden_pack(sums):
    if not in_plane():
        return jnp.stack(sums)
    part, width = sums[0].shape
    return jnp.stack([total.reshape(part, 8, width // 8).transpose(1, 0, 2) for total in sums], 1)


def hidden_spread(packed):
    if not in_plane():
        return lax.psum_scatter(packed, SPREAD, scatter_dimension=2, tiled=True)
    return lax.all_to_all(packed, SPREAD, 0, 0)


def hidden_weight_grads(spread_sums):
    wide = spread_sums.astype(jnp.float32)
    if not in_plane():
        return [wide[place] for place in range(3)]
    return [wide[:, place].reshape(-1, wide.shape[-1]) for place in range(3)]


def vector_sums(alphas, hidden_sums):
    count, hidden = hidden_sums.shape
    if not in_plane():
        return jnp.concatenate([butterfly(alphas, ("tp",)), hidden_sums.reshape(-1)])
    parts = hidden_sums.reshape(count, 2, 4, hidden // 8)
    line = (parts[:, 0] + swap(parts[:, 1], "ctx", 1)).reshape(-1)
    width = alphas.shape[0]
    both = butterfly(jnp.concatenate([alphas, line]), ("tp",))
    line = both[width:].reshape(count, 4, hidden // 8)
    line = lax.dynamic_index_in_dim(line, lax.axis_index("tp"), 1, keepdims=True)
    blank = jnp.zeros((count, 8, hidden // 8), jnp.float32)
    placed = lax.dynamic_update_slice_in_dim(blank, line, lax.axis_index(SPREAD), 1)
    return jnp.concatenate([both[:width], placed.reshape(-1)])


def owner_scatter(product_low):
    if not in_plane():
        total = lax.psum_scatter(product_low, SPREAD, scatter_dimension=0, tiled=True)
        return total.astype(jnp.float32)
    place = lax.axis_index("ctx")
    core, along, plane = place % 2, place // 2, lax.axis_index("shard")
    rows, width = product_low.shape
    blocks = product_low.reshape(4, 2, rows // 8, width)

    def of_core(which):
        return lax.dynamic_index_in_dim(blocks, which, 1, keepdims=False)

    blocks = add_low(of_core(core), swap(of_core(1 - core), "ctx", 1))
    chip = plane * 2 + along

    def of_chip(bits):
        return lax.dynamic_index_in_dim(blocks, chip ^ bits, 0, keepdims=False)

    return total_wide([of_chip(0)] + [hop(of_chip(bits), 2 * bits) for bits in (1, 2, 3)])


def row_labels(slots, group_size):
    tree_rows = group_size * lax.axis_size("ctx")
    chunk = group_size // lax.axis_size("tp")
    within = (group_order("tp")[:, None] * chunk + jnp.arange(chunk, dtype=jnp.int32)).reshape(-1)
    keys = (group_order("ctx")[:, None] * group_size + within[None, :]).reshape(-1)
    onehot = (keys[:, None] // SEG == jnp.arange(tree_rows // SEG, dtype=jnp.int32)[None, :])
    segment = jnp.sum(jnp.where(onehot, slots[None, :], 0), axis=1)
    offset = keys % SEG
    if lax.axis_size("ctx") != 4:
        first = lax.axis_index("ctx") * group_size
    else:
        first = 0
    return (
        lax.dynamic_slice_in_dim(segment, first, group_size),
        lax.dynamic_slice_in_dim(offset, first, group_size),
        segment,
        offset,
    )


LOG2_SCALE = math.sqrt(HDIM) * math.log2(math.e)
LANES = 128
KEY_TILE = 1280
GRAD_TILE = 640


def copies(sources, targets, sems):
    moves = [
        pltpu.make_async_copy(source, target, sems.at[place])
        for place, (source, target) in enumerate(zip(sources, targets))
    ]
    for move in moves:
        move.start()
    return moves


def row_blocks(ref, count):
    rows = ref.shape[0] // count
    return [ref.at[pl.ds(place * rows, rows)] for place in range(count)]


ANYWHERE = pl.BlockSpec(memory_space=pl.ANY)


def half_kept(value, unit, axis):
    place = lax.broadcasted_iota(jnp.int32, value.shape, axis)
    inside = (place >= HDIM) if unit % 2 else (place < HDIM)
    return jnp.where(inside, value, jnp.zeros_like(value))


def seen_tile(hot_ref, side_ref):
    hot = hot_ref[...]
    strict = jnp.dot(hot, side_ref[0], preferred_element_type=jnp.float32)
    same = jnp.dot(hot, side_ref[1], preferred_element_type=jnp.float32)
    before = jnp.dot(hot, side_ref[2], preferred_element_type=jnp.float32)
    return (strict + same * before).astype(jnp.bfloat16)


def pair_of(unit):
    return slice(unit // 2 * LANES, unit // 2 * LANES + LANES)


def attend_body(count, query_ref, *refs):
    pieces, refs = refs[:count], refs[count:]
    (hot_ref, side_ref, weight_ref, out_ref, scale_ref), refs = refs[:5], refs[5:]
    outs, (tree_ref, turned_ref, sum_ref, sems) = refs[:-4], refs[-4:]
    heads = query_ref.shape[1] // HDIM
    step = pl.program_id(0)

    @pl.when(step == 0)
    def prepare():
        moves = copies(pieces, row_blocks(tree_ref, count), sems)
        turned = query_ref[...].astype(jnp.float32).T.astype(jnp.bfloat16)
        blank = jnp.zeros((HDIM, turned.shape[1]), jnp.bfloat16)
        for head in range(heads):
            own = turned[head * HDIM : (head + 1) * HDIM]
            halves = [blank, own] if head % 2 else [own, blank]
            turned_ref[head] = jnp.concatenate(halves, axis=0)
        sum_ref[...] = jnp.zeros_like(sum_ref)
        for move in moves:
            move.wait()

    tree = tree_ref[pl.ds(step * KEY_TILE, KEY_TILE)]
    values_turned = tree[:, heads * HDIM :].astype(jnp.float32).T.astype(jnp.bfloat16)
    seen = seen_tile(hot_ref, side_ref)
    ones = jnp.ones((sum_ref.shape[1] - HDIM, tree.shape[0]), jnp.bfloat16)
    for head in range(heads):
        scores = jnp.dot(tree[:, pair_of(head)], turned_ref[head], preferred_element_type=jnp.float32)
        lifted = jnp.exp2(scores * LOG2_SCALE).astype(jnp.bfloat16) * seen
        own = jnp.concatenate([values_turned[head * HDIM : (head + 1) * HDIM], ones], axis=0)
        sum_ref[head] += jnp.dot(own, lifted, preferred_element_type=jnp.float32)

    @pl.when(step == pl.num_programs(0) - 1)
    def finish():
        parts = []
        for head in range(heads):
            inverse = 1.0 / sum_ref[head, HDIM : HDIM + 1]
            scale_ref[head : head + 1] = inverse
            parts.append(sum_ref[head, :HDIM] * inverse)
        low = jnp.concatenate(parts, axis=0).T.astype(jnp.bfloat16)
        out_ref[...] = low
        width = low.shape[1]
        rows = low.shape[0] // len(outs)
        for place, out in enumerate(outs):
            out[...] = contract_cols(
                low[place * rows : (place + 1) * rows], weight_ref[:, 3 * width :]
            ).astype(jnp.bfloat16)


def attend(query, pieces, hot, side, weight, count_out):
    rows, features = query.shape
    wide = weight.shape[0]
    count, width = len(pieces), pieces[0].shape[1]
    keys = pieces[0].shape[0] * count
    heads = features // HDIM
    whole = lambda step: (0, 0)
    return pl.pallas_call(
        lambda *refs: attend_body(count, *refs),
        grid=(keys // KEY_TILE,),
        in_specs=[pl.BlockSpec((rows, features), whole)]
        + [ANYWHERE] * count
        + [
            pl.BlockSpec((KEY_TILE, LANES), lambda step: (step, 0)),
            pl.BlockSpec((3, LANES, rows), lambda step: (0, 0, 0)),
            pl.BlockSpec(weight.shape, whole),
        ],
        out_specs=[
            pl.BlockSpec((rows, features), whole),
            pl.BlockSpec((8, rows), whole),
        ]
        + [pl.BlockSpec((rows // count_out, wide), whole)] * count_out,
        out_shape=[
            jax.ShapeDtypeStruct((rows, features), jnp.bfloat16),
            jax.ShapeDtypeStruct((8, rows), jnp.float32),
        ]
        + [jax.ShapeDtypeStruct((rows // count_out, wide), jnp.bfloat16)] * count_out,
        scratch_shapes=[
            pltpu.VMEM((keys, width), jnp.bfloat16),
            pltpu.VMEM((heads, LANES, rows), jnp.bfloat16),
            pltpu.VMEM((heads, HDIM + 16, rows), jnp.float32),
            pltpu.SemaphoreType.DMA((count,)),
        ],
        compiler_params=pltpu.CompilerParams(vmem_limit_bytes=48 << 20),
        name="attend",
    )(query, *pieces, hot, side, weight)


def attend_grad_body(count, tops, query_ref, heads_ref, *refs):
    pieces, refs = refs[:count], refs[count:]
    top_refs, refs = refs[:tops], refs[tops:]
    (hot_ref, side_ref, scale_ref, weight_ref, query_out), refs = refs[:5], refs[5:]
    outs, refs = refs[:count], refs[count:]
    group_out, tree_ref, tree_out, group, turned_ref, plain_ref, delta_ref, sum_ref = refs[:8]
    sems, top_sems, group_sem = refs[8:]
    heads = heads_ref.shape[1] // HDIM
    units = 2 * heads
    step = pl.program_id(0)

    @pl.when(step == 0)
    def prepare():
        moves = copies(pieces, row_blocks(tree_ref, count), sems)
        gathers = copies(top_refs, row_blocks(group, tops), top_sems)
        for gather in gathers:
            gather.wait()
        keep = pltpu.make_async_copy(group, group_out, group_sem)
        keep.start()
        features = query_ref.shape[1]
        upstream = jnp.dot(
            group[...], weight_ref[:, 3 * features :], preferred_element_type=jnp.float32
        )
        both = jnp.concatenate([query_ref[...], upstream.astype(jnp.bfloat16)], axis=1)
        turned = both.astype(jnp.float32).T
        kept = heads_ref[...].astype(jnp.float32).T
        blank = jnp.zeros((HDIM, turned.shape[1]), jnp.bfloat16)
        for unit in range(units):
            own = turned[unit * HDIM : (unit + 1) * HDIM].astype(jnp.bfloat16)
            halves = [blank, own] if unit % 2 else [own, blank]
            turned_ref[unit] = jnp.concatenate(halves, axis=0)
            plain_ref[unit] = half_kept(both[:, pair_of(unit)], unit, 1)
        for head in range(heads):
            rows = slice(head * HDIM, (head + 1) * HDIM)
            pulled = turned[(heads + head) * HDIM : (heads + head + 1) * HDIM]
            delta_ref[head : head + 1] = jnp.sum(kept[rows] * pulled, axis=0, keepdims=True)
        sum_ref[...] = jnp.zeros_like(sum_ref)
        for move in moves:
            move.wait()
        keep.wait()

    here = pl.ds(step * GRAD_TILE, GRAD_TILE)
    tree = tree_ref[here]
    keys_turned = tree[:, : heads * HDIM].astype(jnp.float32).T.astype(jnp.bfloat16)
    seen = seen_tile(hot_ref, side_ref)
    weights, slopes = [], []
    for head in range(heads):
        scores = jnp.dot(tree[:, pair_of(head)], turned_ref[head], preferred_element_type=jnp.float32)
        weight = jnp.exp2(scores * LOG2_SCALE) * scale_ref[head : head + 1]
        pull = jnp.dot(
            tree[:, pair_of(heads + head)], turned_ref[heads + head], preferred_element_type=jnp.float32
        )
        slope = (weight * (pull - delta_ref[head : head + 1])).astype(jnp.bfloat16) * seen
        rows = slice(head * HDIM, (head + 1) * HDIM)
        sum_ref[rows] += jnp.dot(keys_turned[rows], slope, preferred_element_type=jnp.float32)
        weights.append(weight.astype(jnp.bfloat16) * seen)
        slopes.append(slope)
    terms = slopes + weights
    score_scale = math.sqrt(HDIM)
    for pair in range(heads):
        total = 0.0
        for unit in (2 * pair, 2 * pair + 1):
            part = jnp.dot(terms[unit], plain_ref[unit], preferred_element_type=jnp.float32)
            total = total + (part * score_scale if unit < heads else part)
        tree_out[here, pair * LANES : (pair + 1) * LANES] = total.astype(jnp.bfloat16)

    @pl.when(step == pl.num_programs(0) - 1)
    def finish():
        moves = copies(row_blocks(tree_out, count), outs, sems)
        query_out[...] = sum_ref[...].T * score_scale
        for move in moves:
            move.wait()


def attend_grad(query, tops, outs, pieces, hot, side, scale, weight):
    rows, features = query.shape
    wide = weight.shape[0]
    count, width = len(pieces), pieces[0].shape[1]
    keys = pieces[0].shape[0] * count
    heads = features // HDIM
    whole = lambda step: (0, 0)
    return pl.pallas_call(
        lambda *refs: attend_grad_body(count, len(tops), *refs),
        grid=(keys // GRAD_TILE,),
        in_specs=[pl.BlockSpec((rows, features), whole)] * 2
        + [ANYWHERE] * (count + len(tops))
        + [
            pl.BlockSpec((GRAD_TILE, LANES), lambda step: (step, 0)),
            pl.BlockSpec((3, LANES, rows), lambda step: (0, 0, 0)),
            pl.BlockSpec((8, rows), whole),
            pl.BlockSpec(weight.shape, whole),
        ],
        out_specs=[pl.BlockSpec((rows, features), whole)] + [ANYWHERE] * (count + 1),
        out_shape=[jax.ShapeDtypeStruct((rows, features), jnp.float32)]
        + [jax.ShapeDtypeStruct(piece.shape, jnp.bfloat16) for piece in pieces]
        + [jax.ShapeDtypeStruct((rows, wide), jnp.bfloat16)],
        scratch_shapes=[
            pltpu.VMEM((keys, width), jnp.bfloat16),
            pltpu.VMEM((keys, width), jnp.bfloat16),
            pltpu.VMEM((rows, wide), jnp.bfloat16),
            pltpu.VMEM((2 * heads, LANES, rows), jnp.bfloat16),
            pltpu.VMEM((2 * heads, rows, LANES), jnp.bfloat16),
            pltpu.VMEM((8, rows), jnp.float32),
            pltpu.VMEM((features, rows), jnp.float32),
            pltpu.SemaphoreType.DMA((count,)),
            pltpu.SemaphoreType.DMA((len(tops),)),
            pltpu.SemaphoreType.DMA,
        ],
        compiler_params=pltpu.CompilerParams(vmem_limit_bytes=56 << 20),
        name="attend_grad",
    )(query, outs, *pieces, *tops, hot, side, scale, weight)


def seen_factors(reachable, seg_query, off_query, segment, offset):
    segs = reachable.shape[0]
    labels = jnp.arange(LANES, dtype=jnp.int32)
    key_mark = jnp.where(labels < HDIM, segment[:, None], offset[:, None] + HDIM)
    hot = (key_mark == labels[None, :]).astype(jnp.bfloat16)
    query_hot = (labels[:, None] == seg_query[None, :]).astype(jnp.float32)
    wide = jnp.zeros((LANES, LANES), jnp.float32).at[:segs, :segs].set(reachable.T - jnp.eye(segs, dtype=jnp.float32))
    strict = jnp.dot(wide, query_hot, preferred_element_type=jnp.float32)
    same = query_hot
    before = ((labels[:, None] >= HDIM) & (labels[:, None] - HDIM <= off_query[None, :])).astype(jnp.float32)
    return hot, jnp.stack([strict, same, before]).astype(jnp.bfloat16)


def hold(value, *gates):
    return pl.pallas_call(
        lambda *refs: None,
        in_specs=[ANYWHERE] * (1 + len(gates)),
        out_specs=ANYWHERE,
        out_shape=jax.ShapeDtypeStruct(value.shape, value.dtype),
        input_output_aliases={0: 0},
        name="hold",
    )(value, *gates)


def head_marks(features):
    row = lax.broadcasted_iota(jnp.int32, (features, LANES), 0) // HDIM
    column = lax.broadcasted_iota(jnp.int32, (features, LANES), 1)
    return (row == column).astype(jnp.float32).astype(jnp.bfloat16)


def wide_dot(values, marks, axis):
    high = values.astype(jnp.bfloat16)
    rest = (values - high.astype(jnp.float32)).astype(jnp.bfloat16)
    dims = (((1,), (axis,)), ((), ()))
    return lax.dot_general(
        high, marks, dims, preferred_element_type=jnp.float32
    ) + lax.dot_general(rest, marks, dims, preferred_element_type=jnp.float32)


def over_heads(values, marks):
    return wide_dot(values, marks, 0), lambda heads: wide_dot(heads, marks, 1)


def project_body(count, *refs):
    pieces, refs = refs[:count], refs[count:]
    weight_ref, scale_ref, query_out, tree_out, raw_out, group_out, group, sems, group_sem = refs
    both = raw_out.shape[1]
    features = both // 2
    step = pl.program_id(0)
    keep = pltpu.make_async_copy(group, group_out, group_sem)

    @pl.when(step == 0)
    def assemble():
        moves = copies(pieces, row_blocks(group, count), sems)
        for move in moves:
            move.wait()
        keep.start()

    @pl.when(step == pl.num_programs(0) - 1)
    def kept():
        keep.wait()

    tile = query_out.shape[0]
    product = jnp.dot(
        group[pl.ds(step * tile, tile)], weight_ref[:, : 3 * features], preferred_element_type=jnp.float32
    )
    raw = product[:, :both]
    sums, spread_heads = over_heads(raw * raw, head_marks(both))
    unit = raw * spread_heads(lax.rsqrt(sums + EPSILON))
    scaled = (unit * scale_ref[...]).astype(jnp.bfloat16)
    raw_out[...] = raw
    query_out[...] = scaled[:, :features]
    tree_out[...] = jnp.concatenate(
        [scaled[:, features:], product[:, both:].astype(jnp.bfloat16)], axis=1
    )


def project(pieces, weight, scale):
    count, width = len(pieces), pieces[0].shape[1]
    rows = pieces[0].shape[0] * count
    features = weight.shape[1] // 4
    tile = rows // 4
    whole = lambda step: (0, 0)
    block = lambda columns: pl.BlockSpec((tile, columns), lambda step: (step, 0))
    return pl.pallas_call(
        lambda *refs: project_body(count, *refs),
        grid=(4,),
        in_specs=[ANYWHERE] * count
        + [
            pl.BlockSpec(weight.shape, whole),
            pl.BlockSpec((1, 2 * features), whole),
        ],
        out_specs=[block(features), block(2 * features), block(2 * features), ANYWHERE],
        out_shape=[
            jax.ShapeDtypeStruct((rows, features), jnp.bfloat16),
            jax.ShapeDtypeStruct((rows, 2 * features), jnp.bfloat16),
            jax.ShapeDtypeStruct((rows, 2 * features), jnp.float32),
            jax.ShapeDtypeStruct((rows, width), jnp.bfloat16),
        ],
        scratch_shapes=[
            pltpu.VMEM((rows, width), jnp.bfloat16),
            pltpu.SemaphoreType.DMA((count,)),
            pltpu.SemaphoreType.DMA,
        ],
        compiler_params=pltpu.CompilerParams(vmem_limit_bytes=40 << 20),
        name="project",
    )(*pieces, weight, scale)


def project_grad_body(count, query_ref, *refs):
    tree_refs, refs = refs[:count], refs[count:]
    (raw_ref, weight_ref, scale_ref, low_out, scale_out), part_outs = refs[:5], refs[5:]
    step = pl.program_id(0)
    both = raw_ref.shape[1]
    features = both // 2
    tree = sum(ref[...].astype(jnp.float32) for ref in tree_refs)
    upstream = jnp.concatenate([query_ref[...], tree[:, :features]], axis=1)
    raw = raw_ref[...]
    marks = head_marks(both)
    sums, spread_heads = over_heads(raw * raw, marks)
    inverse = spread_heads(lax.rsqrt(sums + EPSILON))
    unit = raw * inverse
    scale_out[...] = jnp.sum(upstream * unit, axis=0, keepdims=True)[None]
    pulled = upstream * scale_ref[...]
    inner = spread_heads(over_heads(unit * pulled, marks)[0])
    grads = inverse * (pulled - unit * inner)
    low = jnp.concatenate([grads, tree[:, features:]], axis=1).astype(jnp.bfloat16)
    low_out[...] = low
    part = contract_cols(low, weight_ref[:, : 3 * features]).astype(jnp.bfloat16)
    for place, part_out in enumerate(part_outs):

        @pl.when((step == place) | (len(part_outs) == 1))
        def store():
            part_out[...] = part


def project_grad(query_grad, tree_parts, raw, weight, scale, count_out):
    rows, both = raw.shape
    width = weight.shape[0]
    features = both // 2
    tile = rows // 4
    whole = lambda step: (0, 0)
    block = lambda columns: pl.BlockSpec((tile, columns), lambda step: (step, 0))
    return pl.pallas_call(
        lambda *refs: project_grad_body(len(tree_parts), *refs),
        grid=(4,),
        in_specs=[block(features)]
        + [block(both) for part in tree_parts]
        + [block(both), pl.BlockSpec(weight.shape, whole), pl.BlockSpec((1, both), whole)],
        out_specs=[
            block(3 * features),
            pl.BlockSpec((1, 1, both), lambda step: (step, 0, 0)),
        ]
        + ([block(width)] if count_out == 1 else [pl.BlockSpec((tile, width), whole)] * 4),
        out_shape=[
            jax.ShapeDtypeStruct((rows, 3 * features), jnp.bfloat16),
            jax.ShapeDtypeStruct((4, 1, both), jnp.float32),
        ]
        + [jax.ShapeDtypeStruct((rows // count_out, width), jnp.bfloat16)] * count_out,
        compiler_params=pltpu.CompilerParams(vmem_limit_bytes=40 << 20),
        name="project_grad",
    )(query_grad, *tree_parts, raw, weight, scale)


def gated(up, gate, scale_up, scale_gate):
    raw = gate * (scale_gate * math.sqrt(D))
    curve = 1.0 / (1.0 + jnp.exp(-raw))
    return raw, curve, raw * curve, up * scale_up


def hidden_body(count, halves, *refs):
    pieces, refs = refs[:count], refs[count:]
    weights, refs = refs[:halves], refs[halves:]
    scale_ref, refs = refs[0], refs[1:]
    outs, refs = refs[:count], refs[count:]
    group_out, up_out, gate_out, mixed_out, group, matrices, total, sems, out_sem = refs
    half = up_out.shape[1] // halves
    moves = copies(pieces, row_blocks(group, count), sems)
    loads = [
        pltpu.make_async_copy(
            weights[place % halves].at[:, place // halves], matrices.at[place], sems.at[count + place]
        )
        for place in range(3 * halves)
    ]
    for load in loads:
        load.start()
    for move in moves:
        move.wait()
    keep = pltpu.make_async_copy(group, group_out, out_sem)
    keep.start()
    for place in range(halves):
        columns = slice(place * half, (place + 1) * half)
        for matrix in range(3):
            loads[matrix * halves + place].wait()
        tokens = group[...]
        up = contract_cols(tokens, matrices[place].reshape(half, -1))
        gate = contract_cols(tokens, matrices[halves + place].reshape(half, -1))
        up_out[:, columns] = up.astype(jnp.bfloat16)
        gate_out[:, columns] = gate.astype(jnp.bfloat16)
        raw, curve, silu, scaled = gated(up, gate, scale_ref[0:1, columns], scale_ref[1:2, columns])
        mixed = (scaled * silu).astype(jnp.bfloat16)
        mixed_out[:, columns] = mixed
        part = jnp.dot(
            mixed, matrices[2 * halves + place].reshape(half, -1), preferred_element_type=jnp.float32
        )
        total[...] = part if place == 0 else total[...] + part
    rows = group.shape[0] // count
    for place in range(count):
        outs[place][...] = total[place * rows : (place + 1) * rows].astype(jnp.bfloat16)
    keep.wait()


def hidden_forward(pieces, weights, scales):
    count, halves = len(pieces), len(weights)
    rows, width = pieces[0].shape[0] * count, pieces[0].shape[1]
    half = weights[0].shape[0] * weights[0].shape[2]
    hidden = half * halves
    low = lambda columns: jax.ShapeDtypeStruct((rows, columns), jnp.bfloat16)
    vmem = pl.BlockSpec(memory_space=pltpu.VMEM)
    return pl.pallas_call(
        lambda *refs: hidden_body(count, halves, *refs),
        in_specs=[ANYWHERE] * (count + halves) + [vmem],
        out_specs=[vmem] * count + [ANYWHERE] + [vmem] * 3,
        out_shape=[jax.ShapeDtypeStruct(piece.shape, jnp.bfloat16) for piece in pieces]
        + [low(width), low(hidden), low(hidden), low(hidden)],
        scratch_shapes=[
            pltpu.VMEM((rows, width), jnp.bfloat16),
            pltpu.VMEM((3 * halves, weights[0].shape[0]) + weights[0].shape[2:], jnp.bfloat16),
            pltpu.VMEM((rows, width), jnp.float32),
            pltpu.SemaphoreType.DMA((count + 3 * halves,)),
            pltpu.SemaphoreType.DMA,
        ],
        compiler_params=pltpu.CompilerParams(vmem_limit_bytes=52 << 20),
        name="hidden",
    )(*pieces, *weights, jnp.stack(scales))


def hidden_grad_body(count, halves, *refs):
    pieces, refs = refs[:count], refs[count:]
    weights, refs = refs[:halves], refs[halves:]
    scale_ref, up_ref, gate_ref = refs[:3]
    outs, refs = refs[3 : 3 + count], refs[3 + count :]
    group_out, up_out, gate_out, scale_out, group, matrices, total, sems, out_sem = refs
    half = up_out.shape[1] // halves
    moves = copies(pieces, row_blocks(group, count), sems)
    loads = [
        pltpu.make_async_copy(
            weights[place % halves].at[:, place // halves], matrices.at[place], sems.at[count + place]
        )
        for place in range(3 * halves)
    ]
    for load in loads:
        load.start()
    for move in moves:
        move.wait()
    keep = pltpu.make_async_copy(group, group_out, out_sem)
    keep.start()
    for place in range(halves):
        columns = slice(place * half, (place + 1) * half)
        for matrix in range(3):
            loads[matrix * halves + place].wait()
        pulled = contract_cols(group[...], matrices[2 * halves + place].reshape(half, -1))
        pulled = pulled.astype(jnp.bfloat16).astype(jnp.float32)
        up = up_ref[:, columns].astype(jnp.float32)
        gate = gate_ref[:, columns].astype(jnp.float32)
        scale_up, scale_gate = scale_ref[0:1, columns], scale_ref[1:2, columns]
        raw, curve, silu, scaled = gated(up, gate, scale_up, scale_gate)
        curved = pulled * silu
        up_low = (curved * scale_up).astype(jnp.bfloat16)
        bent = pulled * scaled * (curve * (1.0 + raw * (1.0 - curve)))
        gate_low = (bent * (scale_gate * math.sqrt(D))).astype(jnp.bfloat16)
        scale_out[0:1, columns] = jnp.sum(curved * up, axis=0, keepdims=True)
        scale_out[1:2, columns] = jnp.sum(bent * gate, axis=0, keepdims=True) * math.sqrt(D)
        up_out[:, columns] = up_low
        gate_out[:, columns] = gate_low
        part = jnp.dot(
            up_low, matrices[place].reshape(half, -1), preferred_element_type=jnp.float32
        )
        part = part + jnp.dot(
            gate_low, matrices[halves + place].reshape(half, -1), preferred_element_type=jnp.float32
        )
        total[...] = part if place == 0 else total[...] + part
    rows = group.shape[0] // count
    for place in range(count):
        outs[place][...] = total[place * rows : (place + 1) * rows].astype(jnp.bfloat16)
    keep.wait()


def hidden_backward(pieces, weights, scales, up, gate):
    count, halves = len(pieces), len(weights)
    rows, width = pieces[0].shape[0] * count, pieces[0].shape[1]
    half = weights[0].shape[0] * weights[0].shape[2]
    hidden = half * halves
    low = lambda columns: jax.ShapeDtypeStruct((rows, columns), jnp.bfloat16)
    vmem = pl.BlockSpec(memory_space=pltpu.VMEM)
    return pl.pallas_call(
        lambda *refs: hidden_grad_body(count, halves, *refs),
        in_specs=[ANYWHERE] * (count + halves) + [vmem] * 3,
        out_specs=[vmem] * count + [ANYWHERE] + [vmem] * 3,
        out_shape=[jax.ShapeDtypeStruct(piece.shape, jnp.bfloat16) for piece in pieces]
        + [low(width), low(hidden), low(hidden), jax.ShapeDtypeStruct((8, hidden), jnp.float32)],
        scratch_shapes=[
            pltpu.VMEM((rows, width), jnp.bfloat16),
            pltpu.VMEM((3 * halves, weights[0].shape[0]) + weights[0].shape[2:], jnp.bfloat16),
            pltpu.VMEM((rows, width), jnp.float32),
            pltpu.SemaphoreType.DMA((count + 3 * halves,)),
            pltpu.SemaphoreType.DMA,
        ],
        compiler_params=pltpu.CompilerParams(vmem_limit_bytes=56 << 20),
        name="hidden_grad",
    )(*pieces, *weights, jnp.stack(scales), up, gate)


def visibility(parents, slots, group_size):
    labels = jnp.arange(SEGS, dtype=jnp.int32)
    linked = (parents[:, None] == labels[None, :]).astype(jnp.float32)
    reachable = jnp.maximum(linked, jnp.eye(SEGS, dtype=jnp.float32))
    for doubling in range(SEGS.bit_length()):
        reachable = jnp.minimum(jnp.dot(reachable, reachable, precision=HIGHEST), 1.0)
    return seen_factors(reachable, *row_labels(slots, group_size))


def prepare_attention(packed, scale_both, pieces, parents, slots):
    rows = pieces[0].shape[0] * len(pieces)
    queries, tree_own, raw, group = project(pieces, packed, scale_both)
    return visibility(parents, slots, rows), queries, group_gather(tree_own, "ctx"), raw, group


def forward_attention(packed, prepared, count):
    seen, queries, tree, raw, group = prepared
    heads_low, inverse, *parts = attend(queries, tree, *seen, packed, count)
    return group_scatter(parts, "tp")[0], (group, seen, queries, tree, raw, heads_low, inverse)


def first_mix(tokens_own, branch_parts, alpha_attn, gates):
    tokens_wide = tokens_own.astype(jnp.float32)
    hidden_one, pull_in = jax.vjp(
        mix_rows, tokens_wide, total_wide(branch_parts), after(alpha_attn, *gates)
    )
    hidden_low = hidden_one.astype(jnp.bfloat16)
    return (hidden_one, pull_in), hidden_low, hidden_gather(hidden_low)


def second_mix(hidden_one, branch_parts, alpha_mlp, cotangent_own, gates):
    output_wide, pull_out = jax.vjp(
        mix_rows, hidden_one, total_wide(branch_parts), after(alpha_mlp, *gates)
    )
    hidden_direct, branch_grad, grad_alpha_mlp = pull_out(cotangent_own.astype(jnp.float32))
    branch_low = branch_grad.astype(jnp.bfloat16)
    kept = (output_wide.astype(jnp.bfloat16), hidden_direct, grad_alpha_mlp)
    return kept, branch_low, hidden_gather(branch_low)


def third_mix(pull_in, hidden_parts, hidden_direct, gates):
    hidden_grad = total_wide(hidden_parts) + after(hidden_direct, *gates)
    tokens_direct, branch_grad, grad_alpha_attn = pull_in(hidden_grad)
    return tokens_direct, branch_grad.astype(jnp.bfloat16), grad_alpha_attn


def backward_attention(packed, kept, tops, hops):
    group, seen, queries, tree, raw, heads_low, inverse = kept
    query_grads, *rest = attend_grad(queries, tops, heads_low, tree, *seen, inverse, packed)
    tree_parts, first = group_scatter(rest[:-1], "ctx", hops)
    return query_grads, tree_parts, (rest[-1], heads_low)


def backward_projection(packed, scale_both, kept, attended, tokens_direct, hops):
    group, raw = kept[0], kept[4]
    query_grads, tree_parts, heads_factors = attended
    count = lax.axis_size("tp") if lax.axis_size("tp") == 4 else 1
    low, scale_sums, *parts = project_grad(
        query_grads, tree_parts, raw, packed, scale_both, count
    )
    own_parts, first = group_scatter(parts, "tp", hops)
    grad_tokens = tokens_direct + total_wide(own_parts)
    features = scale_both.shape[1] // 2
    scale_sum = jnp.sum(scale_sums, axis=(0, 1))
    scale_sum = scale_sum[:features] + scale_sum[features:]
    return grad_tokens, ((group, low), heads_factors), scale_sum, first


def joint_product(factors):
    formers, latters = zip(*factors)
    return contract_rows(jnp.concatenate(formers, axis=0), jnp.concatenate(latters, axis=0))


def per_device(
    tokens,
    parents,
    slot_segment,
    w_query,
    w_key,
    w_value,
    w_attn_out,
    w_up,
    w_gate,
    w_down,
    alpha_attn,
    alpha_mlp,
    scale_qk,
    scale_up,
    scale_gate,
    cotangent,
):
    width = tokens.shape[-1]
    micros = range(tokens.shape[0])
    last = tokens.shape[0] - 1
    groups = [group_gather(tokens[0, 0], "tp")]
    packed = lax.all_gather(
        jnp.concatenate([w_query, w_key, w_value, w_attn_out.T], axis=1),
        SPREAD,
        axis=0,
        tiled=True,
    )
    scales = hidden_scales(scale_up, scale_gate)
    scale_both = jnp.concatenate([scale_qk, scale_qk])[None]
    blocks = hidden_blocks(w_up, w_gate, w_down)
    prepared = []
    gates = scales
    for m in micros:
        early = after(scale_both, *gates)
        prepared.append(
            prepare_attention(packed, early, groups[m], parents[m, 0], slot_segment[m, 0])
        )
        if m == last:
            break
        ahead = groups[m][len(groups[m]) // 2]
        groups.append(group_gather(after(tokens[m + 1, 0], ahead), "tp", prepared[m][1:2]))
        if m == 0:
            shards = hidden_shards(after(blocks, groups[1][-1]))
        tree = prepared[m][2]
        gates = (tree[len(tree) // 2], shards)
    if last == 0:
        shards = hidden_shards(blocks)
    weights = hidden_weights(shards)
    front = [forward_attention(packed, prepared[m], len(groups[m])) for m in micros]
    gates = ()
    opened, forwards, mixed, backwards, closed, tops = [], [], [], [], [], []
    for m in micros:
        kept, mark, pieces = first_mix(tokens[m, 0], front[m][0], alpha_attn, gates)
        gates = (mark,)
        count = len(pieces)
        outs = hidden_forward(pieces, weights, scales)
        opened.append(kept)
        forwards.append((hidden_scatter(outs[:count]), outs[count:]))
    for m in micros:
        kept, mark, pieces = second_mix(
            opened[m][0], forwards[m][0], alpha_mlp, cotangent[m, 0], gates
        )
        gates = (mark,)
        up, gate = forwards[m][1][1:3]
        outs = hidden_backward(pieces, weights, scales, up, gate)
        mixed.append(kept)
        backwards.append((hidden_scatter(outs[:count]), outs[count:]))
    joined = []
    for m in micros:
        hidden_group, hidden_mixed = forwards[m][1][0], forwards[m][1][3]
        top_group, up_low, gate_low = backwards[m][1][:3]
        if m == last:
            sent = backwards[0][0][len(backwards[0][0]) // 4]
            up_low, gate_low, hidden_mixed = (
                hold(value, sent) for value in (up_low, gate_low, hidden_mixed)
            )
        joined.append(((up_low, hidden_group), (gate_low, hidden_group), (hidden_mixed, top_group)))
    products = [
        joint_product([joined[m][place] for m in micros]).astype(jnp.bfloat16)
        for place in range(3)
    ]
    for m in micros:
        closed.append(
            third_mix(
                opened[m][1],
                backwards[m][0],
                mixed[m][1],
                gates,
            )
        )
        gates = (closed[-1][1],)
        tops.append(group_gather(closed[-1][1], "tp", products if m == last else ()))
    lines = core_sums(products)
    line_sums = hidden_line_sums([after(line, *[top[-1] for top in tops]) for line in lines])
    packed_sums = hidden_pack(line_sums)
    spread_sums = hidden_spread(packed_sums)
    attended = [backward_attention(packed, front[m][1], tops[m], 1) for m in micros]
    vectors = vector_sums(
        after(
            sum(jnp.concatenate([closed[m][2], mixed[m][2]]) for m in micros), attended[-1][0]
        ),
        sum(backwards[m][1][3][:2] for m in micros),
    )
    gates = ()
    back = []
    for m in micros:
        back.append(
            backward_projection(
                packed,
                after(scale_both, *gates),
                front[m][1],
                attended[m],
                closed[m][0],
                1 if m == last else 2,
            )
        )
        gates = (back[-1][3], packed_sums, vectors)
    product = jnp.concatenate(
        [joint_product([back[m][1][place] for m in micros]) for place in range(2)], axis=1
    )
    grad_attention = owner_scatter(product.astype(jnp.bfloat16))
    grad_q, grad_k, grad_v, grad_o = jnp.split(grad_attention, 4, axis=1)
    grad_u, grad_g, grad_d = hidden_weight_grads(spread_sums)
    sums = butterfly(jnp.concatenate([vectors, sum(back[m][2] for m in micros)]), SPREAD)
    sum_alphas, sum_hidden, sum_qk = jnp.split(sums, [2 * width, sums.shape[0] - scale_qk.shape[0]])
    sum_up, sum_gate = jnp.split(sum_hidden, 2)
    return (
        jnp.stack([mixed[m][0] for m in micros])[:, None],
        jnp.stack([back[m][0] for m in micros])[:, None],
        grad_q,
        grad_k,
        grad_v,
        grad_o.T,
        grad_u.T,
        grad_g.T,
        grad_d,
        sum_alphas[:width],
        sum_alphas[width:],
        sum_qk,
        sum_up,
        sum_gate,
    )


def solution(mesh):
    return jax.shard_map(
        per_device,
        mesh=mesh,
        in_specs=(
            P(None, "shard", ("ctx", "tp"), None),
            P(None, "shard", None),
            P(None, "shard", None),
            P(("shard", "ctx"), "tp"),
            P(("shard", "ctx"), "tp"),
            P(("shard", "ctx"), "tp"),
            P("tp", ("shard", "ctx")),
            P(("shard", "ctx"), "tp"),
            P(("shard", "ctx"), "tp"),
            P("tp", ("shard", "ctx")),
            P(),
            P(),
            P("tp"),
            P("tp"),
            P("tp"),
            P(None, "shard", ("ctx", "tp"), None),
        ),
        out_specs=(
            P(None, "shard", ("ctx", "tp"), None),
            P(None, "shard", ("ctx", "tp"), None),
            P(("shard", "ctx"), "tp"),
            P(("shard", "ctx"), "tp"),
            P(("shard", "ctx"), "tp"),
            P("tp", ("shard", "ctx")),
            P(("shard", "ctx"), "tp"),
            P(("shard", "ctx"), "tp"),
            P("tp", ("shard", "ctx")),
            P(),
            P(),
            P("tp"),
            P("tp"),
            P("tp"),
        ),
        check_vma=False,
    )
```
